256 devices in a mesh: space: 64 (over x, y, z_lo), load: 4 (over z_hi, core).
Axes of the slice: x: 4, y: 4, z: 8 (z_hi: 2, z_lo: 4; z = z_hi * 4 + z_lo), core: 2. Of those that a mesh axis runs over, the one named last changes fastest.
Arguments:
- load_force: float32 [4, 3, 512, 16, 256], P('load', None, 'space'), may hold values from -6 to 6
- stiffness: float32 [512, 16, 256], P('space'), may hold values from 0.5 to 4
- material: int32 [64, 2], P('space'), may hold values from 0 to 2
- face_src: int32 [64, 64, 256], P('space'), may hold values from 0 to 32767
- face_count: int32 [64, 64], P('space'), may hold values from 0 to 256, as said below
- face_dst: int32 [64, 64, 256], P('space'), may hold values from 0 to 4095
Outputs:
- displacement: float32 [4, 3, 512, 16, 256], P('load', None, 'space')
- sensitivity: float32 [3, 512, 16, 256], P(None, 'space', 'load')
The draws below stay inside these ranges and needn't reach their ends.
Inputs may be any that keep to these rules, and one draw needn't show every extreme that they name: face_count[s, o] counts the live first slots from slab s to owner o; in every row one owner gets all 256.
All inputs are finite; a program needn't handle non-finite values.
Results may differ from the reference program's by a relative error of at most 0.0001.
Values sent between devices are 32-bit elements; how exact they have to be, the bound alone decides.
No kernel may reach another device: no remote copies, remote signals or barrier semaphores. Data moves between devices by JAX's collectives and lax.ppermute only.
A program may use at most 192 MiB of HBM per device.

```python
import math
import jax
import jax.numpy as jnp

CX = 8
NY = 16
NZ = 256
BY = 8
SLOTS = 256
FINE_STEPS = 3
COARSE_STEPS = 4
NX = 512
OWNERS = 64
LOADS = 4


def draw_face_count(key, part):
    key_quiet, key_busy, key_hot = jax.random.split(key, 3)
    quiet_load = jax.random.randint(key_quiet, (OWNERS, OWNERS), 0, SLOTS // 2 + 1)
    busy_load = jax.random.randint(key_busy, (OWNERS, OWNERS), SLOTS // 2, SLOTS + 1)
    hot_owner = jax.random.randint(key_hot, (1, OWNERS), 0, 8) == 0
    counts = jnp.where(hot_owner, busy_load, quiet_load)
    row_ids = jnp.arange(OWNERS, dtype=jnp.int32)[:, None]
    col_ids = jnp.arange(OWNERS, dtype=jnp.int32)[None, :]
    return jnp.where(col_ids == (row_ids + 1) % OWNERS, SLOTS, counts).astype(jnp.int32)


def place_ends(drawn, rng, smallest, high):
    extent = drawn.shape
    spot = [jax.random.randint(jax.random.fold_in(rng, axis), (), 0, extent[axis]) for axis in range(len(extent))]
    drawn = drawn.at[tuple(spot)].set(smallest)
    longest = extent.index(max(extent))
    spot[longest] = (spot[longest] + 1) % extent[longest]
    return drawn.at[tuple(spot)].set(high)


def steps_of(own_key, shape, cuts, least, high):
    level, own = 1.0, jax.random.fold_in(own_key, 6)
    for position, shards_of in cuts:
        steps = jnp.exp(jax.random.uniform(jax.random.fold_in(own, position), (shards_of,), jnp.float32, least / len(cuts), high / len(cuts)))
        level = level * jnp.repeat(steps, shape[position] // shards_of).reshape([-1 if axis == position else 1 for axis in range(len(shape))])
    return level


def bell_draw(rng, dims, scale, reach, cuts=(), kind=jnp.bfloat16):
    factor_of = steps_of(rng, dims, cuts, -0.22, 0.18) if cuts else 1.0
    values = jax.random.normal(rng, dims, jnp.float32) * scale * factor_of
    return jnp.minimum(jnp.maximum(values, -reach), reach).astype(kind)


def setup_inputs(seed: int = 0) -> dict:
    key_list = jax.random.split(jax.random.key(seed), 7)
    return {
        "load_force": bell_draw(key_list[0], (LOADS, 3, NX, NY, NZ), 1.0, 6.0, ((0, 4), (2, 64)), jnp.float32),
        "stiffness": jnp.clip(jnp.exp(math.log(4.0) - 2.0794415 * jax.random.uniform(key_list[1], (NX, NY, NZ), jnp.float32) ** steps_of(key_list[1], (NX, NY, NZ), ((0, 64),), -0.2, 0.2)), 0.5, 4.0),
        "material": place_ends(jax.random.randint(key_list[2], (OWNERS, NY // BY), 0, 3), jax.random.fold_in(key_list[2], 1), 0, 2).astype(jnp.int32),
        "face_src": place_ends(jax.random.randint(key_list[3], (OWNERS, OWNERS, SLOTS), 0, CX * NY * NZ), jax.random.fold_in(key_list[3], 1), 0, (CX * NY * NZ) - 1).astype(jnp.int32),
        "face_count": draw_face_count(jax.random.fold_in(key_list[6], 71), 0),
        "face_dst": place_ends(jax.random.randint(key_list[5], (OWNERS, OWNERS, SLOTS), 0, (CX // 2) * (NY // 2) * (NZ // 2)), jax.random.fold_in(key_list[5], 1), 0, ((CX // 2) * (NY // 2) * (NZ // 2)) - 1).astype(jnp.int32),
    }


UPPER_EDGE = 2.1
LOWER_EDGE = 0.15
COUPLING = 0.1
MODULI = (1.0, 0.55, 0.25)


def neighbour_list():
    entries = []
    for shift_x in (-1, 0, 1):
        for shift_y in (-1, 0, 1):
            for shift_z in (-1, 0, 1):
                reach_len = abs(shift_x) + abs(shift_y) + abs(shift_z)
                if reach_len > 0:
                    entries.append((shift_x, shift_y, shift_z, (1.0, 0.5, 0.25)[reach_len - 1] / 14.0))
    return entries


def window(padded, shift_x, shift_y, shift_z, inner_shape):
    size_x, size_y, size_z = inner_shape
    return padded[:, 1 + shift_x:1 + shift_x + size_x, 1 + shift_y:1 + shift_y + size_y, 1 + shift_z:1 + shift_z + size_z]


def operate(padded_field, padded_coef):
    inner_shape = (padded_field.shape[1] - 2, padded_field.shape[2] - 2, padded_field.shape[3] - 2)
    centre = window(padded_field, 0, 0, 0, inner_shape)
    coef_mid = window(padded_coef, 0, 0, 0, inner_shape)
    result = jnp.zeros_like(centre)
    for shift_x, shift_y, shift_z, weight in neighbour_list():
        face_coef = 0.5 * (coef_mid + window(padded_coef, shift_x, shift_y, shift_z, inner_shape))
        result = result + (weight * face_coef) * (centre - window(padded_field, shift_x, shift_y, shift_z, inner_shape))
    pieces = []
    for component in range(3):
        mixed_term = jnp.zeros_like(coef_mid[0])
        for partner in range(3):
            if partner != component:
                for sign_a in (1, -1):
                    for sign_b in (1, -1):
                        offset = [0, 0, 0]
                        offset[component] += sign_a
                        offset[partner] += sign_b
                        mixed_term = mixed_term + (0.25 * sign_a * sign_b) * window(padded_field[partner:partner + 1], offset[0], offset[1], offset[2], inner_shape)[0]
        pieces.append(result[component] - COUPLING * coef_mid[0] * mixed_term)
    return jnp.stack(pieces)


def diagonal_of(padded_coef):
    inner_shape = (padded_coef.shape[1] - 2, padded_coef.shape[2] - 2, padded_coef.shape[3] - 2)
    coef_mid = window(padded_coef, 0, 0, 0, inner_shape)
    total_sum = jnp.zeros_like(coef_mid)
    for shift_x, shift_y, shift_z, weight in neighbour_list():
        total_sum = total_sum + weight * 0.5 * (coef_mid + window(padded_coef, shift_x, shift_y, shift_z, inner_shape))
    return total_sum


def pad_global(grid_field):
    return jnp.pad(grid_field, ((0, 0), (1, 1), (1, 1), (1, 1)))


def chebyshev(source, padded_coef, diagonal, sweep_count, widen):
    midpoint = (UPPER_EDGE + LOWER_EDGE) / 2.0
    halfwidth = (UPPER_EDGE - LOWER_EDGE) / 2.0
    spread_ratio = midpoint / halfwidth
    rho_old = 1.0 / spread_ratio
    update = source / (midpoint * diagonal)
    solution = update
    for sweep_idx in range(1, sweep_count):
        residual = source - operate(widen(solution), padded_coef)
        rho_new = 1.0 / (2.0 * spread_ratio - rho_old)
        update = (rho_new * rho_old) * update + (2.0 * rho_new / halfwidth) * residual / diagonal
        solution = solution + update
        rho_old = rho_new
    return solution


def coarsen(grid_field):
    comps, size_x, size_y, size_z = grid_field.shape
    return grid_field.reshape(comps, size_x // 2, 2, size_y // 2, 2, size_z // 2, 2).mean(axis=(2, 4, 6))


def refine(grid_field):
    return jnp.repeat(jnp.repeat(jnp.repeat(grid_field, 2, axis=1), 2, axis=2), 2, axis=3)


def modulus_rows(material, brick_rows):
    onehot = (material[..., None] == jnp.arange(len(MODULI), dtype=jnp.int32)).astype(jnp.float32)
    values = jnp.sum(onehot * jnp.array(MODULI, jnp.float32), axis=-1)
    return jnp.repeat(values, brick_rows, axis=-1)


def reference(load_force, stiffness, material, face_src, face_count, face_dst):
    owners = NX // CX
    fine_cells = CX * NY * NZ
    coarse_cells = (CX // 2) * (NY // 2) * (NZ // 2)
    own_cells = jnp.repeat(modulus_rows(material, BY), CX, axis=0)[:, :, None]
    coef = stiffness * own_cells
    padded_coef = pad_global(coef[None])
    diag_fine = diagonal_of(padded_coef)
    padded_coarse = pad_global(coarsen(coef[None]))
    diag_coarse = diagonal_of(padded_coarse)
    sender = jnp.broadcast_to(jnp.arange(owners, dtype=jnp.int32)[:, None, None], face_src.shape)
    owner_idx = jnp.broadcast_to(jnp.arange(owners, dtype=jnp.int32)[None, :, None], face_src.shape)
    live_mask = (jnp.arange(SLOTS, dtype=jnp.int32)[None, None, :] < face_count[:, :, None]).astype(jnp.float32)
    targets = jnp.transpose(face_dst, (1, 0, 2))
    energy = jnp.zeros((NX, NY, NZ), jnp.float32)
    outputs = []
    for load_idx in range(LOADS):
        source = load_force[load_idx]
        smooth = chebyshev(source, padded_coef, diag_fine, FINE_STEPS, pad_global)
        residual = source - operate(pad_global(smooth), padded_coef)
        coarse_source = 4.0 * coarsen(residual)
        coarse_shape = coarse_source.shape
        picked = residual.reshape(3, owners, fine_cells)[:, sender, face_src] * live_mask
        coarse_source = coarse_source.reshape(3, owners, coarse_cells).at[:, owner_idx, targets].add(picked).reshape(coarse_shape)
        correction = chebyshev(coarse_source, padded_coarse, diag_coarse, COARSE_STEPS, pad_global)
        displaced = smooth + refine(correction)
        image = operate(pad_global(displaced), padded_coef)
        energy = energy + jnp.sum(displaced * image, axis=0)
        outputs.append(displaced)
    moduli = jnp.array(MODULI, jnp.float32)[:, None, None, None]
    sensitivity = (moduli - own_cells[None]) / own_cells[None] * energy[None]
    return jnp.stack(outputs), sensitivity
```

```python
import jax
import jax.numpy as jnp
import numpy as np
from jax import lax
from jax.experimental import pallas as pl
from jax.experimental.pallas import tpu as pltpu
from jax.sharding import PartitionSpec as P

CX = 8
NY = 16
NZ = 256
BY = 8
SLOTS = 256
FINE_STEPS = 3
COARSE_STEPS = 4

UPPER_EDGE = 2.1
LOWER_EDGE = 0.15
COUPLING = 0.1
MODULI = (1.0, 0.55, 0.25)

MIDPOINT = (UPPER_EDGE + LOWER_EDGE) / 2.0
HALFWIDTH = (UPPER_EDGE - LOWER_EDGE) / 2.0

HX, HY, HZ = CX // 2, NY // 2, NZ // 2
FINE_PLANES = CX + 6
COEF_PLANES = CX + 8
PACK = 3 * 3 + 4 + 1
F32 = jnp.float32
BF16 = jnp.bfloat16
HIGHEST = lax.Precision.HIGHEST


def step_factors(count):
    ratio = MIDPOINT / HALFWIDTH
    rho_old = 1.0 / ratio
    factors = []
    for _ in range(1, count):
        rho_new = 1.0 / (2.0 * ratio - rho_old)
        factors.append((rho_new * rho_old, 2.0 * rho_new / HALFWIDTH))
        rho_old = rho_new
    return factors


class Shifts:
    def __init__(self, shape):
        self.nd = len(shape)
        self.shape = shape
        y = lax.broadcasted_iota(jnp.int32, shape, self.nd - 2)
        z = lax.broadcasted_iota(jnp.int32, shape, self.nd - 1)
        self.edge = {
            self.nd - 2: (y == 0, y == shape[-2] - 1),
            self.nd - 1: (z == 0, z == shape[-1] - 1),
        }

    def pair(self, x, axis):
        first, last = self.edge[axis]
        size = self.shape[axis]
        below = jnp.where(first, 0.0, pltpu.roll(x, 1, axis))
        above = jnp.where(last, 0.0, pltpu.roll(x, size - 1, axis))
        return below, above

    def diff(self, x, axis):
        below, above = self.pair(x, axis)
        return above - below

    def dy(self, x):
        return self.diff(x, self.nd - 2)

    def dz(self, x):
        return self.diff(x, self.nd - 1)

    def spread(self, x):
        for axis in (self.nd - 2, self.nd - 1):
            below, above = self.pair(x, axis)
            x = x + 0.5 * (below + above)
        return x


def diagonal(sh, k_below, k_mid, k_above):
    return (3.0 / 7.0) * k_mid + (1.0 / 14.0) * sh.spread(k_mid + 0.5 * (k_below + k_above))


def operate(sh, below, mid, above, k_below, k_mid, k_above, diag):
    centre = diag + (1.0 / 7.0) * k_mid
    slope = [above[c] - below[c] for c in range(3)]
    mixed = (
        sh.dy(slope[1]) + sh.dz(slope[2]),
        sh.dy(slope[0] + sh.dz(mid[2])),
        sh.dz(slope[0] + sh.dy(mid[1])),
    )
    result = []
    for c in range(3):
        plain = sh.spread(mid[c] + 0.5 * (below[c] + above[c]))
        scaled = sh.spread(k_mid * mid[c] + 0.5 * (k_below * below[c] + k_above * above[c]))
        result.append(
            centre * mid[c]
            - (1.0 / 14.0) * (k_mid * plain + scaled)
            - (0.25 * COUPLING) * (k_mid * mixed[c])
        )
    return result


def modulus(material_ref, brick):
    ident = material_ref[0, brick]
    return jnp.where(ident == 0, MODULI[0], jnp.where(ident == 1, MODULI[1], MODULI[2])).astype(F32)


def own_plane(material_ref):
    row = lax.broadcasted_iota(jnp.int32, (NY, NZ), 0)
    return jnp.where(row < BY, modulus(material_ref, 0), modulus(material_ref, 1))


def pair_columns():
    fine = lax.broadcasted_iota(jnp.int32, (NZ, HZ), 0)
    coarse = lax.broadcasted_iota(jnp.int32, (NZ, HZ), 1)
    return (lax.shift_right_logical(fine, 1) == coarse).astype(F32)


def coarse_sum(planes, narrow_ref):
    narrow_ref[...] = jnp.dot(
        planes, pair_columns(), precision=HIGHEST, preferred_element_type=F32
    )
    rows = narrow_ref.shape[0] // 2
    return narrow_ref[pl.ds(0, rows, stride=2), :] + narrow_ref[pl.ds(1, rows, stride=2), :]


def pack_kernel(material_ref, force_ref, stiff_ref, low_ref, high_ref, coarse_ref, sums):
    own = own_plane(material_ref)
    for c in range(3):
        for p in range(3):
            low_ref[3 * c + p] = force_ref[0, c, p]
            high_ref[3 * c + p] = force_ref[0, c, CX - 3 + p]
    coef = [stiff_ref[p] * own for p in range(CX)]
    for p in range(4):
        low_ref[9 + p] = coef[p]
        high_ref[9 + p] = coef[CX - 4 + p]
    pairs = jnp.concatenate([coef[2 * p] + coef[2 * p + 1] for p in range(HX)], axis=0)
    coarse = (0.125 * coarse_sum(pairs, sums)).reshape(HX, HY, HZ)
    coarse_ref[...] = coarse
    for p in range(HX):
        y, z = (p // 2) * HY, (p % 2) * HZ
        low_ref[13, y : y + HY, z : z + HZ] = coarse[p]
        high_ref[13, y : y + HY, z : z + HZ] = coarse[p]


def unpack_coarse(plane_ref):
    return [
        plane_ref[0, (p // 2) * HY : (p // 2) * HY + HY, (p % 2) * HZ : (p % 2) * HZ + HZ]
        for p in range(HX)
    ]


def fine_kernel(
    material_ref,
    count_ref,
    force_ref,
    stiff_ref,
    below_ref,
    above_ref,
    index_ref,
    smooth_ref,
    coef_out_ref,
    diag_out_ref,
    coarse_ref,
    picked_ref,
    coef,
    diag,
    inverse,
    force,
    first,
    second,
    table,
    sums,
    residual,
):
    slab = lax.axis_index("space")
    slabs = lax.axis_size("space")
    sh = Shifts((NY, NZ))
    own = own_plane(material_ref)
    has_below = slab > 0
    has_above = slab < slabs - 1
    for p in range(CX):
        coef[4 + p] = stiff_ref[p] * own
    for p in range(4):
        coef[p] = jnp.where(has_below, below_ref[9 + p], 0.0)
        coef[4 + CX + p] = jnp.where(has_above, above_ref[9 + p], 0.0)
    for c in range(3):
        for p in range(3):
            force[c, p] = below_ref[3 * c + p]
            force[c, 3 + CX + p] = above_ref[3 * c + p]
        for p in range(CX):
            force[c, 3 + p] = force_ref[0, c, p]

    @pl.loop(0, FINE_PLANES)
    def _(p):
        d = diagonal(sh, coef[p], coef[p + 1], coef[p + 2])
        where = slab * CX + p - 3
        valid = jnp.logical_and(where >= 0, where < slabs * CX)
        inv = jnp.where(valid, 1.0 / d, 0.0)
        diag[p] = d
        inverse[p] = inv
        for c in range(3):
            first[c, p] = force[c, p] * inv * (1.0 / MIDPOINT)

    def remainder(src, p, base):
        planes = [[src[c, p + o - base] for c in range(3)] for o in (-1, 0, 1)]
        image = operate(sh, *planes, coef[p], coef[p + 1], coef[p + 2], diag[p])
        return planes[1], [force[c, p] - image[c] for c in range(3)]

    (keep_2, gain_2), (keep_3, gain_3) = step_factors(FINE_STEPS)

    @pl.loop(1, FINE_PLANES - 1)
    def _(p):
        value, left = remainder(first, p, 0)
        for c in range(3):
            second[c, p] = (1.0 + keep_2) * value[c] + gain_2 * (left[c] * inverse[p])

    @pl.loop(2, FINE_PLANES - 2)
    def _(p):
        value, left = remainder(second, p, 0)
        for c in range(3):
            step = keep_3 * (value[c] - first[c, p]) + gain_3 * (left[c] * inverse[p])
            smooth_ref[c, p - 2] = value[c] + step

    @pl.loop(3, FINE_PLANES - 3)
    def _(p):
        _, left = remainder(smooth_ref, p, 2)
        for c in range(3):
            row = pl.multiple_of(c * (CX * NY) + (p - 3) * NY, NY)
            residual[pl.ds(row, NY), :] = left[c]
            head = left[c].astype(BF16)
            table[pl.ds(row, NY), 0:NZ] = head
            table[pl.ds(row, NY), NZ : 2 * NZ] = (left[c] - head.astype(F32)).astype(BF16)

    for p in range(CX + 2):
        coef_out_ref[p] = coef[p + 3]
    for p in range(CX):
        diag_out_ref[p] = diag[p + 3]

    planes = residual[...].reshape(3 * HX, 2, NY, NZ)
    pairs = (planes[:, 0] + planes[:, 1]).reshape(3 * HX * NY, NZ)
    coarse_ref[...] = 0.5 * coarse_sum(pairs, sums)

    plane_rows = CX * NY
    column = lax.broadcasted_iota(jnp.int32, (NZ, SLOTS), 0)
    line = lax.broadcasted_iota(jnp.int32, (plane_rows, SLOTS), 0)
    slot = lax.broadcasted_iota(jnp.int32, (1, SLOTS), 1)

    @pl.loop(0, slabs)
    def _(o):
        index = index_ref[0, pl.ds(o, 1), :]
        hot = (column == (index & (NZ - 1))).astype(BF16)
        both = jnp.dot(table[:, 0:NZ], hot, preferred_element_type=F32) + jnp.dot(
            table[:, NZ : 2 * NZ], hot, preferred_element_type=F32
        )
        chosen = line == lax.shift_right_logical(index, 8)
        live = slot < count_ref[0, o]
        for c in range(3):
            part = jnp.where(chosen, both[c * plane_rows : (c + 1) * plane_rows, :], 0.0)
            value = jnp.sum(part, axis=0, keepdims=True)
            picked_ref[pl.ds(o, 1), c * SLOTS : (c + 1) * SLOTS] = jnp.where(live, value, 0.0)


def coarse_extent(below_pack_ref, coarse_ref, above_pack_ref, slab, slabs):
    low = [jnp.where(slab > 0, x, 0.0) for x in unpack_coarse(below_pack_ref)]
    high = [jnp.where(slab < slabs - 1, x, 0.0) for x in unpack_coarse(above_pack_ref)]
    return low + [coarse_ref[p] for p in range(HX)] + high


def gather_kernel(
    arrived_ref,
    target_ref,
    local_ref,
    coef_below_ref,
    coef_ref,
    coef_above_ref,
    source_ref,
    low_ref,
    high_ref,
    total,
    rows,
):
    slab = lax.axis_index("space")
    slabs = lax.axis_size("space")
    half_rows = HX * HY * HZ // SLOTS
    column = lax.broadcasted_iota(jnp.int32, (SLOTS, SLOTS), 0)
    line = lax.broadcasted_iota(jnp.int32, (half_rows, SLOTS), 0)
    total[...] = jnp.zeros_like(total)

    @pl.loop(0, slabs)
    def _(s):
        index = target_ref[0, pl.ds(s, 1), :]
        hot = (column == (index & (SLOTS - 1))).astype(BF16)
        chosen = line == lax.shift_right_logical(index, 8)
        parts = [
            jnp.where(chosen, arrived_ref[pl.ds(s, 1), c * SLOTS : (c + 1) * SLOTS], 0.0)
            for c in range(3)
        ]
        values = jnp.concatenate(parts, axis=0)
        head = values.astype(BF16)
        tail = (values - head.astype(F32)).astype(BF16)
        total[...] += lax.dot_general(
            jnp.concatenate([head, tail], axis=0),
            hot,
            (((1,), (1,)), ((), ())),
            preferred_element_type=F32,
        )

    count = 3 * half_rows
    joined = total[0:count, :] + total[count : 2 * count, :]
    rows[pl.ds(0, count, stride=2), :] = joined[:, 0:HZ]
    rows[pl.ds(1, count, stride=2), :] = joined[:, HZ:]
    source = (rows[...] + local_ref[...]).reshape(3, HX, HY, HZ)
    source_ref[...] = source
    low_ref[...] = source
    high_ref[...] = source
    coef = coarse_extent(coef_below_ref, coef_ref, coef_above_ref, slab, slabs)
    sh = Shifts((HY, HZ))
    for ref, p in ((high_ref, 0), (low_ref, HX - 1)):
        d = diagonal(sh, coef[HX + p - 1], coef[HX + p], coef[HX + p + 1])
        scale = (1.0 / MIDPOINT) / d
        for c in range(3):
            ref[c, p] = source[c, p] * scale


def coarse_kernel(
    source_ref,
    below_ref,
    above_ref,
    coef_below_ref,
    coarse_coef_ref,
    coef_above_ref,
    smooth_ref,
    coef_ref,
    diag_ref,
    moved_ref,
    kept_ref,
    sent_1_ref,
    sent_2_ref,
    sent_3_ref,
    rows,
    field,
    energy,
):
    slab = lax.axis_index("space")
    slabs = lax.axis_size("space")
    mine = lax.axis_index("load")
    coef = jnp.stack(coarse_extent(coef_below_ref, coarse_coef_ref, coef_above_ref, slab, slabs))
    source = [
        jnp.concatenate([below_ref[c], source_ref[c], above_ref[c]], axis=0) for c in range(3)
    ]
    count = 3 * HX - 2
    place = lax.broadcasted_iota(jnp.int32, (count, HY, HZ), 0) + (slab * HX - HX + 1)
    valid = jnp.logical_and(place >= 0, place < slabs * HX)
    diag = diagonal(Shifts((count, HY, HZ)), coef[:-2], coef[1:-1], coef[2:])
    inverse = jnp.where(valid, 1.0 / diag, 0.0)
    older = None
    value = []
    for c in range(3):
        low = jnp.where(slab > 0, source[c][:1], 0.0)
        high = jnp.where(slab < slabs - 1, source[c][-1:], 0.0)
        inner = source[c][1:-1] * inverse * (1.0 / MIDPOINT)
        value.append(jnp.concatenate([low, inner, high], axis=0))
    for number, (keep, gain) in enumerate(step_factors(COARSE_STEPS)):
        size = count - 2 * number
        inside = slice(number, number + size)
        window = slice(number + 1, number + 1 + size)
        image = operate(
            Shifts((size, HY, HZ)),
            [v[:-2] for v in value],
            [v[1:-1] for v in value],
            [v[2:] for v in value],
            coef[number : number + size],
            coef[window],
            coef[number + 2 : number + 2 + size],
            diag[inside],
        )
        newer = []
        for c in range(3):
            mid = value[c][1:-1]
            change = mid if older is None else mid - older[c][2:-2]
            left = source[c][window] - image[c]
            newer.append(mid + keep * change + gain * (left * inverse[inside]))
        older, value = value, newer

    planes = HX + 2
    flat = jnp.concatenate([v.reshape(planes * HY, HZ) for v in value], axis=0)
    fine = lax.broadcasted_iota(jnp.int32, (HZ, NZ), 1)
    half = lax.broadcasted_iota(jnp.int32, (HZ, NZ), 0)
    repeat = (lax.shift_right_logical(fine, 1) == half).astype(F32)
    amount = 3 * planes * HY
    rows[pl.ds(0, amount, stride=2), :] = flat
    rows[pl.ds(1, amount, stride=2), :] = flat
    wide = jnp.dot(rows[...], repeat, precision=HIGHEST, preferred_element_type=F32)
    for c in range(3):
        for p in range(CX + 2):
            at = (c * planes + (p + 1) // 2) * NY
            moved = smooth_ref[c, p] + wide[at : at + NY, :]
            field[c, p] = moved
            if 0 < p <= CX:
                moved_ref[0, c, p - 1] = moved

    sh = Shifts((NY, NZ))

    @pl.loop(1, CX + 1)
    def _(p):
        planes = [[field[c, p + o] for c in range(3)] for o in (-1, 0, 1)]
        image = operate(
            sh, *planes, coef_ref[p - 1], coef_ref[p], coef_ref[p + 1], diag_ref[p - 1]
        )
        mid = planes[1]
        energy[p - 1] = mid[0] * image[0] + mid[1] * image[1] + mid[2] * image[2]

    part = NY // 4
    for q in range(4):

        @pl.when(mine == q)
        def _():
            for k, ref in enumerate((kept_ref, sent_1_ref, sent_2_ref, sent_3_ref)):
                y = ((q + k) % 4) * part
                ref[...] = energy[:, y : y + part, :]


def close_kernel(material_ref, kept_ref, got_1_ref, got_2_ref, got_3_ref, out_ref):
    mine = lax.axis_index("load")
    ident = jnp.where(mine < 2, material_ref[0, 0], material_ref[0, 1])
    total = kept_ref[...] + got_1_ref[...] + got_2_ref[...] + got_3_ref[...]
    base = np.array(MODULI, np.float32)
    for m in range(3):
        factor = [float((base[m] - base[i]) / base[i]) for i in range(3)]
        scale = jnp.where(ident == 0, factor[0], jnp.where(ident == 1, factor[1], factor[2]))
        out_ref[m] = total * scale.astype(F32)


VMEM = pl.BlockSpec(memory_space=pltpu.VMEM)
SMEM = pl.BlockSpec(memory_space=pltpu.SMEM)
PARAMS = pltpu.CompilerParams(vmem_limit_bytes=32 << 20)


def shaped(*shape):
    return jax.ShapeDtypeStruct(shape, F32)


def body(load_force, stiffness, material, face_src, face_count, face_dst):
    slabs = lax.axis_size("space")
    forward = [(i, (i + 1) % slabs) for i in range(slabs)]
    backward = [(target, origin) for origin, target in forward]
    pack_low, pack_high, coarse_coef = pl.pallas_call(
        pack_kernel,
        out_shape=(shaped(PACK, NY, NZ), shaped(PACK, NY, NZ), shaped(HX, HY, HZ)),
        in_specs=[SMEM, VMEM, VMEM],
        out_specs=(VMEM, VMEM, VMEM),
        scratch_shapes=[pltpu.VMEM((HX * NY, HZ), F32)],
        compiler_params=PARAMS,
        name="pack",
    )(material, load_force, stiffness)
    below = lax.ppermute(pack_high, "space", forward)
    above = lax.ppermute(pack_low, "space", backward)

    smooth, coef, diag, local, picked = pl.pallas_call(
        fine_kernel,
        out_shape=(
            shaped(3, CX + 2, NY, NZ),
            shaped(CX + 2, NY, NZ),
            shaped(CX, NY, NZ),
            shaped(3 * HX * HY, HZ),
            shaped(slabs, 3 * SLOTS),
        ),
        in_specs=[SMEM, SMEM, VMEM, VMEM, VMEM, VMEM, VMEM],
        out_specs=(VMEM, VMEM, VMEM, VMEM, VMEM),
        scratch_shapes=[
            pltpu.VMEM((COEF_PLANES, NY, NZ), F32),
            pltpu.VMEM((FINE_PLANES, NY, NZ), F32),
            pltpu.VMEM((FINE_PLANES, NY, NZ), F32),
            pltpu.VMEM((3, FINE_PLANES, NY, NZ), F32),
            pltpu.VMEM((3, FINE_PLANES, NY, NZ), F32),
            pltpu.VMEM((3, FINE_PLANES, NY, NZ), F32),
            pltpu.VMEM((3 * CX * NY, 2 * NZ), BF16),
            pltpu.VMEM((3 * HX * NY, HZ), F32),
            pltpu.VMEM((3 * CX * NY, NZ), F32),
        ],
        compiler_params=PARAMS,
        name="fine",
    )(material, face_count, load_force, stiffness, below, above, face_src)

    arrived = lax.all_to_all(picked, "space", split_axis=0, concat_axis=0, tiled=True)

    tail = pl.BlockSpec((1, NY, NZ), lambda i: (PACK - 1, 0, 0))

    def whole(*shape):
        return pl.BlockSpec(shape, lambda i: (0,) * len(shape))

    grid_shape = (3, HX, HY, HZ)
    source, send_low, send_high = pl.pallas_call(
        gather_kernel,
        grid=(1,),
        out_shape=(shaped(*grid_shape), shaped(*grid_shape), shaped(*grid_shape)),
        in_specs=[
            whole(slabs, 3 * SLOTS),
            whole(1, slabs, SLOTS),
            whole(3 * HX * HY, HZ),
            tail,
            whole(HX, HY, HZ),
            tail,
        ],
        out_specs=(whole(*grid_shape), whole(*grid_shape), whole(*grid_shape)),
        scratch_shapes=[
            pltpu.VMEM((6 * HX * HY * HZ // SLOTS, SLOTS), F32),
            pltpu.VMEM((3 * HX * HY, HZ), F32),
        ],
        compiler_params=PARAMS,
        name="reflux",
    )(arrived, face_dst, local, below, coarse_coef, above)
    source_below = lax.ppermute(send_high, "space", forward)
    source_above = lax.ppermute(send_low, "space", backward)

    part = (CX, NY // 4, NZ)
    moved, kept, sent_1, sent_2, sent_3 = pl.pallas_call(
        coarse_kernel,
        grid=(1,),
        out_shape=(shaped(1, 3, CX, NY, NZ),) + (shaped(*part),) * 4,
        in_specs=[
            whole(*grid_shape),
            whole(*grid_shape),
            whole(*grid_shape),
            tail,
            whole(HX, HY, HZ),
            tail,
            whole(3, CX + 2, NY, NZ),
            whole(CX + 2, NY, NZ),
            whole(CX, NY, NZ),
        ],
        out_specs=(whole(1, 3, CX, NY, NZ),) + (whole(*part),) * 4,
        scratch_shapes=[
            pltpu.VMEM((3 * (HX + 2) * NY, HZ), F32),
            pltpu.VMEM((3, CX + 2, NY, NZ), F32),
            pltpu.VMEM((CX, NY, NZ), F32),
        ],
        compiler_params=PARAMS,
        name="coarse",
    )(source, source_below, source_above, below, coarse_coef, above, smooth, coef, diag)
    got = [
        lax.ppermute(piece, "load", [(i, (i + k) % 4) for i in range(4)])
        for k, piece in ((1, sent_1), (2, sent_2), (3, sent_3))
    ]
    sensitivity = pl.pallas_call(
        close_kernel,
        out_shape=shaped(3, *part),
        in_specs=[SMEM, VMEM, VMEM, VMEM, VMEM],
        out_specs=VMEM,
        name="close",
    )(material, kept, *got)
    return moved, sensitivity


def solution(mesh):
    return jax.shard_map(
        body,
        mesh=mesh,
        in_specs=(
            P("load", None, "space", None, None),
            P("space", None, None),
            P("space", None),
            P("space", None, None),
            P("space", None),
            P("space", None, None),
        ),
        out_specs=(P("load", None, "space", None, None), P(None, "space", "load", None)),
        check_vma=False,
    )
```

```python
import jax
import jax.numpy as jnp
import numpy as np
from jax import lax
from jax.experimental import pallas as pl
from jax.experimental.pallas import tpu as pltpu
from jax.sharding import PartitionSpec as P

CX = 8
NY = 16
NZ = 256
BY = 8
SLOTS = 256
FINE_STEPS = 3
COARSE_STEPS = 4

UPPER_EDGE = 2.1
LOWER_EDGE = 0.15
COUPLING = 0.1
MODULI = (1.0, 0.55, 0.25)

MIDPOINT = (UPPER_EDGE + LOWER_EDGE) / 2.0
HALFWIDTH = (UPPER_EDGE - LOWER_EDGE) / 2.0

HX, HY, HZ = CX // 2, NY // 2, NZ // 2
FINE_PLANES = CX + 6
COEF_PLANES = CX + 6
PACK = 3 * 3 + 3 + 1
F32 = jnp.float32
BF16 = jnp.bfloat16
HIGHEST = lax.Precision.HIGHEST


def step_factors(count):
    ratio = MIDPOINT / HALFWIDTH
    rho_old = 1.0 / ratio
    factors = []
    for _ in range(1, count):
        rho_new = 1.0 / (2.0 * ratio - rho_old)
        factors.append((rho_new * rho_old, 2.0 * rho_new / HALFWIDTH))
        rho_old = rho_new
    return factors


class Shifts:
    def __init__(self, shape):
        self.nd = len(shape)
        self.shape = shape
        y = lax.broadcasted_iota(jnp.int32, shape, self.nd - 2)
        z = lax.broadcasted_iota(jnp.int32, shape, self.nd - 1)
        self.edge = {
            self.nd - 2: (y == 0, y == shape[-2] - 1),
            self.nd - 1: (z == 0, z == shape[-1] - 1),
        }

    def pair(self, x, axis):
        first, last = self.edge[axis]
        size = self.shape[axis]
        below = jnp.where(first, 0.0, pltpu.roll(x, 1, axis))
        above = jnp.where(last, 0.0, pltpu.roll(x, size - 1, axis))
        return below, above

    def diff(self, x, axis):
        below, above = self.pair(x, axis)
        return above - below

    def dy(self, x):
        return self.diff(x, self.nd - 2)

    def dz(self, x):
        return self.diff(x, self.nd - 1)

    def spread(self, x):
        for axis in (self.nd - 2, self.nd - 1):
            below, above = self.pair(x, axis)
            x = x + 0.5 * (below + above)
        return x


def diagonal(sh, k_below, k_mid, k_above):
    return (3.0 / 7.0) * k_mid + (1.0 / 14.0) * sh.spread(k_mid + 0.5 * (k_below + k_above))


def operate(sh, below, mid, above, k_below, k_mid, k_above, diag):
    centre = diag + (1.0 / 7.0) * k_mid
    slope = [above[c] - below[c] for c in range(3)]
    mixed = (
        sh.dy(slope[1]) + sh.dz(slope[2]),
        sh.dy(slope[0] + sh.dz(mid[2])),
        sh.dz(slope[0] + sh.dy(mid[1])),
    )
    result = []
    for c in range(3):
        plain = sh.spread(mid[c] + 0.5 * (below[c] + above[c]))
        scaled = sh.spread(k_mid * mid[c] + 0.5 * (k_below * below[c] + k_above * above[c]))
        result.append(
            centre * mid[c]
            - (1.0 / 14.0) * (k_mid * plain + scaled)
            - (0.25 * COUPLING) * (k_mid * mixed[c])
        )
    return result


def modulus(material_ref, brick):
    ident = material_ref[0, brick]
    return jnp.where(ident == 0, MODULI[0], jnp.where(ident == 1, MODULI[1], MODULI[2])).astype(F32)


def own_plane(material_ref):
    row = lax.broadcasted_iota(jnp.int32, (NY, NZ), 0)
    return jnp.where(row < BY, modulus(material_ref, 0), modulus(material_ref, 1))


def pair_columns():
    fine = lax.broadcasted_iota(jnp.int32, (NZ, HZ), 0)
    coarse = lax.broadcasted_iota(jnp.int32, (NZ, HZ), 1)
    return (lax.shift_right_logical(fine, 1) == coarse).astype(F32)


def coarse_sum(planes, narrow_ref):
    narrow_ref[...] = jnp.dot(
        planes, pair_columns(), precision=HIGHEST, preferred_element_type=F32
    )
    rows = narrow_ref.shape[0] // 2
    return narrow_ref[pl.ds(0, rows, stride=2), :] + narrow_ref[pl.ds(1, rows, stride=2), :]


def pack_kernel(
    material_hbm, force_hbm, stiff_hbm, low_ref, high_ref, coarse_ref, material, stiff, sums, sems
):
    copies = [
        pltpu.make_async_copy(stiff_hbm, stiff, sems.at[0]),
        pltpu.make_async_copy(material_hbm, material, sems.at[1]),
    ]
    for c in range(3):
        rows = pl.ds(3 * c, 3)
        copies += [
            pltpu.make_async_copy(force_hbm.at[0, c, pl.ds(0, 3)], low_ref.at[rows], sems.at[2 + c]),
            pltpu.make_async_copy(
                force_hbm.at[0, c, pl.ds(CX - 3, 3)], high_ref.at[rows], sems.at[5 + c]
            ),
        ]
    for copy in copies:
        copy.start()
    for copy in copies:
        copy.wait()
    own = own_plane(material)
    sh = Shifts((NY, NZ))
    coef = [stiff[p] * own for p in range(CX)]
    for p in range(3):
        low_ref[9 + p] = coef[p]
        high_ref[9 + p] = coef[CX - 3 + p]
    for ref, p, slot in ((low_ref, 2, 2), (high_ref, CX - 3, 0)):
        scale = (1.0 / MIDPOINT) / diagonal(sh, coef[p - 1], coef[p], coef[p + 1])
        for c in range(3):
            ref[3 * c + slot] = ref[3 * c + slot] * scale
    pairs = jnp.concatenate([coef[2 * p] + coef[2 * p + 1] for p in range(HX)], axis=0)
    coarse = (0.125 * coarse_sum(pairs, sums)).reshape(HX, HY, HZ)
    coarse_ref[...] = coarse
    for p in range(HX):
        y, z = (p // 2) * HY, (p % 2) * HZ
        low_ref[PACK - 1, y : y + HY, z : z + HZ] = coarse[p]
        high_ref[PACK - 1, y : y + HY, z : z + HZ] = coarse[p]


def plan_kernel(count_ref, source_ref, target_ref, line_ref, column_ref, where_ref, index_ref):
    slabs = count_ref.shape[1]
    lane = lax.broadcasted_iota(jnp.int32, (1, SLOTS), 1)
    cells = target_ref[0]
    line_ref[...] = lax.shift_right_logical(cells, 7).astype(F32)
    column_ref[...] = (cells & (HZ - 1)).astype(F32)

    def place(o, at):
        where_ref[o] = at
        tile = lax.shift_right_logical(at, 8)
        offset = at & (SLOTS - 1)
        turned = pltpu.roll(source_ref[0, pl.ds(o, 1), :], offset, 1)
        index_ref[pl.ds(tile, 1), :] = jnp.where(
            lane >= offset, turned, index_ref[pl.ds(tile, 1), :]
        )
        index_ref[pl.ds(tile + 1, 1), :] = turned
        return at + count_ref[0, o]

    where_ref[slabs] = lax.fori_loop(0, slabs, place, jnp.int32(0))


def unpack_coarse(plane_ref):
    return [
        plane_ref[0, (p // 2) * HY : (p // 2) * HY + HY, (p % 2) * HZ : (p % 2) * HZ + HZ]
        for p in range(HX)
    ]


def fine_kernel(
    material_ref,
    count_ref,
    where_ref,
    force_ref,
    stiff_ref,
    below_ref,
    above_ref,
    index_ref,
    smooth_ref,
    coef_out_ref,
    diag_out_ref,
    coarse_ref,
    picked_ref,
    coef,
    diag,
    inverse,
    force,
    first,
    second,
    table,
    sums,
    residual,
    found,
):
    slab = lax.axis_index("space")
    slabs = lax.axis_size("space")
    sh = Shifts((NY, NZ))
    own = own_plane(material_ref)
    has_below = slab > 0
    has_above = slab < slabs - 1
    for p in range(CX):
        coef[3 + p] = stiff_ref[p] * own
    for p in range(3):
        coef[p] = jnp.where(has_below, below_ref[9 + p], 0.0)
        coef[3 + CX + p] = jnp.where(has_above, above_ref[9 + p], 0.0)
    for c in range(3):
        first[c, 0] = jnp.where(has_below, below_ref[3 * c], 0.0)
        first[c, FINE_PLANES - 1] = jnp.where(has_above, above_ref[3 * c + 2], 0.0)
        for p in range(2):
            force[c, 1 + p] = below_ref[3 * c + 1 + p]
            force[c, 3 + CX + p] = above_ref[3 * c + p]
        for p in range(CX):
            force[c, 3 + p] = force_ref[0, c, p]

    @pl.loop(1, FINE_PLANES - 1)
    def _(p):
        d = diagonal(sh, coef[p - 1], coef[p], coef[p + 1])
        place = slab * CX + p - 3
        valid = jnp.logical_and(place >= 0, place < slabs * CX)
        inv = jnp.where(valid, 1.0 / d, 0.0)
        diag[p] = d
        inverse[p] = inv
        for c in range(3):
            first[c, p] = force[c, p] * inv * (1.0 / MIDPOINT)

    def remainder(src, p, base):
        planes = [[src[c, p + o - base] for c in range(3)] for o in (-1, 0, 1)]
        image = operate(sh, *planes, coef[p - 1], coef[p], coef[p + 1], diag[p])
        return planes[1], [force[c, p] - image[c] for c in range(3)]

    (keep_2, gain_2), (keep_3, gain_3) = step_factors(FINE_STEPS)

    @pl.loop(1, FINE_PLANES - 1)
    def _(p):
        value, left = remainder(first, p, 0)
        for c in range(3):
            second[c, p] = (1.0 + keep_2) * value[c] + gain_2 * (left[c] * inverse[p])

    @pl.loop(2, FINE_PLANES - 2)
    def _(p):
        value, left = remainder(second, p, 0)
        for c in range(3):
            step = keep_3 * (value[c] - first[c, p]) + gain_3 * (left[c] * inverse[p])
            smooth_ref[c, p - 2] = value[c] + step

    @pl.loop(3, FINE_PLANES - 3)
    def _(p):
        _, left = remainder(smooth_ref, p, 2)
        for c in range(3):
            row = pl.multiple_of(c * (CX * NY) + (p - 3) * NY, NY)
            residual[pl.ds(row, NY), :] = left[c]
            head = left[c].astype(BF16)
            table[pl.ds(row, NY), 0:NZ] = head
            table[pl.ds(row, NY), NZ : 2 * NZ] = (left[c] - head.astype(F32)).astype(BF16)

    for p in range(CX + 2):
        coef_out_ref[p] = coef[p + 2]
    for p in range(CX):
        diag_out_ref[p] = diag[p + 3]

    planes = residual[...].reshape(3 * HX, 2, NY, NZ)
    pairs = (planes[:, 0] + planes[:, 1]).reshape(3 * HX * NY, NZ)
    coarse_ref[...] = 0.5 * coarse_sum(pairs, sums)

    plane_rows = CX * NY
    groups = plane_rows // 8
    column = lax.broadcasted_iota(jnp.int32, (NZ, SLOTS), 0).astype(F32).astype(BF16)
    line = lax.broadcasted_iota(jnp.int32, (8, SLOTS), 0)
    lane = lax.broadcasted_iota(jnp.int32, (8, SLOTS), 1)
    one = jnp.ones((), BF16)
    zero = jnp.zeros((), BF16)

    def pick(t):
        index = index_ref[pl.ds(t, 1), :]
        group = lax.shift_right_logical(index, 11)
        inner = line == (lax.shift_right_logical(index, 8) & 7)
        hot = jnp.where(column == (index & (NZ - 1)).astype(F32).astype(BF16), one, zero)
        both = jnp.dot(table[:, 0:NZ], hot, preferred_element_type=F32) + jnp.dot(
            table[:, NZ : 2 * NZ], hot, preferred_element_type=F32
        )
        for c in range(3):
            held = both[c * plane_rows : c * plane_rows + 8, :]
            for g in range(1, groups):
                at = c * plane_rows + 8 * g
                held = jnp.where(group == g, both[at : at + 8, :], held)
            found[t, c : c + 1, :] = jnp.sum(jnp.where(inner, held, 0.0), axis=0, keepdims=True)

    @pl.loop(0, lax.shift_right_logical(where_ref[slabs] + 2 * SLOTS - 1, 9))
    def _(pair):
        pick(2 * pair)
        pick(2 * pair + 1)

    @pl.loop(0, slabs, unroll=4)
    def _(o):
        at = where_ref[o]
        tile = lax.shift_right_logical(at, 8)
        offset = at & (SLOTS - 1)
        joined = jnp.where(lane >= offset, found[tile], found[tile + 1])
        turned = pltpu.roll(joined, SLOTS - offset, 1)
        turned = jnp.where(lane < count_ref[0, o], turned, 0.0)
        for c in range(3):
            picked_ref[pl.ds(o, 1), c * SLOTS : (c + 1) * SLOTS] = turned[c : c + 1, :]


def coarse_extent(below_pack_ref, coarse_ref, above_pack_ref, slab, slabs):
    low = [jnp.where(slab > 0, x, 0.0) for x in unpack_coarse(below_pack_ref)]
    high = [jnp.where(slab < slabs - 1, x, 0.0) for x in unpack_coarse(above_pack_ref)]
    return low + [coarse_ref[p] for p in range(HX)] + high


def gather_kernel(
    arrived_ref,
    line_ref,
    column_ref,
    local_ref,
    coef_below_ref,
    coef_ref,
    coef_above_ref,
    source_ref,
    low_ref,
    high_ref,
    total,
):
    slab = lax.axis_index("space")
    slabs = lax.axis_size("space")
    lines = HX * HY
    column = lax.broadcasted_iota(jnp.int32, (HZ, SLOTS), 0).astype(F32).astype(BF16)
    line = lax.broadcasted_iota(jnp.int32, (lines, SLOTS), 0).astype(F32).astype(BF16)
    total[...] = jnp.zeros_like(total)
    one = jnp.ones((), BF16)
    zero = jnp.zeros((), BF16)

    @pl.loop(0, slabs, step=4)
    def _(s):
        add = None
        for u in range(4):
            hot = jnp.where(column == column_ref[pl.ds(s + u, 1), :].astype(BF16), one, zero)
            chosen = line == line_ref[pl.ds(s + u, 1), :].astype(BF16)
            heads, tails = [], []
            for c in range(3):
                value = arrived_ref[pl.ds(s + u, 1), c * SLOTS : (c + 1) * SLOTS]
                head = value.astype(BF16)
                tail = (value - head.astype(F32)).astype(BF16)
                heads.append(jnp.where(chosen, head, zero))
                tails.append(jnp.where(chosen, tail, zero))
            part = lax.dot_general(
                jnp.concatenate(heads + tails, axis=0),
                hot,
                (((1,), (1,)), ((), ())),
                preferred_element_type=F32,
            )
            add = part if add is None else add + part
        total[...] += add

    count = 3 * lines
    source = (total[0:count, :] + total[count : 2 * count, :] + local_ref[...]).reshape(3, HX, HY, HZ)
    source_ref[...] = source
    low_ref[...] = source
    high_ref[...] = source
    coef = coarse_extent(coef_below_ref, coef_ref, coef_above_ref, slab, slabs)
    sh = Shifts((HY, HZ))
    for ref, p in ((high_ref, 0), (low_ref, HX - 1)):
        d = diagonal(sh, coef[HX + p - 1], coef[HX + p], coef[HX + p + 1])
        scale = (1.0 / MIDPOINT) / d
        for c in range(3):
            ref[c, p] = source[c, p] * scale


def coarse_kernel(
    source_ref,
    below_ref,
    above_ref,
    coef_below_ref,
    coarse_coef_ref,
    coef_above_ref,
    smooth_ref,
    coef_ref,
    diag_ref,
    moved_ref,
    kept_ref,
    sent_1_ref,
    sent_2_ref,
    sent_3_ref,
    rows,
    field,
    energy,
):
    slab = lax.axis_index("space")
    slabs = lax.axis_size("space")
    mine = lax.axis_index("load")
    coef = jnp.stack(coarse_extent(coef_below_ref, coarse_coef_ref, coef_above_ref, slab, slabs))
    source = [
        jnp.concatenate([below_ref[c], source_ref[c], above_ref[c]], axis=0) for c in range(3)
    ]
    count = 3 * HX - 2
    place = lax.broadcasted_iota(jnp.int32, (count, HY, HZ), 0) + (slab * HX - HX + 1)
    valid = jnp.logical_and(place >= 0, place < slabs * HX)
    diag = diagonal(Shifts((count, HY, HZ)), coef[:-2], coef[1:-1], coef[2:])
    inverse = jnp.where(valid, 1.0 / diag, 0.0)
    older = None
    value = []
    for c in range(3):
        low = jnp.where(slab > 0, source[c][:1], 0.0)
        high = jnp.where(slab < slabs - 1, source[c][-1:], 0.0)
        inner = source[c][1:-1] * inverse * (1.0 / MIDPOINT)
        value.append(jnp.concatenate([low, inner, high], axis=0))
    for number, (keep, gain) in enumerate(step_factors(COARSE_STEPS)):
        size = count - 2 * number
        inside = slice(number, number + size)
        window = slice(number + 1, number + 1 + size)
        image = operate(
            Shifts((size, HY, HZ)),
            [v[:-2] for v in value],
            [v[1:-1] for v in value],
            [v[2:] for v in value],
            coef[number : number + size],
            coef[window],
            coef[number + 2 : number + 2 + size],
            diag[inside],
        )
        newer = []
        for c in range(3):
            mid = value[c][1:-1]
            change = mid if older is None else mid - older[c][2:-2]
            left = source[c][window] - image[c]
            newer.append(mid + keep * change + gain * (left * inverse[inside]))
        older, value = value, newer

    planes = HX + 2
    flat = jnp.concatenate([v.reshape(planes * HY, HZ) for v in value], axis=0)
    fine = lax.broadcasted_iota(jnp.int32, (HZ, NZ), 1)
    half = lax.broadcasted_iota(jnp.int32, (HZ, NZ), 0)
    repeat = (lax.shift_right_logical(fine, 1) == half).astype(F32)
    amount = 3 * planes * HY
    rows[pl.ds(0, amount, stride=2), :] = flat
    rows[pl.ds(1, amount, stride=2), :] = flat
    wide = jnp.dot(rows[...], repeat, precision=HIGHEST, preferred_element_type=F32)
    for c in range(3):
        for p in range(CX + 2):
            at = (c * planes + (p + 1) // 2) * NY
            moved = smooth_ref[c, p] + wide[at : at + NY, :]
            field[c, p] = moved
            if 0 < p <= CX:
                moved_ref[0, c, p - 1] = moved

    sh = Shifts((NY, NZ))

    @pl.loop(1, CX + 1)
    def _(p):
        planes = [[field[c, p + o] for c in range(3)] for o in (-1, 0, 1)]
        image = operate(
            sh, *planes, coef_ref[p - 1], coef_ref[p], coef_ref[p + 1], diag_ref[p - 1]
        )
        mid = planes[1]
        energy[p - 1] = mid[0] * image[0] + mid[1] * image[1] + mid[2] * image[2]

    part = NY // 4
    for q in range(4):

        @pl.when(mine == q)
        def _():
            for k, ref in enumerate((kept_ref, sent_1_ref, sent_2_ref, sent_3_ref)):
                y = ((q + k) % 4) * part
                ref[...] = energy[:, y : y + part, :]


VMEM = pl.BlockSpec(memory_space=pltpu.VMEM)
HBM = pl.BlockSpec(memory_space=pltpu.HBM)
SMEM = pl.BlockSpec(memory_space=pltpu.SMEM)
PARAMS = pltpu.CompilerParams(vmem_limit_bytes=32 << 20)


def shaped(*shape):
    return jax.ShapeDtypeStruct(shape, F32)


def body(load_force, stiffness, material, face_src, face_count, face_dst):
    slabs = lax.axis_size("space")
    forward = [(i, (i + 1) % slabs) for i in range(slabs)]
    backward = [(target, origin) for origin, target in forward]
    pack_low, pack_high, coarse_coef = pl.pallas_call(
        pack_kernel,
        out_shape=(shaped(PACK, NY, NZ), shaped(PACK, NY, NZ), shaped(HX, HY, HZ)),
        in_specs=[HBM, HBM, HBM],
        out_specs=(VMEM, VMEM, VMEM),
        scratch_shapes=[
            pltpu.SMEM((1, NY // BY), jnp.int32),
            pltpu.VMEM((CX, NY, NZ), F32),
            pltpu.VMEM((HX * NY, HZ), F32),
            pltpu.SemaphoreType.DMA((8,)),
        ],
        compiler_params=PARAMS,
        name="pack",
    )(material, load_force, stiffness)
    below = lax.ppermute(pack_high, "space", forward)
    above = lax.ppermute(pack_low, "space", backward)

    rows_kept = slabs + 8
    line, column, where, index = pl.pallas_call(
        plan_kernel,
        out_shape=(
            shaped(slabs, SLOTS),
            shaped(slabs, SLOTS),
            jax.ShapeDtypeStruct((slabs + 1,), jnp.int32),
            jax.ShapeDtypeStruct((rows_kept, SLOTS), jnp.int32),
        ),
        in_specs=[SMEM, VMEM, VMEM],
        out_specs=(VMEM, VMEM, SMEM, VMEM),
        compiler_params=PARAMS,
        name="plan",
    )(face_count, face_src, face_dst)

    smooth, coef, diag, local, picked = pl.pallas_call(
        fine_kernel,
        out_shape=(
            shaped(3, CX + 2, NY, NZ),
            shaped(CX + 2, NY, NZ),
            shaped(CX, NY, NZ),
            shaped(3 * HX * HY, HZ),
            shaped(slabs, 3 * SLOTS),
        ),
        in_specs=[SMEM, SMEM, SMEM, VMEM, VMEM, VMEM, VMEM, VMEM],
        out_specs=(VMEM, VMEM, VMEM, VMEM, VMEM),
        scratch_shapes=[
            pltpu.VMEM((COEF_PLANES, NY, NZ), F32),
            pltpu.VMEM((FINE_PLANES, NY, NZ), F32),
            pltpu.VMEM((FINE_PLANES, NY, NZ), F32),
            pltpu.VMEM((3, FINE_PLANES, NY, NZ), F32),
            pltpu.VMEM((3, FINE_PLANES, NY, NZ), F32),
            pltpu.VMEM((3, FINE_PLANES, NY, NZ), F32),
            pltpu.VMEM((3 * CX * NY, 2 * NZ), BF16),
            pltpu.VMEM((3 * HX * NY, HZ), F32),
            pltpu.VMEM((3 * CX * NY, NZ), F32),
            pltpu.VMEM((rows_kept, 8, SLOTS), F32),
        ],
        compiler_params=PARAMS,
        name="fine",
    )(material, face_count, where, load_force, stiffness, below, above, index)

    arrived = lax.all_to_all(picked, "space", split_axis=0, concat_axis=0, tiled=True)

    tail = pl.BlockSpec((1, NY, NZ), lambda i: (PACK - 1, 0, 0))

    def whole(*shape):
        return pl.BlockSpec(shape, lambda i: (0,) * len(shape))

    grid_shape = (3, HX, HY, HZ)
    source, send_low, send_high = pl.pallas_call(
        gather_kernel,
        grid=(1,),
        out_shape=(shaped(*grid_shape), shaped(*grid_shape), shaped(*grid_shape)),
        in_specs=[
            whole(slabs, 3 * SLOTS),
            whole(slabs, SLOTS),
            whole(slabs, SLOTS),
            whole(3 * HX * HY, HZ),
            tail,
            whole(HX, HY, HZ),
            tail,
        ],
        out_specs=(whole(*grid_shape), whole(*grid_shape), whole(*grid_shape)),
        scratch_shapes=[
            pltpu.VMEM((6 * HX * HY, HZ), F32),
        ],
        compiler_params=PARAMS,
        name="reflux",
    )(arrived, line, column, local, below, coarse_coef, above)
    source_below = lax.ppermute(send_high, "space", forward)
    source_above = lax.ppermute(send_low, "space", backward)

    part = (CX, NY // 4, NZ)
    moved, kept, sent_1, sent_2, sent_3 = pl.pallas_call(
        coarse_kernel,
        grid=(1,),
        out_shape=(shaped(1, 3, CX, NY, NZ),) + (shaped(*part),) * 4,
        in_specs=[
            whole(*grid_shape),
            whole(*grid_shape),
            whole(*grid_shape),
            tail,
            whole(HX, HY, HZ),
            tail,
            whole(3, CX + 2, NY, NZ),
            whole(CX + 2, NY, NZ),
            whole(CX, NY, NZ),
        ],
        out_specs=(whole(1, 3, CX, NY, NZ),) + (whole(*part),) * 4,
        scratch_shapes=[
            pltpu.VMEM((3 * (HX + 2) * NY, HZ), F32),
            pltpu.VMEM((3, CX + 2, NY, NZ), F32),
            pltpu.VMEM((CX, NY, NZ), F32),
        ],
        compiler_params=PARAMS,
        name="coarse",
    )(source, source_below, source_above, below, coarse_coef, above, smooth, coef, diag)
    got = [
        lax.ppermute(piece, "load", [(i, (i + k) % 4) for i in range(4)])
        for k, piece in ((1, sent_1), (2, sent_2), (3, sent_3))
    ]
    mine = lax.axis_index("load")
    ident = jnp.where(mine < 2, material[0, 0], material[0, 1])
    base = np.array(MODULI, np.float32)
    factors = jnp.asarray((base[None, :] - base[:, None]) / base[:, None])
    scale = jnp.where(ident == 0, factors[0], jnp.where(ident == 1, factors[1], factors[2]))
    total = kept + got[0] + got[1] + got[2]
    sensitivity = scale[:, None, None, None] * total[None]
    return moved, sensitivity


def solution(mesh):
    return jax.shard_map(
        body,
        mesh=mesh,
        in_specs=(
            P("load", None, "space", None, None),
            P("space", None, None),
            P("space", None),
            P("space", None, None),
            P("space", None),
            P("space", None, None),
        ),
        out_specs=(P("load", None, "space", None, None), P(None, "space", "load", None)),
        check_vma=False,
    )
```

```python
import jax
import jax.numpy as jnp
import numpy as np
from jax import lax
from jax.experimental import pallas as pl
from jax.experimental.pallas import tpu as pltpu
from jax.sharding import PartitionSpec as P

CX = 8
NY = 16
NZ = 256
BY = 8
SLOTS = 256
FINE_STEPS = 3
COARSE_STEPS = 4

UPPER_EDGE = 2.1
LOWER_EDGE = 0.15
COUPLING = 0.1
MODULI = (1.0, 0.55, 0.25)

MIDPOINT = (UPPER_EDGE + LOWER_EDGE) / 2.0
HALFWIDTH = (UPPER_EDGE - LOWER_EDGE) / 2.0

HX, HY, HZ = CX // 2, NY // 2, NZ // 2
FINE_PLANES = CX + 6
COEF_PLANES = CX + 6
PACK = 3 * 3 + 3 + 1
BATCH = 32
UNROLL = 2
F32 = jnp.float32
BF16 = jnp.bfloat16
HIGHEST = lax.Precision.HIGHEST


def step_factors(count):
    ratio = MIDPOINT / HALFWIDTH
    rho_old = 1.0 / ratio
    factors = []
    for _ in range(1, count):
        rho_new = 1.0 / (2.0 * ratio - rho_old)
        factors.append((rho_new * rho_old, 2.0 * rho_new / HALFWIDTH))
        rho_old = rho_new
    return factors


def tiles(plane):
    return jnp.stack([plane[:HY, :HZ], plane[:HY, HZ:], plane[HY:, :HZ], plane[HY:, HZ:]])


def plane(quarters):
    return jnp.concatenate(
        [
            jnp.concatenate([quarters[0], quarters[1]], axis=1),
            jnp.concatenate([quarters[2], quarters[3]], axis=1),
        ],
        axis=0,
    )


class Shifts:
    def __init__(self, count, quarters):
        shape = (count, HY, HZ)
        y = lax.broadcasted_iota(jnp.int32, shape, 1)
        z = lax.broadcasted_iota(jnp.int32, shape, 2)
        self.quarters = quarters
        self.first_y, self.last_y = y == 0, y == HY - 1
        self.first_z, self.last_z = z == 0, z == HZ - 1

    def fill(self, turned, order):
        if not self.quarters:
            return 0.0
        zero = jnp.zeros((HY, HZ), F32)
        return jnp.stack([zero if i is None else turned[i] for i in order])

    def up_y(self, x):
        turned = pltpu.roll(x, HY - 1, 1)
        return jnp.where(self.last_y, self.fill(turned, (2, 3, None, None)), turned)

    def down_y(self, x):
        turned = pltpu.roll(x, 1, 1)
        return jnp.where(self.first_y, self.fill(turned, (None, None, 0, 1)), turned)

    def up_z(self, x):
        turned = pltpu.roll(x, HZ - 1, 2)
        return jnp.where(self.last_z, self.fill(turned, (1, None, 3, None)), turned)

    def down_z(self, x):
        turned = pltpu.roll(x, 1, 2)
        return jnp.where(self.first_z, self.fill(turned, (None, 0, None, 2)), turned)

    def spread_y(self, x):
        return x + 0.5 * (self.up_y(x) + self.down_y(x))

    def spread_z(self, x):
        return x + 0.5 * (self.up_z(x) + self.down_z(x))

    def spread(self, x):
        return self.spread_z(self.spread_y(x))


def diagonal(sh, k_below, k_mid, k_above):
    return (3.0 / 7.0) * k_mid + (1.0 / 14.0) * sh.spread(k_mid + 0.5 * (k_below + k_above))


def operate(sh, below, mid, above, k_below, k_mid, k_above, diag):
    centre = diag + (1.0 / 7.0) * k_mid
    slope = [above[c] - below[c] for c in range(3)]
    cross = 0.25 * COUPLING
    plain = [mid[c] + 0.5 * (below[c] + above[c]) for c in range(3)]

    def close_y(x, skew):
        x, skew, own = (1.0 / 28.0) * x, cross * skew, (1.0 / 14.0) * x
        return own + sh.up_y(x + skew) + sh.down_y(x - skew)

    def close_z(x, skew):
        x, skew, own = (1.0 / 28.0) * x, cross * skew, (1.0 / 14.0) * x
        return own + sh.up_z(x + skew) + sh.down_z(x - skew)

    inner = (
        close_z(sh.spread_y(plain[0]), slope[2])
        + cross * (sh.up_y(slope[1]) - sh.down_y(slope[1])),
        close_y(sh.spread_z(plain[1]), slope[0] + (sh.up_z(mid[2]) - sh.down_z(mid[2]))),
        close_z(sh.spread_y(plain[2]), slope[0] + (sh.up_y(mid[1]) - sh.down_y(mid[1]))),
    )
    result = []
    for c in range(3):
        scaled = sh.spread(k_mid * mid[c] + 0.5 * (k_below * below[c] + k_above * above[c]))
        result.append(centre * mid[c] - k_mid * inner[c] - (1.0 / 14.0) * scaled)
    return result


def modulus(material_ref, brick):
    ident = material_ref[0, brick]
    return jnp.where(ident == 0, MODULI[0], jnp.where(ident == 1, MODULI[1], MODULI[2])).astype(F32)


def own_plane(material_ref):
    row = lax.broadcasted_iota(jnp.int32, (NY, NZ), 0)
    return jnp.where(row < BY, modulus(material_ref, 0), modulus(material_ref, 1))


def pair_columns():
    fine = lax.broadcasted_iota(jnp.int32, (NZ, HZ), 0)
    coarse = lax.broadcasted_iota(jnp.int32, (NZ, HZ), 1)
    return (lax.shift_right_logical(fine, 1) == coarse).astype(F32)


def coarse_sum(planes, narrow_ref):
    narrow_ref[...] = jnp.dot(
        planes, pair_columns(), precision=HIGHEST, preferred_element_type=F32
    )
    rows = narrow_ref.shape[0] // 2
    return narrow_ref[pl.ds(0, rows, stride=2), :] + narrow_ref[pl.ds(1, rows, stride=2), :]


def pack_kernel(
    material_hbm, force_hbm, stiff_hbm,
    low_ref, high_ref, coarse_ref, coef_ref,
    material, stiff, sums, sems,
):
    copies = [
        pltpu.make_async_copy(stiff_hbm, stiff, sems.at[0]),
        pltpu.make_async_copy(material_hbm, material, sems.at[1]),
    ]
    for c in range(3):
        rows = pl.ds(3 * c, 3)
        copies += [
            pltpu.make_async_copy(force_hbm.at[0, c, pl.ds(0, 3)], low_ref.at[rows], sems.at[2 + c]),
            pltpu.make_async_copy(
                force_hbm.at[0, c, pl.ds(CX - 3, 3)], high_ref.at[rows], sems.at[5 + c]
            ),
        ]
    for copy in copies:
        copy.start()
    for copy in copies:
        copy.wait()
    own = own_plane(material)
    sh = Shifts(4, True)
    coef = [stiff[p] * own for p in range(CX)]
    for p in range(CX):
        coef_ref[p] = coef[p]
    for p in range(3):
        low_ref[9 + p] = coef[p]
        high_ref[9 + p] = coef[CX - 3 + p]
    for ref, p, slot in ((low_ref, 2, 2), (high_ref, CX - 3, 0)):
        scale = (1.0 / MIDPOINT) / diagonal(sh, *[tiles(coef[p + o]) for o in (-1, 0, 1)])
        scale = plane(scale)
        for c in range(3):
            ref[3 * c + slot] = ref[3 * c + slot] * scale
    pairs = jnp.concatenate([coef[2 * p] + coef[2 * p + 1] for p in range(HX)], axis=0)
    coarse = (0.125 * coarse_sum(pairs, sums)).reshape(HX, HY, HZ)
    coarse_ref[...] = coarse
    for p in range(HX):
        y, z = (p // 2) * HY, (p % 2) * HZ
        low_ref[PACK - 1, y : y + HY, z : z + HZ] = coarse[p]
        high_ref[PACK - 1, y : y + HY, z : z + HZ] = coarse[p]


def plan_kernel(count_ref, source_ref, target_ref, line_ref, column_ref, where_ref, index_ref):
    slabs = count_ref.shape[1]
    lane = lax.broadcasted_iota(jnp.int32, (1, SLOTS), 1)
    cells = target_ref[0]
    line_ref[...] = lax.shift_right_logical(cells, 7).astype(F32)
    column_ref[...] = (cells & (HZ - 1)).astype(F32)

    def place(o, at):
        where_ref[o] = at
        tile = lax.shift_right_logical(at, 8)
        offset = at & (SLOTS - 1)
        turned = pltpu.roll(source_ref[0, pl.ds(o, 1), :], offset, 1)
        index_ref[pl.ds(tile, 1), :] = jnp.where(
            lane >= offset, turned, index_ref[pl.ds(tile, 1), :]
        )
        index_ref[pl.ds(tile + 1, 1), :] = turned
        return at + count_ref[0, o]

    where_ref[slabs] = lax.fori_loop(0, slabs, place, jnp.int32(0))


def unpack_coarse(plane_ref):
    return [
        plane_ref[0, (p // 2) * HY : (p // 2) * HY + HY, (p % 2) * HZ : (p % 2) * HZ + HZ]
        for p in range(HX)
    ]


def fine_kernel(
    count_ref,
    where_ref,
    force_ref,
    own_ref,
    below_ref,
    above_ref,
    index_ref,
    smooth_ref,
    coef_out_ref,
    diag_out_ref,
    coarse_ref,
    picked_ref,
    coef,
    diag,
    inverse,
    force,
    first,
    second,
    table,
    sums,
    residual,
    found,
):
    slab = lax.axis_index("space")
    slabs = lax.axis_size("space")
    sh = Shifts(4, True)
    has_below = slab > 0
    has_above = slab < slabs - 1
    for p in range(CX):
        coef[3 + p] = own_ref[p]
    for p in range(3):
        coef[p] = jnp.where(has_below, below_ref[9 + p], 0.0)
        coef[3 + CX + p] = jnp.where(has_above, above_ref[9 + p], 0.0)
    for c in range(3):
        first[c, 0] = jnp.where(has_below, below_ref[3 * c], 0.0)
        first[c, FINE_PLANES - 1] = jnp.where(has_above, above_ref[3 * c + 2], 0.0)
        for p in range(2):
            force[c, 1 + p] = below_ref[3 * c + 1 + p]
            force[c, 3 + CX + p] = above_ref[3 * c + p]
        for p in range(CX):
            force[c, 3 + p] = force_ref[0, c, p]

    @pl.loop(1, FINE_PLANES - 1)
    def _(p):
        d = plane(diagonal(sh, *[tiles(coef[p + o]) for o in (-1, 0, 1)]))
        place = slab * CX + p - 3
        valid = jnp.logical_and(place >= 0, place < slabs * CX)
        inv = jnp.where(valid, 1.0 / d, 0.0)
        diag[p] = d
        inverse[p] = inv
        for c in range(3):
            first[c, p] = force[c, p] * inv * (1.0 / MIDPOINT)

    def remainder(src, p, base):
        planes = [[tiles(src[c, p + o - base]) for c in range(3)] for o in (-1, 0, 1)]
        factors = [tiles(coef[p + o]) for o in (-1, 0, 1)]
        image = operate(sh, *planes, *factors, tiles(diag[p]))
        return planes[1], [tiles(force[c, p]) - image[c] for c in range(3)]

    (keep_2, gain_2), (keep_3, gain_3) = step_factors(FINE_STEPS)

    @pl.loop(1, FINE_PLANES - 1, unroll=UNROLL)
    def _(p):
        value, left = remainder(first, p, 0)
        inv = tiles(inverse[p])
        for c in range(3):
            second[c, p] = plane((1.0 + keep_2) * value[c] + gain_2 * (left[c] * inv))

    @pl.loop(2, FINE_PLANES - 2, unroll=UNROLL)
    def _(p):
        value, left = remainder(second, p, 0)
        inv = tiles(inverse[p])
        for c in range(3):
            step = keep_3 * (value[c] - tiles(first[c, p])) + gain_3 * (left[c] * inv)
            smooth_ref[c, p - 2] = plane(value[c] + step)

    @pl.loop(3, FINE_PLANES - 3, unroll=UNROLL)
    def _(p):
        _, left = remainder(smooth_ref, p, 2)
        for c in range(3):
            row = pl.multiple_of(c * (CX * NY) + (p - 3) * NY, NY)
            whole = plane(left[c])
            residual[pl.ds(row, NY), :] = whole
            head = whole.astype(BF16)
            table[pl.ds(row, NY), 0:NZ] = head
            table[pl.ds(row, NY), NZ : 2 * NZ] = (whole - head.astype(F32)).astype(BF16)

    for p in range(CX + 2):
        coef_out_ref[p] = coef[p + 2]
    for p in range(CX):
        diag_out_ref[p] = diag[p + 3]

    planes = residual[...].reshape(3 * HX, 2, NY, NZ)
    pairs = (planes[:, 0] + planes[:, 1]).reshape(3 * HX * NY, NZ)
    coarse_ref[...] = 0.5 * coarse_sum(pairs, sums)

    plane_rows = CX * NY
    groups = plane_rows // 8
    column = lax.broadcasted_iota(jnp.int32, (NZ, SLOTS), 0).astype(F32).astype(BF16)
    line = lax.broadcasted_iota(jnp.int32, (8, SLOTS), 0)
    lane = lax.broadcasted_iota(jnp.int32, (8, SLOTS), 1)
    one = jnp.ones((), BF16)
    zero = jnp.zeros((), BF16)

    def pick(t):
        index = index_ref[pl.ds(t, 1), :]
        group = lax.shift_right_logical(index, 11)
        inner = line == (lax.shift_right_logical(index, 8) & 7)
        hot = jnp.where(column == (index & (NZ - 1)).astype(F32).astype(BF16), one, zero)
        both = jnp.dot(table[:, 0:NZ], hot, preferred_element_type=F32) + jnp.dot(
            table[:, NZ : 2 * NZ], hot, preferred_element_type=F32
        )
        for c in range(3):
            held = both[c * plane_rows : c * plane_rows + 8, :]
            for g in range(1, groups):
                at = c * plane_rows + 8 * g
                held = jnp.where(group == g, both[at : at + 8, :], held)
            found[t, c : c + 1, :] = jnp.sum(jnp.where(inner, held, 0.0), axis=0, keepdims=True)

    @pl.loop(0, lax.shift_right_logical(where_ref[slabs] + 2 * SLOTS - 1, 9))
    def _(pair):
        pick(2 * pair)
        pick(2 * pair + 1)

    @pl.loop(0, slabs, unroll=4)
    def _(o):
        at = where_ref[o]
        tile = lax.shift_right_logical(at, 8)
        offset = at & (SLOTS - 1)
        joined = jnp.where(lane >= offset, found[tile], found[tile + 1])
        turned = pltpu.roll(joined, SLOTS - offset, 1)
        turned = jnp.where(lane < count_ref[0, o], turned, 0.0)
        for c in range(3):
            picked_ref[pl.ds(o, 1), c * SLOTS : (c + 1) * SLOTS] = turned[c : c + 1, :]


def coarse_extent(below_pack_ref, coarse_ref, above_pack_ref, slab, slabs):
    low = [jnp.where(slab > 0, x, 0.0) for x in unpack_coarse(below_pack_ref)]
    high = [jnp.where(slab < slabs - 1, x, 0.0) for x in unpack_coarse(above_pack_ref)]
    return low + [coarse_ref[p] for p in range(HX)] + high


def gather_kernel(
    arrived_ref,
    line_ref,
    column_ref,
    local_ref,
    coef_below_ref,
    coef_ref,
    coef_above_ref,
    source_ref,
    low_ref,
    high_ref,
    total,
):
    slab = lax.axis_index("space")
    slabs = lax.axis_size("space")
    lines = HX * HY
    column = lax.broadcasted_iota(jnp.int32, (HZ, SLOTS), 0).astype(F32).astype(BF16)
    line = lax.broadcasted_iota(jnp.int32, (lines, SLOTS), 0).astype(F32).astype(BF16)
    total[...] = jnp.zeros_like(total)
    one = jnp.ones((), BF16)
    zero = jnp.zeros((), BF16)

    @pl.loop(0, slabs, step=BATCH)
    def _(s):
        hots, lefts = [], []
        for u in range(BATCH):
            hots.append(jnp.where(column == column_ref[pl.ds(s + u, 1), :].astype(BF16), one, zero))
            chosen = line == line_ref[pl.ds(s + u, 1), :].astype(BF16)
            heads, tails = [], []
            for c in range(3):
                value = arrived_ref[pl.ds(s + u, 1), c * SLOTS : (c + 1) * SLOTS]
                head = value.astype(BF16)
                tail = (value - head.astype(F32)).astype(BF16)
                heads.append(jnp.where(chosen, head, zero))
                tails.append(jnp.where(chosen, tail, zero))
            lefts.append(jnp.concatenate(heads + tails, axis=0))
        total[...] += lax.dot_general(
            jnp.concatenate(lefts, axis=1),
            jnp.concatenate(hots, axis=1),
            (((1,), (1,)), ((), ())),
            preferred_element_type=F32,
        )

    count = 3 * lines
    source = (total[0:count, :] + total[count : 2 * count, :] + local_ref[...]).reshape(3, HX, HY, HZ)
    source_ref[...] = source
    low_ref[...] = source
    high_ref[...] = source
    coef = coarse_extent(coef_below_ref, coef_ref, coef_above_ref, slab, slabs)
    sh = Shifts(1, False)
    for ref, p in ((high_ref, 0), (low_ref, HX - 1)):
        d = diagonal(sh, *[coef[HX + p + o][None] for o in (-1, 0, 1)])
        scale = (1.0 / MIDPOINT) / d[0]
        for c in range(3):
            ref[c, p] = source[c, p] * scale


def coarse_kernel(
    source_ref,
    below_ref,
    above_ref,
    coef_below_ref,
    coarse_coef_ref,
    coef_above_ref,
    smooth_ref,
    coef_ref,
    diag_ref,
    moved_ref,
    kept_ref,
    sent_1_ref,
    sent_2_ref,
    rows,
    field,
    energy,
):
    slab = lax.axis_index("space")
    slabs = lax.axis_size("space")
    mine = lax.axis_index("load")
    coef = jnp.stack(coarse_extent(coef_below_ref, coarse_coef_ref, coef_above_ref, slab, slabs))
    source = [
        jnp.concatenate([below_ref[c], source_ref[c], above_ref[c]], axis=0) for c in range(3)
    ]
    count = 3 * HX - 2
    place = lax.broadcasted_iota(jnp.int32, (count, HY, HZ), 0) + (slab * HX - HX + 1)
    valid = jnp.logical_and(place >= 0, place < slabs * HX)
    diag = diagonal(Shifts(count, False), coef[:-2], coef[1:-1], coef[2:])
    inverse = jnp.where(valid, 1.0 / diag, 0.0)
    older = None
    value = []
    for c in range(3):
        low = jnp.where(slab > 0, source[c][:1], 0.0)
        high = jnp.where(slab < slabs - 1, source[c][-1:], 0.0)
        inner = source[c][1:-1] * inverse * (1.0 / MIDPOINT)
        value.append(jnp.concatenate([low, inner, high], axis=0))
    for number, (keep, gain) in enumerate(step_factors(COARSE_STEPS)):
        size = count - 2 * number
        inside = slice(number, number + size)
        window = slice(number + 1, number + 1 + size)
        image = operate(
            Shifts(size, False),
            [v[:-2] for v in value],
            [v[1:-1] for v in value],
            [v[2:] for v in value],
            coef[number : number + size],
            coef[window],
            coef[number + 2 : number + 2 + size],
            diag[inside],
        )
        newer = []
        for c in range(3):
            mid = value[c][1:-1]
            change = mid if older is None else mid - older[c][2:-2]
            left = source[c][window] - image[c]
            newer.append(mid + keep * change + gain * (left * inverse[inside]))
        older, value = value, newer

    planes = HX + 2
    flat = jnp.concatenate([v.reshape(planes * HY, HZ) for v in value], axis=0)
    fine = lax.broadcasted_iota(jnp.int32, (HZ, NZ), 1)
    half = lax.broadcasted_iota(jnp.int32, (HZ, NZ), 0)
    repeat = (lax.shift_right_logical(fine, 1) == half).astype(F32)
    amount = 3 * planes * HY
    rows[pl.ds(0, amount, stride=2), :] = flat
    rows[pl.ds(1, amount, stride=2), :] = flat
    wide = jnp.dot(rows[...], repeat, precision=HIGHEST, preferred_element_type=F32)
    for c in range(3):
        for p in range(CX + 2):
            at = (c * planes + (p + 1) // 2) * NY
            moved = smooth_ref[c, p] + wide[at : at + NY, :]
            field[c, p] = moved
            if 0 < p <= CX:
                moved_ref[0, c, p - 1] = moved

    sh = Shifts(4, True)

    @pl.loop(1, CX + 1, unroll=UNROLL)
    def _(p):
        planes = [[tiles(field[c, p + o]) for c in range(3)] for o in (-1, 0, 1)]
        factors = [tiles(coef_ref[p + o]) for o in (-1, 0, 1)]
        image = operate(sh, *planes, *factors, tiles(diag_ref[p - 1]))
        mid = planes[1]
        energy[p - 1] = plane(mid[0] * image[0] + mid[1] * image[1] + mid[2] * image[2])

    part = NY // 4
    for q in range(4):

        @pl.when(mine == q)
        def _():
            for ref, owner in ((kept_ref, q), (sent_1_ref, q ^ 1), (sent_2_ref.at[0], q ^ 2), (sent_2_ref.at[1], q ^ 3)):
                ref[...] = energy[:, owner * part : owner * part + part, :]


VMEM = pl.BlockSpec(memory_space=pltpu.VMEM)
HBM = pl.BlockSpec(memory_space=pltpu.HBM)
SMEM = pl.BlockSpec(memory_space=pltpu.SMEM)
PARAMS = pltpu.CompilerParams(vmem_limit_bytes=32 << 20)


def shaped(*shape):
    return jax.ShapeDtypeStruct(shape, F32)


def body(load_force, stiffness, material, face_src, face_count, face_dst):
    slabs = lax.axis_size("space")
    forward = [(i, (i + 1) % slabs) for i in range(slabs)]
    backward = [(target, origin) for origin, target in forward]
    pack_low, pack_high, coarse_coef, own_coef = pl.pallas_call(
        pack_kernel,
        out_shape=(
            shaped(PACK, NY, NZ),
            shaped(PACK, NY, NZ),
            shaped(HX, HY, HZ),
            shaped(CX, NY, NZ),
        ),
        in_specs=[HBM, HBM, HBM],
        out_specs=(VMEM, VMEM, VMEM, VMEM),
        scratch_shapes=[
            pltpu.SMEM((1, NY // BY), jnp.int32),
            pltpu.VMEM((CX, NY, NZ), F32),
            pltpu.VMEM((HX * NY, HZ), F32),
            pltpu.SemaphoreType.DMA((8,)),
        ],
        compiler_params=PARAMS,
        name="pack",
    )(*[
        pltpu.with_memory_space_constraint(x, pltpu.HBM) for x in (material, load_force, stiffness)
    ])
    below = lax.ppermute(pack_high, "space", forward)
    above = lax.ppermute(pack_low, "space", backward)

    rows_kept = slabs + 8
    line, column, where, index = pl.pallas_call(
        plan_kernel,
        out_shape=(
            shaped(slabs, SLOTS),
            shaped(slabs, SLOTS),
            jax.ShapeDtypeStruct((slabs + 1,), jnp.int32),
            jax.ShapeDtypeStruct((rows_kept, SLOTS), jnp.int32),
        ),
        in_specs=[SMEM, VMEM, VMEM],
        out_specs=(VMEM, VMEM, SMEM, VMEM),
        compiler_params=PARAMS,
        name="plan",
    )(face_count, face_src, face_dst)

    smooth, coef, diag, local, picked = pl.pallas_call(
        fine_kernel,
        out_shape=(
            shaped(3, CX + 2, NY, NZ),
            shaped(CX + 2, NY, NZ),
            shaped(CX, NY, NZ),
            shaped(3 * HX * HY, HZ),
            shaped(slabs, 3 * SLOTS),
        ),
        in_specs=[SMEM, SMEM, VMEM, VMEM, VMEM, VMEM, VMEM],
        out_specs=(VMEM, VMEM, VMEM, VMEM, VMEM),
        scratch_shapes=[
            pltpu.VMEM((COEF_PLANES, NY, NZ), F32),
            pltpu.VMEM((FINE_PLANES, NY, NZ), F32),
            pltpu.VMEM((FINE_PLANES, NY, NZ), F32),
            pltpu.VMEM((3, FINE_PLANES, NY, NZ), F32),
            pltpu.VMEM((3, FINE_PLANES, NY, NZ), F32),
            pltpu.VMEM((3, FINE_PLANES, NY, NZ), F32),
            pltpu.VMEM((3 * CX * NY, 2 * NZ), BF16),
            pltpu.VMEM((3 * HX * NY, HZ), F32),
            pltpu.VMEM((3 * CX * NY, NZ), F32),
            pltpu.VMEM((rows_kept, 8, SLOTS), F32),
        ],
        compiler_params=PARAMS,
        name="fine",
    )(face_count, where, load_force, own_coef, below, above, index)

    arrived = lax.all_to_all(picked, "space", split_axis=0, concat_axis=0, tiled=True)

    tail = pl.BlockSpec((1, NY, NZ), lambda i: (PACK - 1, 0, 0))

    def whole(*shape):
        return pl.BlockSpec(shape, lambda i: (0,) * len(shape))

    grid_shape = (3, HX, HY, HZ)
    source, send_low, send_high = pl.pallas_call(
        gather_kernel,
        grid=(1,),
        out_shape=(shaped(*grid_shape), shaped(*grid_shape), shaped(*grid_shape)),
        in_specs=[
            whole(slabs, 3 * SLOTS),
            whole(slabs, SLOTS),
            whole(slabs, SLOTS),
            whole(3 * HX * HY, HZ),
            tail,
            whole(HX, HY, HZ),
            tail,
        ],
        out_specs=(whole(*grid_shape), whole(*grid_shape), whole(*grid_shape)),
        scratch_shapes=[
            pltpu.VMEM((6 * HX * HY, HZ), F32),
        ],
        compiler_params=PARAMS,
        name="reflux",
    )(arrived, line, column, local, below, coarse_coef, above)
    source_below = lax.ppermute(send_high, "space", forward)
    source_above = lax.ppermute(send_low, "space", backward)

    part = (CX, NY // 4, NZ)
    moved, kept, near, far = pl.pallas_call(
        coarse_kernel,
        grid=(1,),
        out_shape=(shaped(1, 3, CX, NY, NZ),) + (shaped(*part),) * 2 + (shaped(2, *part),),
        in_specs=[
            whole(*grid_shape),
            whole(*grid_shape),
            whole(*grid_shape),
            tail,
            whole(HX, HY, HZ),
            tail,
            whole(3, CX + 2, NY, NZ),
            whole(CX + 2, NY, NZ),
            whole(CX, NY, NZ),
        ],
        out_specs=(whole(1, 3, CX, NY, NZ),) + (whole(*part),) * 2 + (whole(2, *part),),
        scratch_shapes=[
            pltpu.VMEM((3 * (HX + 2) * NY, HZ), F32),
            pltpu.VMEM((3, CX + 2, NY, NZ), F32),
            pltpu.VMEM((CX, NY, NZ), F32),
        ],
        compiler_params=PARAMS,
        name="coarse",
    )(source, source_below, source_above, below, coarse_coef, above, smooth, coef, diag)
    got = lax.ppermute(far, "load", [(i, i ^ 2) for i in range(4)])
    last = lax.ppermute(near + got[1], "load", [(i, i ^ 1) for i in range(4)])
    mine = lax.axis_index("load")
    ident = jnp.where(mine < 2, material[0, 0], material[0, 1])
    base = np.array(MODULI, np.float32)
    factors = jnp.asarray((base[None, :] - base[:, None]) / base[:, None])
    scale = jnp.where(ident == 0, factors[0], jnp.where(ident == 1, factors[1], factors[2]))
    total = (kept + got[0]) + last
    sensitivity = scale[:, None, None, None] * total[None]
    return moved, sensitivity


def solution(mesh):
    return jax.shard_map(
        body,
        mesh=mesh,
        in_specs=(
            P("load", None, "space", None, None),
            P("space", None, None),
            P("space", None),
            P("space", None, None),
            P("space", None),
            P("space", None, None),
        ),
        out_specs=(P("load", None, "space", None, None), P(None, "space", "load", None)),
        check_vma=False,
    )
```

```python
import jax
import jax.numpy as jnp
import numpy as np
from jax import lax
from jax.experimental import pallas as pl
from jax.experimental.pallas import tpu as pltpu
from jax.sharding import PartitionSpec as P

CX = 8
NY = 16
NZ = 256
BY = 8
SLOTS = 256
FINE_STEPS = 3
COARSE_STEPS = 4

UPPER_EDGE = 2.1
LOWER_EDGE = 0.15
COUPLING = 0.1
MODULI = (1.0, 0.55, 0.25)

MIDPOINT = (UPPER_EDGE + LOWER_EDGE) / 2.0
HALFWIDTH = (UPPER_EDGE - LOWER_EDGE) / 2.0

HX, HY, HZ = CX // 2, NY // 2, NZ // 2
FINE_PLANES = CX + 6
COEF_PLANES = CX + 6
PACK = 3 * 3 + 3 + 1
BATCH = 32
UNROLL = 4
F32 = jnp.float32
BF16 = jnp.bfloat16
HIGHEST = lax.Precision.HIGHEST


def step_factors(count):
    ratio = MIDPOINT / HALFWIDTH
    rho_old = 1.0 / ratio
    factors = []
    for _ in range(1, count):
        rho_new = 1.0 / (2.0 * ratio - rho_old)
        factors.append((rho_new * rho_old, 2.0 * rho_new / HALFWIDTH))
        rho_old = rho_new
    return factors


def tiles(plane):
    return jnp.stack([plane[:HY, :HZ], plane[:HY, HZ:], plane[HY:, :HZ], plane[HY:, HZ:]])


def plane(quarters):
    return jnp.concatenate(
        [
            jnp.concatenate([quarters[0], quarters[1]], axis=1),
            jnp.concatenate([quarters[2], quarters[3]], axis=1),
        ],
        axis=0,
    )


class Shifts:
    def __init__(self, count, quarters):
        shape = (count, HY, HZ)
        y = lax.broadcasted_iota(jnp.int32, shape, 1)
        z = lax.broadcasted_iota(jnp.int32, shape, 2)
        self.quarters = quarters
        self.first_y, self.last_y = y == 0, y == HY - 1
        self.first_z, self.last_z = z == 0, z == HZ - 1

    def fill(self, turned, order):
        if not self.quarters:
            return 0.0
        zero = jnp.zeros((HY, HZ), F32)
        return jnp.stack([zero if i is None else turned[i] for i in order])

    def up_y(self, x):
        turned = pltpu.roll(x, HY - 1, 1)
        return jnp.where(self.last_y, self.fill(turned, (2, 3, None, None)), turned)

    def down_y(self, x):
        turned = pltpu.roll(x, 1, 1)
        return jnp.where(self.first_y, self.fill(turned, (None, None, 0, 1)), turned)

    def up_z(self, x):
        turned = pltpu.roll(x, HZ - 1, 2)
        return jnp.where(self.last_z, self.fill(turned, (1, None, 3, None)), turned)

    def down_z(self, x):
        turned = pltpu.roll(x, 1, 2)
        return jnp.where(self.first_z, self.fill(turned, (None, 0, None, 2)), turned)

    def spread_y(self, x):
        return x + 0.5 * (self.up_y(x) + self.down_y(x))

    def spread_z(self, x):
        return x + 0.5 * (self.up_z(x) + self.down_z(x))

    def spread(self, x):
        return self.spread_z(self.spread_y(x))


def diagonal(sh, k_below, k_mid, k_above):
    return (3.0 / 7.0) * k_mid + (1.0 / 14.0) * sh.spread(k_mid + 0.5 * (k_below + k_above))


def operate(sh, below, mid, above, k_below, k_mid, k_above, diag):
    centre = diag + (1.0 / 7.0) * k_mid
    slope = [above[c] - below[c] for c in range(3)]
    cross = 0.25 * COUPLING
    plain = [mid[c] + 0.5 * (below[c] + above[c]) for c in range(3)]

    def close_y(x, skew):
        x, skew, own = (1.0 / 28.0) * x, cross * skew, (1.0 / 14.0) * x
        return own + sh.up_y(x + skew) + sh.down_y(x - skew)

    def close_z(x, skew):
        x, skew, own = (1.0 / 28.0) * x, cross * skew, (1.0 / 14.0) * x
        return own + sh.up_z(x + skew) + sh.down_z(x - skew)

    inner = (
        close_z(sh.spread_y(plain[0]), slope[2])
        + cross * (sh.up_y(slope[1]) - sh.down_y(slope[1])),
        close_y(sh.spread_z(plain[1]), slope[0] + (sh.up_z(mid[2]) - sh.down_z(mid[2]))),
        close_z(sh.spread_y(plain[2]), slope[0] + (sh.up_y(mid[1]) - sh.down_y(mid[1]))),
    )
    result = []
    for c in range(3):
        scaled = sh.spread(k_mid * mid[c] + 0.5 * (k_below * below[c] + k_above * above[c]))
        result.append(centre * mid[c] - k_mid * inner[c] - (1.0 / 14.0) * scaled)
    return result


def modulus(material_ref, brick):
    ident = material_ref[0, brick]
    return jnp.where(ident == 0, MODULI[0], jnp.where(ident == 1, MODULI[1], MODULI[2])).astype(F32)


def own_plane(material_ref):
    row = lax.broadcasted_iota(jnp.int32, (NY, NZ), 0)
    return jnp.where(row < BY, modulus(material_ref, 0), modulus(material_ref, 1))


def pair_columns():
    fine = lax.broadcasted_iota(jnp.int32, (NZ, HZ), 0)
    coarse = lax.broadcasted_iota(jnp.int32, (NZ, HZ), 1)
    return (lax.shift_right_logical(fine, 1) == coarse).astype(F32)


def coarse_sum(planes, narrow_ref):
    narrow_ref[...] = jnp.dot(
        planes, pair_columns(), precision=HIGHEST, preferred_element_type=F32
    )
    rows = narrow_ref.shape[0] // 2
    return narrow_ref[pl.ds(0, rows, stride=2), :] + narrow_ref[pl.ds(1, rows, stride=2), :]


def pack_kernel(
    material_hbm, force_hbm, stiff_hbm,
    low_ref, high_ref, coarse_ref, coef_ref,
    material, stiff, sums, sems,
):
    copies = [
        pltpu.make_async_copy(stiff_hbm, stiff, sems.at[0]),
        pltpu.make_async_copy(material_hbm, material, sems.at[1]),
    ]
    for c in range(3):
        rows = pl.ds(3 * c, 3)
        copies += [
            pltpu.make_async_copy(force_hbm.at[0, c, pl.ds(0, 3)], low_ref.at[rows], sems.at[2 + c]),
            pltpu.make_async_copy(
                force_hbm.at[0, c, pl.ds(CX - 3, 3)], high_ref.at[rows], sems.at[5 + c]
            ),
        ]
    for copy in copies:
        copy.start()
    for copy in copies:
        copy.wait()
    own = own_plane(material)
    sh = Shifts(4, True)
    coef = [stiff[p] * own for p in range(CX)]
    for p in range(CX):
        coef_ref[p] = coef[p]
    for p in range(3):
        low_ref[9 + p] = coef[p]
        high_ref[9 + p] = coef[CX - 3 + p]
    for ref, p, slot in ((low_ref, 2, 2), (high_ref, CX - 3, 0)):
        scale = (1.0 / MIDPOINT) / diagonal(sh, *[tiles(coef[p + o]) for o in (-1, 0, 1)])
        scale = plane(scale)
        for c in range(3):
            ref[3 * c + slot] = ref[3 * c + slot] * scale
    pairs = jnp.concatenate([coef[2 * p] + coef[2 * p + 1] for p in range(HX)], axis=0)
    coarse = (0.125 * coarse_sum(pairs, sums)).reshape(HX, HY, HZ)
    coarse_ref[...] = coarse
    for p in range(HX):
        y, z = (p // 2) * HY, (p % 2) * HZ
        low_ref[PACK - 1, y : y + HY, z : z + HZ] = coarse[p]
        high_ref[PACK - 1, y : y + HY, z : z + HZ] = coarse[p]


def plan_kernel(
    count_ref,
    source_ref,
    target_ref,
    force_ref,
    coef_ref,
    line_ref,
    column_ref,
    where_ref,
    index_ref,
    diag_ref,
    first_ref,
    second_ref,
    third_ref,
):
    slabs = count_ref.shape[1]
    lane = lax.broadcasted_iota(jnp.int32, (1, SLOTS), 1)
    cells = target_ref[0]
    line_ref[...] = lax.shift_right_logical(cells, 7).astype(F32)
    column_ref[...] = (cells & (HZ - 1)).astype(F32)

    def place(o, carry):
        at, row = carry
        where_ref[o] = at
        tile = lax.shift_right_logical(at, 8)
        offset = at & (SLOTS - 1)
        turned = pltpu.roll(source_ref[0, pl.ds(o, 1), :], offset, 1)
        row = jnp.where(lane >= offset, turned, row)
        index_ref[pl.ds(tile, 1), :] = row
        index_ref[pl.ds(tile + 1, 1), :] = turned
        after = at + count_ref[0, o]
        crossed = lax.shift_right_logical(after, 8) != tile
        return after, jnp.where(crossed, turned, row)

    start = (jnp.int32(0), jnp.zeros((1, SLOTS), jnp.int32))
    where_ref[slabs] = lax.fori_loop(0, slabs, place, start, unroll=8)[0]

    sh = Shifts(4, True)
    (keep_2, gain_2), (keep_3, gain_3) = step_factors(FINE_STEPS)

    @pl.loop(1, CX - 1, unroll=2)
    def _(p):
        d = diagonal(sh, *[tiles(coef_ref[p + o]) for o in (-1, 0, 1)])
        scale = (1.0 / MIDPOINT) / d
        diag_ref[p] = plane(d)
        for c in range(3):
            first_ref[c, p] = plane(tiles(force_ref[0, c, p]) * scale)

    def advance(src, p):
        planes = [[tiles(src[c, p + o]) for c in range(3)] for o in (-1, 0, 1)]
        factors = [tiles(coef_ref[p + o]) for o in (-1, 0, 1)]
        d = tiles(diag_ref[p])
        image = operate(sh, *planes, *factors, d)
        return planes[1], [(tiles(force_ref[0, c, p]) - image[c]) / d for c in range(3)]

    @pl.loop(2, CX - 2, unroll=2)
    def _(p):
        value, left = advance(first_ref, p)
        for c in range(3):
            second_ref[c, p] = plane((1.0 + keep_2) * value[c] + gain_2 * left[c])

    @pl.loop(3, CX - 3, unroll=2)
    def _(p):
        value, left = advance(second_ref, p)
        for c in range(3):
            step = keep_3 * (value[c] - tiles(first_ref[c, p])) + gain_3 * left[c]
            third_ref[c, p - 3] = plane(value[c] + step)


def unpack_coarse(plane_ref):
    return [
        plane_ref[0, (p // 2) * HY : (p // 2) * HY + HY, (p % 2) * HZ : (p % 2) * HZ + HZ]
        for p in range(HX)
    ]


def fine_kernel(
    count_ref,
    where_ref,
    force_ref,
    own_ref,
    below_ref,
    above_ref,
    index_ref,
    inner_diag_ref,
    inner_first_ref,
    inner_second_ref,
    inner_third_ref,
    smooth_ref,
    coef_out_ref,
    diag_out_ref,
    coarse_ref,
    picked_ref,
    coef,
    diag,
    inverse,
    force,
    first,
    second,
    table,
    sums,
    residual,
    found,
):
    slab = lax.axis_index("space")
    slabs = lax.axis_size("space")
    sh = Shifts(4, True)
    has_below = slab > 0
    has_above = slab < slabs - 1
    for p in range(CX):
        coef[3 + p] = own_ref[p]
    for p in range(3):
        coef[p] = jnp.where(has_below, below_ref[9 + p], 0.0)
        coef[3 + CX + p] = jnp.where(has_above, above_ref[9 + p], 0.0)
    for c in range(3):
        first[c, 0] = jnp.where(has_below, below_ref[3 * c], 0.0)
        first[c, FINE_PLANES - 1] = jnp.where(has_above, above_ref[3 * c + 2], 0.0)
        for p in range(2):
            force[c, 1 + p] = below_ref[3 * c + 1 + p]
            force[c, 3 + CX + p] = above_ref[3 * c + p]
        for p in range(CX):
            force[c, 3 + p] = force_ref[0, c, p]

    for p in range(1, CX - 1):
        diag[p + 3] = inner_diag_ref[p]
        for c in range(3):
            first[c, p + 3] = inner_first_ref[c, p]
    for p in (1, 2, CX - 3, CX - 2):
        inverse[p + 3] = 1.0 / inner_diag_ref[p]
    for c in range(3):
        for p in range(2, CX - 2):
            second[c, p + 3] = inner_second_ref[c, p]
        for p in range(3, CX - 3):
            smooth_ref[c, p + 1] = inner_third_ref[c, p - 3]

    @pl.loop(0, 6, unroll=2)
    def _(i):
        p = 1 + i + jnp.where(i >= 3, CX - 2, 0)
        d = plane(diagonal(sh, *[tiles(coef[p + o]) for o in (-1, 0, 1)]))
        place = slab * CX + p - 3
        valid = jnp.logical_and(place >= 0, place < slabs * CX)
        inv = jnp.where(valid, 1.0 / d, 0.0)
        diag[p] = d
        inverse[p] = inv
        for c in range(3):
            first[c, p] = force[c, p] * inv * (1.0 / MIDPOINT)

    def remainder(src, p, base):
        planes = [[tiles(src[c, p + o - base]) for c in range(3)] for o in (-1, 0, 1)]
        factors = [tiles(coef[p + o]) for o in (-1, 0, 1)]
        image = operate(sh, *planes, *factors, tiles(diag[p]))
        return planes[1], [tiles(force[c, p]) - image[c] for c in range(3)]

    (keep_2, gain_2), (keep_3, gain_3) = step_factors(FINE_STEPS)

    @pl.loop(0, 8, unroll=UNROLL)
    def _(i):
        p = 1 + i + jnp.where(i >= 4, CX - 4, 0)
        value, left = remainder(first, p, 0)
        inv = tiles(inverse[p])
        for c in range(3):
            second[c, p] = plane((1.0 + keep_2) * value[c] + gain_2 * (left[c] * inv))

    @pl.loop(0, 8, unroll=UNROLL)
    def _(i):
        p = 2 + i + jnp.where(i >= 4, CX - 6, 0)
        value, left = remainder(second, p, 0)
        inv = tiles(inverse[p])
        for c in range(3):
            step = keep_3 * (value[c] - tiles(first[c, p])) + gain_3 * (left[c] * inv)
            smooth_ref[c, p - 2] = plane(value[c] + step)

    @pl.loop(3, FINE_PLANES - 3, unroll=UNROLL)
    def _(p):
        _, left = remainder(smooth_ref, p, 2)
        for c in range(3):
            row = pl.multiple_of(c * (CX * NY) + (p - 3) * NY, NY)
            whole = plane(left[c])
            residual[pl.ds(row, NY), :] = whole
            head = whole.astype(BF16)
            table[pl.ds(row, NY), 0:NZ] = head
            table[pl.ds(row, NY), NZ : 2 * NZ] = (whole - head.astype(F32)).astype(BF16)

    for p in range(CX + 2):
        coef_out_ref[p] = coef[p + 2]
    for p in range(CX):
        diag_out_ref[p] = diag[p + 3]

    planes = residual[...].reshape(3 * HX, 2, NY, NZ)
    pairs = (planes[:, 0] + planes[:, 1]).reshape(3 * HX * NY, NZ)
    coarse_ref[...] = 0.5 * coarse_sum(pairs, sums)

    plane_rows = CX * NY
    groups = plane_rows // 8
    column = lax.broadcasted_iota(jnp.int32, (NZ, SLOTS), 0).astype(F32).astype(BF16)
    line = lax.broadcasted_iota(jnp.int32, (8, SLOTS), 0)
    lane = lax.broadcasted_iota(jnp.int32, (8, SLOTS), 1)
    one = jnp.ones((), BF16)
    zero = jnp.zeros((), BF16)

    half_line = lax.broadcasted_iota(jnp.int32, (8, HZ), 0)

    def pick(t):
        index = index_ref[pl.ds(t, 1), :]
        group = lax.shift_right_logical(index, 11)
        inner = line == (lax.shift_right_logical(index, 8) & 7)
        hot = jnp.where(column == (index & (NZ - 1)).astype(F32).astype(BF16), one, zero)
        amount = 2 * plane_rows
        both = jnp.dot(table[0:amount, 0:NZ], hot, preferred_element_type=F32) + jnp.dot(
            table[0:amount, NZ : 2 * NZ], hot, preferred_element_type=F32
        )
        for c in range(2):
            held = both[c * plane_rows : c * plane_rows + 8, :]
            for g in range(1, groups):
                at = c * plane_rows + 8 * g
                held = jnp.where(group == g, both[at : at + 8, :], held)
            found[t, c : c + 1, :] = jnp.sum(jnp.where(inner, held, 0.0), axis=0, keepdims=True)
        for c in range(2, 3):
            halves = []
            for h in range(2):
                part = index[:, h * HZ : (h + 1) * HZ]
                lane_of = jnp.broadcast_to(part & (HZ - 1), (8, HZ))
                right = (part & HZ) != 0
                group_h = group[:, h * HZ : (h + 1) * HZ]
                held = None
                for g in range(groups):
                    at = c * plane_rows + 8 * g
                    rows8 = residual[at : at + 8, :]
                    got = jnp.where(
                        right,
                        jnp.take_along_axis(rows8[:, HZ:], lane_of, axis=1, mode="promise_in_bounds"),
                        jnp.take_along_axis(rows8[:, :HZ], lane_of, axis=1, mode="promise_in_bounds"),
                    )
                    held = got if held is None else jnp.where(group_h == g, got, held)
                halves.append(held)
            held = jnp.concatenate(halves, axis=1)
            found[t, c : c + 1, :] = jnp.sum(jnp.where(inner, held, 0.0), axis=0, keepdims=True)

    @pl.loop(0, lax.shift_right_logical(where_ref[slabs] + 4 * SLOTS - 1, 10))
    def _(quad):
        for u in range(4):
            pick(4 * quad + u)

    @pl.loop(0, slabs, unroll=16)
    def _(o):
        at = where_ref[o]
        tile = lax.shift_right_logical(at, 8)
        offset = at & (SLOTS - 1)
        joined = jnp.where(lane >= offset, found[tile], found[tile + 1])
        turned = pltpu.roll(joined, SLOTS - offset, 1)
        turned = jnp.where(lane < count_ref[0, o], turned, 0.0)
        for c in range(3):
            picked_ref[pl.ds(o, 1), c * SLOTS : (c + 1) * SLOTS] = turned[c : c + 1, :]


def coarse_extent(below_pack_ref, coarse_ref, above_pack_ref, slab, slabs):
    low = [jnp.where(slab > 0, x, 0.0) for x in unpack_coarse(below_pack_ref)]
    high = [jnp.where(slab < slabs - 1, x, 0.0) for x in unpack_coarse(above_pack_ref)]
    return low + [coarse_ref[p] for p in range(HX)] + high


def gather_kernel(
    arrived_ref,
    line_ref,
    column_ref,
    local_ref,
    coef_below_ref,
    coef_ref,
    coef_above_ref,
    source_ref,
    low_ref,
    high_ref,
    total,
):
    slab = lax.axis_index("space")
    slabs = lax.axis_size("space")
    lines = HX * HY
    column = lax.broadcasted_iota(jnp.int32, (HZ, SLOTS), 0).astype(F32).astype(BF16)
    line = lax.broadcasted_iota(jnp.int32, (lines, SLOTS), 0).astype(F32).astype(BF16)
    total[...] = jnp.zeros_like(total)
    one = jnp.ones((), BF16)
    zero = jnp.zeros((), BF16)

    @pl.loop(0, slabs, step=BATCH)
    def _(s):
        hots, lefts = [], []
        for u in range(BATCH):
            hots.append(jnp.where(column == column_ref[pl.ds(s + u, 1), :].astype(BF16), one, zero))
            chosen = line == line_ref[pl.ds(s + u, 1), :].astype(BF16)
            heads, tails = [], []
            for c in range(3):
                value = arrived_ref[pl.ds(s + u, 1), c * SLOTS : (c + 1) * SLOTS]
                head = value.astype(BF16)
                tail = (value - head.astype(F32)).astype(BF16)
                heads.append(jnp.where(chosen, head, zero))
                tails.append(jnp.where(chosen, tail, zero))
            lefts.append(jnp.concatenate(heads + tails, axis=0))
        total[...] += lax.dot_general(
            jnp.concatenate(lefts, axis=1),
            jnp.concatenate(hots, axis=1),
            (((1,), (1,)), ((), ())),
            preferred_element_type=F32,
        )

    count = 3 * lines
    source = (total[0:count, :] + total[count : 2 * count, :] + local_ref[...]).reshape(3, HX, HY, HZ)
    source_ref[...] = source
    low_ref[...] = source
    high_ref[...] = source
    coef = coarse_extent(coef_below_ref, coef_ref, coef_above_ref, slab, slabs)
    sh = Shifts(1, False)
    for ref, p in ((high_ref, 0), (low_ref, HX - 1)):
        d = diagonal(sh, *[coef[HX + p + o][None] for o in (-1, 0, 1)])
        scale = (1.0 / MIDPOINT) / d[0]
        for c in range(3):
            ref[c, p] = source[c, p] * scale


def coarse_kernel(
    source_ref,
    below_ref,
    above_ref,
    coef_below_ref,
    coarse_coef_ref,
    coef_above_ref,
    smooth_ref,
    coef_ref,
    diag_ref,
    moved_ref,
    kept_ref,
    sent_1_ref,
    sent_2_ref,
    rows,
    field,
    energy,
):
    slab = lax.axis_index("space")
    slabs = lax.axis_size("space")
    mine = lax.axis_index("load")
    coef = jnp.stack(coarse_extent(coef_below_ref, coarse_coef_ref, coef_above_ref, slab, slabs))
    source = [
        jnp.concatenate([below_ref[c], source_ref[c], above_ref[c]], axis=0) for c in range(3)
    ]
    count = 3 * HX - 2
    place = lax.broadcasted_iota(jnp.int32, (count, HY, HZ), 0) + (slab * HX - HX + 1)
    valid = jnp.logical_and(place >= 0, place < slabs * HX)
    diag = diagonal(Shifts(count, False), coef[:-2], coef[1:-1], coef[2:])
    inverse = jnp.where(valid, 1.0 / diag, 0.0)
    older = None
    value = []
    for c in range(3):
        low = jnp.where(slab > 0, source[c][:1], 0.0)
        high = jnp.where(slab < slabs - 1, source[c][-1:], 0.0)
        inner = source[c][1:-1] * inverse * (1.0 / MIDPOINT)
        value.append(jnp.concatenate([low, inner, high], axis=0))
    for number, (keep, gain) in enumerate(step_factors(COARSE_STEPS)):
        size = count - 2 * number
        inside = slice(number, number + size)
        window = slice(number + 1, number + 1 + size)
        image = operate(
            Shifts(size, False),
            [v[:-2] for v in value],
            [v[1:-1] for v in value],
            [v[2:] for v in value],
            coef[number : number + size],
            coef[window],
            coef[number + 2 : number + 2 + size],
            diag[inside],
        )
        newer = []
        for c in range(3):
            mid = value[c][1:-1]
            change = mid if older is None else mid - older[c][2:-2]
            left = source[c][window] - image[c]
            newer.append(mid + keep * change + gain * (left * inverse[inside]))
        older, value = value, newer

    planes = HX + 2
    flat = jnp.concatenate([v.reshape(planes * HY, HZ) for v in value], axis=0)
    fine = lax.broadcasted_iota(jnp.int32, (HZ, NZ), 1)
    half = lax.broadcasted_iota(jnp.int32, (HZ, NZ), 0)
    repeat = (lax.shift_right_logical(fine, 1) == half).astype(F32)
    amount = 3 * planes * HY
    rows[pl.ds(0, amount, stride=2), :] = flat
    rows[pl.ds(1, amount, stride=2), :] = flat
    wide = jnp.dot(rows[...], repeat, precision=HIGHEST, preferred_element_type=F32)
    for c in range(3):
        for p in range(CX + 2):
            at = (c * planes + (p + 1) // 2) * NY
            moved = smooth_ref[c, p] + wide[at : at + NY, :]
            field[c, p] = moved
            if 0 < p <= CX:
                moved_ref[0, c, p - 1] = moved

    sh = Shifts(4, True)

    @pl.loop(1, CX + 1, unroll=UNROLL)
    def _(p):
        planes = [[tiles(field[c, p + o]) for c in range(3)] for o in (-1, 0, 1)]
        factors = [tiles(coef_ref[p + o]) for o in (-1, 0, 1)]
        image = operate(sh, *planes, *factors, tiles(diag_ref[p - 1]))
        mid = planes[1]
        energy[p - 1] = plane(mid[0] * image[0] + mid[1] * image[1] + mid[2] * image[2])

    part = NY // 4
    for q in range(4):

        @pl.when(mine == q)
        def _():
            for ref, owner in ((kept_ref, q), (sent_1_ref, q ^ 1), (sent_2_ref.at[0], q ^ 2), (sent_2_ref.at[1], q ^ 3)):
                ref[...] = energy[:, owner * part : owner * part + part, :]


VMEM = pl.BlockSpec(memory_space=pltpu.VMEM)
HBM = pl.BlockSpec(memory_space=pltpu.HBM)
SMEM = pl.BlockSpec(memory_space=pltpu.SMEM)
PARAMS = pltpu.CompilerParams(vmem_limit_bytes=32 << 20)


def shaped(*shape):
    return jax.ShapeDtypeStruct(shape, F32)


def body(load_force, stiffness, material, face_src, face_count, face_dst):
    slabs = lax.axis_size("space")
    forward = [(i, (i + 1) % slabs) for i in range(slabs)]
    backward = [(target, origin) for origin, target in forward]
    pack_low, pack_high, coarse_coef, own_coef = pl.pallas_call(
        pack_kernel,
        out_shape=(
            shaped(PACK, NY, NZ),
            shaped(PACK, NY, NZ),
            shaped(HX, HY, HZ),
            shaped(CX, NY, NZ),
        ),
        in_specs=[HBM, HBM, HBM],
        out_specs=(VMEM, VMEM, VMEM, VMEM),
        scratch_shapes=[
            pltpu.SMEM((1, NY // BY), jnp.int32),
            pltpu.VMEM((CX, NY, NZ), F32),
            pltpu.VMEM((HX * NY, HZ), F32),
            pltpu.SemaphoreType.DMA((8,)),
        ],
        compiler_params=PARAMS,
        name="pack",
    )(*[
        pltpu.with_memory_space_constraint(x, pltpu.HBM) for x in (material, load_force, stiffness)
    ])
    below = lax.ppermute(pack_high, "space", forward)
    above = lax.ppermute(pack_low, "space", backward)

    rows_kept = slabs + 8
    line, column, where, index, *inner = pl.pallas_call(
        plan_kernel,
        out_shape=(
            shaped(slabs, SLOTS),
            shaped(slabs, SLOTS),
            jax.ShapeDtypeStruct((slabs + 1,), jnp.int32),
            jax.ShapeDtypeStruct((rows_kept, SLOTS), jnp.int32),
            shaped(CX, NY, NZ),
            shaped(3, CX, NY, NZ),
            shaped(3, CX, NY, NZ),
            shaped(3, CX - 6, NY, NZ),
        ),
        in_specs=[SMEM, VMEM, VMEM, VMEM, VMEM],
        out_specs=(VMEM, VMEM, SMEM, VMEM, VMEM, VMEM, VMEM, VMEM),
        compiler_params=PARAMS,
        name="plan",
    )(face_count, face_src, face_dst, load_force, own_coef)

    smooth, coef, diag, local, picked = pl.pallas_call(
        fine_kernel,
        out_shape=(
            shaped(3, CX + 2, NY, NZ),
            shaped(CX + 2, NY, NZ),
            shaped(CX, NY, NZ),
            shaped(3 * HX * HY, HZ),
            shaped(slabs, 3 * SLOTS),
        ),
        in_specs=[SMEM, SMEM] + [VMEM] * 9,
        out_specs=(VMEM, VMEM, VMEM, VMEM, VMEM),
        scratch_shapes=[
            pltpu.VMEM((COEF_PLANES, NY, NZ), F32),
            pltpu.VMEM((FINE_PLANES, NY, NZ), F32),
            pltpu.VMEM((FINE_PLANES, NY, NZ), F32),
            pltpu.VMEM((3, FINE_PLANES, NY, NZ), F32),
            pltpu.VMEM((3, FINE_PLANES, NY, NZ), F32),
            pltpu.VMEM((3, FINE_PLANES, NY, NZ), F32),
            pltpu.VMEM((3 * CX * NY, 2 * NZ), BF16),
            pltpu.VMEM((3 * HX * NY, HZ), F32),
            pltpu.VMEM((3 * CX * NY, NZ), F32),
            pltpu.VMEM((rows_kept, 8, SLOTS), F32),
        ],
        compiler_params=PARAMS,
        name="fine",
    )(face_count, where, load_force, own_coef, below, above, index, *inner)

    arrived = lax.all_to_all(picked, "space", split_axis=0, concat_axis=0, tiled=True)

    tail = pl.BlockSpec((1, NY, NZ), lambda i: (PACK - 1, 0, 0))

    def whole(*shape):
        return pl.BlockSpec(shape, lambda i: (0,) * len(shape))

    grid_shape = (3, HX, HY, HZ)
    source, send_low, send_high = pl.pallas_call(
        gather_kernel,
        grid=(1,),
        out_shape=(shaped(*grid_shape), shaped(*grid_shape), shaped(*grid_shape)),
        in_specs=[
            whole(slabs, 3 * SLOTS),
            whole(slabs, SLOTS),
            whole(slabs, SLOTS),
            whole(3 * HX * HY, HZ),
            tail,
            whole(HX, HY, HZ),
            tail,
        ],
        out_specs=(whole(*grid_shape), whole(*grid_shape), whole(*grid_shape)),
        scratch_shapes=[
            pltpu.VMEM((6 * HX * HY, HZ), F32),
        ],
        compiler_params=PARAMS,
        name="reflux",
    )(arrived, line, column, local, below, coarse_coef, above)
    source_below = lax.ppermute(send_high, "space", forward)
    source_above = lax.ppermute(send_low, "space", backward)

    part = (CX, NY // 4, NZ)
    moved, kept, near, far = pl.pallas_call(
        coarse_kernel,
        grid=(1,),
        out_shape=(shaped(1, 3, CX, NY, NZ),) + (shaped(*part),) * 2 + (shaped(2, *part),),
        in_specs=[
            whole(*grid_shape),
            whole(*grid_shape),
            whole(*grid_shape),
            tail,
            whole(HX, HY, HZ),
            tail,
            whole(3, CX + 2, NY, NZ),
            whole(CX + 2, NY, NZ),
            whole(CX, NY, NZ),
        ],
        out_specs=(whole(1, 3, CX, NY, NZ),) + (whole(*part),) * 2 + (whole(2, *part),),
        scratch_shapes=[
            pltpu.VMEM((3 * (HX + 2) * NY, HZ), F32),
            pltpu.VMEM((3, CX + 2, NY, NZ), F32),
            pltpu.VMEM((CX, NY, NZ), F32),
        ],
        compiler_params=PARAMS,
        name="coarse",
    )(source, source_below, source_above, below, coarse_coef, above, smooth, coef, diag)
    got = lax.ppermute(far, "load", [(i, i ^ 2) for i in range(4)])
    last = lax.ppermute(near + got[1], "load", [(i, i ^ 1) for i in range(4)])
    mine = lax.axis_index("load")
    ident = jnp.where(mine < 2, material[0, 0], material[0, 1])
    base = np.array(MODULI, np.float32)
    factors = jnp.asarray((base[None, :] - base[:, None]) / base[:, None])
    scale = jnp.where(ident == 0, factors[0], jnp.where(ident == 1, factors[1], factors[2]))
    total = (kept + got[0]) + last
    sensitivity = scale[:, None, None, None] * total[None]
    return moved, sensitivity


def solution(mesh):
    return jax.shard_map(
        body,
        mesh=mesh,
        in_specs=(
            P("load", None, "space", None, None),
            P("space", None, None),
            P("space", None),
            P("space", None, None),
            P("space", None),
            P("space", None, None),
        ),
        out_specs=(P("load", None, "space", None, None), P(None, "space", "load", None)),
        check_vma=False,
    )
```

```python
import jax
import jax.numpy as jnp
import numpy as np
from jax import lax
from jax.experimental import pallas as pl
from jax.experimental.pallas import tpu as pltpu
from jax.sharding import PartitionSpec as P

CX = 8
NY = 16
NZ = 256
BY = 8
SLOTS = 256
FINE_STEPS = 3
COARSE_STEPS = 4

UPPER_EDGE = 2.1
LOWER_EDGE = 0.15
COUPLING = 0.1
MODULI = (1.0, 0.55, 0.25)

MIDPOINT = (UPPER_EDGE + LOWER_EDGE) / 2.0
HALFWIDTH = (UPPER_EDGE - LOWER_EDGE) / 2.0

HX, HY, HZ = CX // 2, NY // 2, NZ // 2
FINE_PLANES = CX + 6
COEF_PLANES = CX + 6
PACK = 3 * 3 + 3 + 1
BATCH = 32
UNROLL = 4
F32 = jnp.float32
BF16 = jnp.bfloat16
HIGHEST = lax.Precision.HIGHEST


def step_factors(count):
    ratio = MIDPOINT / HALFWIDTH
    rho_old = 1.0 / ratio
    factors = []
    for _ in range(1, count):
        rho_new = 1.0 / (2.0 * ratio - rho_old)
        factors.append((rho_new * rho_old, 2.0 * rho_new / HALFWIDTH))
        rho_old = rho_new
    return factors


def tiles(plane):
    return jnp.stack([plane[:HY, :HZ], plane[:HY, HZ:], plane[HY:, :HZ], plane[HY:, HZ:]])


def plane(quarters):
    return jnp.concatenate(
        [
            jnp.concatenate([quarters[0], quarters[1]], axis=1),
            jnp.concatenate([quarters[2], quarters[3]], axis=1),
        ],
        axis=0,
    )


class Shifts:
    def __init__(self, count, quarters):
        shape = (count, HY, HZ)
        y = lax.broadcasted_iota(jnp.int32, shape, 1)
        z = lax.broadcasted_iota(jnp.int32, shape, 2)
        self.quarters = quarters
        self.first_y, self.last_y = y == 0, y == HY - 1
        self.first_z, self.last_z = z == 0, z == HZ - 1

    def fill(self, turned, order):
        if not self.quarters:
            return 0.0
        zero = jnp.zeros((HY, HZ), F32)
        return jnp.stack([zero if i is None else turned[i] for i in order])

    def up_y(self, x):
        turned = pltpu.roll(x, HY - 1, 1)
        return jnp.where(self.last_y, self.fill(turned, (2, 3, None, None)), turned)

    def down_y(self, x):
        turned = pltpu.roll(x, 1, 1)
        return jnp.where(self.first_y, self.fill(turned, (None, None, 0, 1)), turned)

    def up_z(self, x):
        turned = pltpu.roll(x, HZ - 1, 2)
        return jnp.where(self.last_z, self.fill(turned, (1, None, 3, None)), turned)

    def down_z(self, x):
        turned = pltpu.roll(x, 1, 2)
        return jnp.where(self.first_z, self.fill(turned, (None, 0, None, 2)), turned)

    def spread_y(self, x):
        return x + 0.5 * (self.up_y(x) + self.down_y(x))

    def spread_z(self, x):
        return x + 0.5 * (self.up_z(x) + self.down_z(x))

    def spread(self, x):
        return self.spread_z(self.spread_y(x))


def diagonal(sh, k_below, k_mid, k_above):
    return (3.0 / 7.0) * k_mid + (1.0 / 14.0) * sh.spread(k_mid + 0.5 * (k_below + k_above))


def operate(sh, below, mid, above, k_below, k_mid, k_above, diag):
    centre = diag + (1.0 / 7.0) * k_mid
    slope = [above[c] - below[c] for c in range(3)]
    cross = 0.25 * COUPLING
    plain = [mid[c] + 0.5 * (below[c] + above[c]) for c in range(3)]

    def close_y(x, skew):
        x, skew, own = (1.0 / 28.0) * x, cross * skew, (1.0 / 14.0) * x
        return own + sh.up_y(x + skew) + sh.down_y(x - skew)

    def close_z(x, skew):
        x, skew, own = (1.0 / 28.0) * x, cross * skew, (1.0 / 14.0) * x
        return own + sh.up_z(x + skew) + sh.down_z(x - skew)

    inner = (
        close_z(sh.spread_y(plain[0]), slope[2])
        + cross * (sh.up_y(slope[1]) - sh.down_y(slope[1])),
        close_y(sh.spread_z(plain[1]), slope[0] + (sh.up_z(mid[2]) - sh.down_z(mid[2]))),
        close_z(sh.spread_y(plain[2]), slope[0] + (sh.up_y(mid[1]) - sh.down_y(mid[1]))),
    )
    result = []
    for c in range(3):
        scaled = sh.spread(k_mid * mid[c] + 0.5 * (k_below * below[c] + k_above * above[c]))
        result.append(centre * mid[c] - k_mid * inner[c] - (1.0 / 14.0) * scaled)
    return result


def modulus(material_ref, brick):
    ident = material_ref[0, brick]
    return jnp.where(ident == 0, MODULI[0], jnp.where(ident == 1, MODULI[1], MODULI[2])).astype(F32)


def own_plane(material_ref):
    row = lax.broadcasted_iota(jnp.int32, (NY, NZ), 0)
    return jnp.where(row < BY, modulus(material_ref, 0), modulus(material_ref, 1))


def pair_columns():
    fine = lax.broadcasted_iota(jnp.int32, (NZ, HZ), 0)
    coarse = lax.broadcasted_iota(jnp.int32, (NZ, HZ), 1)
    return (lax.shift_right_logical(fine, 1) == coarse).astype(F32)


def coarse_sum(planes, narrow_ref):
    narrow_ref[...] = jnp.dot(
        planes, pair_columns(), precision=HIGHEST, preferred_element_type=F32
    )
    rows = narrow_ref.shape[0] // 2
    return narrow_ref[pl.ds(0, rows, stride=2), :] + narrow_ref[pl.ds(1, rows, stride=2), :]


def pack_kernel(
    material_hbm, force_hbm, stiff_hbm,
    low_ref, high_ref, coarse_ref, coef_ref,
    material, stiff, sums, sems,
):
    copies = [
        pltpu.make_async_copy(stiff_hbm, stiff, sems.at[0]),
        pltpu.make_async_copy(material_hbm, material, sems.at[1]),
    ]
    for c in range(3):
        rows = pl.ds(3 * c, 3)
        copies += [
            pltpu.make_async_copy(force_hbm.at[0, c, pl.ds(0, 3)], low_ref.at[rows], sems.at[2 + c]),
            pltpu.make_async_copy(
                force_hbm.at[0, c, pl.ds(CX - 3, 3)], high_ref.at[rows], sems.at[5 + c]
            ),
        ]
    for copy in copies:
        copy.start()
    for copy in copies:
        copy.wait()
    own = own_plane(material)
    sh = Shifts(4, True)
    coef = [stiff[p] * own for p in range(CX)]
    for p in range(CX):
        coef_ref[p] = coef[p]
    for p in range(3):
        low_ref[9 + p] = coef[p]
        high_ref[9 + p] = coef[CX - 3 + p]
    for ref, p, slot in ((low_ref, 2, 2), (high_ref, CX - 3, 0)):
        scale = (1.0 / MIDPOINT) / diagonal(sh, *[tiles(coef[p + o]) for o in (-1, 0, 1)])
        scale = plane(scale)
        for c in range(3):
            ref[3 * c + slot] = ref[3 * c + slot] * scale
    pairs = jnp.concatenate([coef[2 * p] + coef[2 * p + 1] for p in range(HX)], axis=0)
    coarse = (0.125 * coarse_sum(pairs, sums)).reshape(HX, HY, HZ)
    coarse_ref[...] = coarse
    for p in range(HX):
        y, z = (p // 2) * HY, (p % 2) * HZ
        low_ref[PACK - 1, y : y + HY, z : z + HZ] = coarse[p]
        high_ref[PACK - 1, y : y + HY, z : z + HZ] = coarse[p]


def plan_kernel(
    count_ref,
    source_ref,
    target_ref,
    force_ref,
    coef_ref,
    line_ref,
    column_ref,
    where_ref,
    index_ref,
    diag_ref,
    first_ref,
    second_ref,
    third_ref,
):
    slabs = count_ref.shape[1]
    lane = lax.broadcasted_iota(jnp.int32, (1, SLOTS), 1)
    cells = target_ref[0]
    line_ref[...] = lax.shift_right_logical(cells, 7).astype(F32)
    column_ref[...] = (cells & (HZ - 1)).astype(F32)

    def place(o, carry):
        at, row = carry
        where_ref[o] = at
        tile = lax.shift_right_logical(at, 8)
        offset = at & (SLOTS - 1)
        turned = pltpu.roll(source_ref[0, pl.ds(o, 1), :], offset, 1)
        row = jnp.where(lane >= offset, turned, row)
        index_ref[pl.ds(tile, 1), :] = row
        index_ref[pl.ds(tile + 1, 1), :] = turned
        after = at + count_ref[0, o]
        crossed = lax.shift_right_logical(after, 8) != tile
        return after, jnp.where(crossed, turned, row)

    start = (jnp.int32(0), jnp.zeros((1, SLOTS), jnp.int32))
    where_ref[slabs] = lax.fori_loop(0, slabs, place, start, unroll=8)[0]

    sh = Shifts(4, True)
    (keep_2, gain_2), (keep_3, gain_3) = step_factors(FINE_STEPS)

    @pl.loop(1, CX - 1, unroll=2)
    def _(p):
        d = diagonal(sh, *[tiles(coef_ref[p + o]) for o in (-1, 0, 1)])
        scale = (1.0 / MIDPOINT) / d
        diag_ref[p] = plane(d)
        for c in range(3):
            first_ref[c, p] = plane(tiles(force_ref[0, c, p]) * scale)

    def advance(src, p):
        planes = [[tiles(src[c, p + o]) for c in range(3)] for o in (-1, 0, 1)]
        factors = [tiles(coef_ref[p + o]) for o in (-1, 0, 1)]
        d = tiles(diag_ref[p])
        image = operate(sh, *planes, *factors, d)
        return planes[1], [(tiles(force_ref[0, c, p]) - image[c]) / d for c in range(3)]

    @pl.loop(2, CX - 2, unroll=2)
    def _(p):
        value, left = advance(first_ref, p)
        for c in range(3):
            second_ref[c, p] = plane((1.0 + keep_2) * value[c] + gain_2 * left[c])

    @pl.loop(3, CX - 3, unroll=2)
    def _(p):
        value, left = advance(second_ref, p)
        for c in range(3):
            step = keep_3 * (value[c] - tiles(first_ref[c, p])) + gain_3 * left[c]
            third_ref[c, p - 3] = plane(value[c] + step)


def unpack_coarse(plane_ref):
    return [
        plane_ref[0, (p // 2) * HY : (p // 2) * HY + HY, (p % 2) * HZ : (p % 2) * HZ + HZ]
        for p in range(HX)
    ]


def fine_kernel(
    count_ref,
    where_ref,
    force_ref,
    own_ref,
    below_ref,
    above_ref,
    index_ref,
    inner_diag_ref,
    inner_first_ref,
    inner_second_ref,
    inner_third_ref,
    smooth_ref,
    coef_out_ref,
    diag_out_ref,
    coarse_ref,
    picked_ref,
    coef,
    diag,
    inverse,
    force,
    first,
    second,
    table,
    sums,
    residual,
    found,
):
    slab = lax.axis_index("space")
    slabs = lax.axis_size("space")
    sh = Shifts(4, True)
    has_below = slab > 0
    has_above = slab < slabs - 1
    for p in range(CX):
        coef[3 + p] = own_ref[p]
    for p in range(3):
        coef[p] = jnp.where(has_below, below_ref[9 + p], 0.0)
        coef[3 + CX + p] = jnp.where(has_above, above_ref[9 + p], 0.0)
    for c in range(3):
        first[c, 0] = jnp.where(has_below, below_ref[3 * c], 0.0)
        first[c, FINE_PLANES - 1] = jnp.where(has_above, above_ref[3 * c + 2], 0.0)
        for p in range(2):
            force[c, 1 + p] = below_ref[3 * c + 1 + p]
            force[c, 3 + CX + p] = above_ref[3 * c + p]
        for p in range(CX):
            force[c, 3 + p] = force_ref[0, c, p]

    for p in range(1, CX - 1):
        diag[p + 3] = inner_diag_ref[p]
        for c in range(3):
            first[c, p + 3] = inner_first_ref[c, p]
    for p in (1, 2, CX - 3, CX - 2):
        inverse[p + 3] = 1.0 / inner_diag_ref[p]
    for c in range(3):
        for p in range(2, CX - 2):
            second[c, p + 3] = inner_second_ref[c, p]
        for p in range(3, CX - 3):
            smooth_ref[c, p + 1] = inner_third_ref[c, p - 3]

    @pl.loop(0, 6, unroll=2)
    def _(i):
        p = 1 + i + jnp.where(i >= 3, CX - 2, 0)
        d = plane(diagonal(sh, *[tiles(coef[p + o]) for o in (-1, 0, 1)]))
        place = slab * CX + p - 3
        valid = jnp.logical_and(place >= 0, place < slabs * CX)
        inv = jnp.where(valid, 1.0 / d, 0.0)
        diag[p] = d
        inverse[p] = inv
        for c in range(3):
            first[c, p] = force[c, p] * inv * (1.0 / MIDPOINT)

    def remainder(src, p, base):
        planes = [[tiles(src[c, p + o - base]) for c in range(3)] for o in (-1, 0, 1)]
        factors = [tiles(coef[p + o]) for o in (-1, 0, 1)]
        image = operate(sh, *planes, *factors, tiles(diag[p]))
        return planes[1], [tiles(force[c, p]) - image[c] for c in range(3)]

    (keep_2, gain_2), (keep_3, gain_3) = step_factors(FINE_STEPS)

    @pl.loop(0, 8, unroll=UNROLL)
    def _(i):
        p = 1 + i + jnp.where(i >= 4, CX - 4, 0)
        value, left = remainder(first, p, 0)
        inv = tiles(inverse[p])
        for c in range(3):
            second[c, p] = plane((1.0 + keep_2) * value[c] + gain_2 * (left[c] * inv))

    @pl.loop(0, 8, unroll=UNROLL)
    def _(i):
        p = 2 + i + jnp.where(i >= 4, CX - 6, 0)
        value, left = remainder(second, p, 0)
        inv = tiles(inverse[p])
        for c in range(3):
            step = keep_3 * (value[c] - tiles(first[c, p])) + gain_3 * (left[c] * inv)
            smooth_ref[c, p - 2] = plane(value[c] + step)

    @pl.loop(3, FINE_PLANES - 3, unroll=UNROLL)
    def _(p):
        _, left = remainder(smooth_ref, p, 2)
        for c in range(3):
            row = pl.multiple_of(c * (CX * NY) + (p - 3) * NY, NY)
            whole = plane(left[c])
            residual[pl.ds(row, NY), :] = whole
            head = whole.astype(BF16)
            table[pl.ds(row, NY), 0:NZ] = head
            table[pl.ds(row, NY), NZ : 2 * NZ] = (whole - head.astype(F32)).astype(BF16)

    for p in range(CX + 2):
        coef_out_ref[p] = coef[p + 2]
    for p in range(CX):
        diag_out_ref[p] = diag[p + 3]

    planes = residual[...].reshape(3 * HX, 2, NY, NZ)
    pairs = (planes[:, 0] + planes[:, 1]).reshape(3 * HX * NY, NZ)
    coarse_ref[...] = 0.5 * coarse_sum(pairs, sums)

    plane_rows = CX * NY
    groups = plane_rows // 8
    column = lax.broadcasted_iota(jnp.int32, (NZ, SLOTS), 0).astype(F32).astype(BF16)
    line = lax.broadcasted_iota(jnp.int32, (8, SLOTS), 0)
    lane = lax.broadcasted_iota(jnp.int32, (8, SLOTS), 1)
    one = jnp.ones((), BF16)
    zero = jnp.zeros((), BF16)

    half_line = lax.broadcasted_iota(jnp.int32, (8, HZ), 0)

    def pick(t):
        index = index_ref[pl.ds(t, 1), :]
        group = lax.shift_right_logical(index, 11)
        inner = line == (lax.shift_right_logical(index, 8) & 7)
        hot = jnp.where(column == (index & (NZ - 1)).astype(F32).astype(BF16), one, zero)
        amount = 2 * plane_rows
        both = jnp.dot(table[0:amount, 0:NZ], hot, preferred_element_type=F32) + jnp.dot(
            table[0:amount, NZ : 2 * NZ], hot, preferred_element_type=F32
        )
        for c in range(2):
            held = both[c * plane_rows : c * plane_rows + 8, :]
            for g in range(1, groups):
                at = c * plane_rows + 8 * g
                held = jnp.where(group == g, both[at : at + 8, :], held)
            found[t, c : c + 1, :] = jnp.sum(jnp.where(inner, held, 0.0), axis=0, keepdims=True)
        for c in range(2, 3):
            halves = []
            for h in range(2):
                part = index[:, h * HZ : (h + 1) * HZ]
                lane_of = jnp.broadcast_to(part & (HZ - 1), (8, HZ))
                right = (part & HZ) != 0
                group_h = group[:, h * HZ : (h + 1) * HZ]
                held = None
                for g in range(groups):
                    at = c * plane_rows + 8 * g
                    rows8 = residual[at : at + 8, :]
                    got = jnp.where(
                        right,
                        jnp.take_along_axis(rows8[:, HZ:], lane_of, axis=1, mode="promise_in_bounds"),
                        jnp.take_along_axis(rows8[:, :HZ], lane_of, axis=1, mode="promise_in_bounds"),
                    )
                    held = got if held is None else jnp.where(group_h == g, got, held)
                halves.append(held)
            held = jnp.concatenate(halves, axis=1)
            found[t, c : c + 1, :] = jnp.sum(jnp.where(inner, held, 0.0), axis=0, keepdims=True)

    @pl.loop(0, lax.div(where_ref[slabs] + (6 * SLOTS - 1), jnp.int32(6 * SLOTS)))
    def _(trip):
        for u in range(6):
            pick(6 * trip + u)

    @pl.loop(0, slabs, unroll=16)
    def _(o):
        at = where_ref[o]
        tile = lax.shift_right_logical(at, 8)
        offset = at & (SLOTS - 1)
        joined = jnp.where(lane >= offset, found[tile], found[tile + 1])
        turned = pltpu.roll(joined, SLOTS - offset, 1)
        turned = jnp.where(lane < count_ref[0, o], turned, 0.0)
        for c in range(3):
            picked_ref[pl.ds(o, 1), c * SLOTS : (c + 1) * SLOTS] = turned[c : c + 1, :]


def coarse_extent(below_pack_ref, coarse_ref, above_pack_ref, slab, slabs):
    low = [jnp.where(slab > 0, x, 0.0) for x in unpack_coarse(below_pack_ref)]
    high = [jnp.where(slab < slabs - 1, x, 0.0) for x in unpack_coarse(above_pack_ref)]
    return low + [coarse_ref[p] for p in range(HX)] + high


def gather_kernel(
    arrived_ref,
    line_ref,
    column_ref,
    local_ref,
    coef_below_ref,
    coef_ref,
    coef_above_ref,
    source_ref,
    first_ref,
    second_ref,
    total,
):
    slab = lax.axis_index("space")
    slabs = lax.axis_size("space")
    lines = HX * HY
    column = lax.broadcasted_iota(jnp.int32, (HZ, SLOTS), 0).astype(F32).astype(BF16)
    line = lax.broadcasted_iota(jnp.int32, (lines, SLOTS), 0).astype(F32).astype(BF16)
    total[...] = jnp.zeros_like(total)
    one = jnp.ones((), BF16)
    zero = jnp.zeros((), BF16)

    @pl.loop(0, slabs, step=BATCH)
    def _(s):
        hots, lefts = [], []
        for u in range(BATCH):
            hots.append(jnp.where(column == column_ref[pl.ds(s + u, 1), :].astype(BF16), one, zero))
            chosen = line == line_ref[pl.ds(s + u, 1), :].astype(BF16)
            heads, tails = [], []
            for c in range(3):
                value = arrived_ref[pl.ds(s + u, 1), c * SLOTS : (c + 1) * SLOTS]
                head = value.astype(BF16)
                tail = (value - head.astype(F32)).astype(BF16)
                heads.append(jnp.where(chosen, head, zero))
                tails.append(jnp.where(chosen, tail, zero))
            lefts.append(jnp.concatenate(heads + tails, axis=0))
        total[...] += lax.dot_general(
            jnp.concatenate(lefts, axis=1),
            jnp.concatenate(hots, axis=1),
            (((1,), (1,)), ((), ())),
            preferred_element_type=F32,
        )

    count = 3 * lines
    source = (total[0:count, :] + total[count : 2 * count, :] + local_ref[...]).reshape(3, HX, HY, HZ)
    source_ref[...] = source
    first_ref[...] = source
    second_ref[...] = source
    coef = coarse_extent(coef_below_ref, coef_ref, coef_above_ref, slab, slabs)
    sh = Shifts(1, False)
    even = (slab & 1) == 0
    for p, upward in ((0, True), (HX - 1, False)):
        d = diagonal(sh, *[coef[HX + p + o][None] for o in (-1, 0, 1)])
        scale = (1.0 / MIDPOINT) / d[0]
        to_first = even if upward else jnp.logical_not(even)
        for c in range(3):
            plain, scaled = source[c, p], source[c, p] * scale
            first_ref[c, p] = jnp.where(to_first, scaled, plain)
            second_ref[c, p] = jnp.where(to_first, plain, scaled)


def coarse_kernel(
    source_ref,
    first_ref,
    second_ref,
    coef_below_ref,
    coarse_coef_ref,
    coef_above_ref,
    smooth_ref,
    coef_ref,
    diag_ref,
    moved_ref,
    kept_ref,
    sent_1_ref,
    sent_2_ref,
    rows,
    field,
    energy,
):
    slab = lax.axis_index("space")
    slabs = lax.axis_size("space")
    mine = lax.axis_index("load")
    coef = jnp.stack(coarse_extent(coef_below_ref, coarse_coef_ref, coef_above_ref, slab, slabs))
    even = (slab & 1) == 0
    source = []
    for c in range(3):
        below = jnp.where(even, second_ref[c], first_ref[c])
        above = jnp.where(even, first_ref[c], second_ref[c])
        source.append(jnp.concatenate([below, source_ref[c], above], axis=0))
    count = 3 * HX - 2
    place = lax.broadcasted_iota(jnp.int32, (count, HY, HZ), 0) + (slab * HX - HX + 1)
    valid = jnp.logical_and(place >= 0, place < slabs * HX)
    diag = diagonal(Shifts(count, False), coef[:-2], coef[1:-1], coef[2:])
    inverse = jnp.where(valid, 1.0 / diag, 0.0)
    older = None
    value = []
    for c in range(3):
        low = jnp.where(slab > 0, source[c][:1], 0.0)
        high = jnp.where(slab < slabs - 1, source[c][-1:], 0.0)
        inner = source[c][1:-1] * inverse * (1.0 / MIDPOINT)
        value.append(jnp.concatenate([low, inner, high], axis=0))
    for number, (keep, gain) in enumerate(step_factors(COARSE_STEPS)):
        size = count - 2 * number
        inside = slice(number, number + size)
        window = slice(number + 1, number + 1 + size)
        image = operate(
            Shifts(size, False),
            [v[:-2] for v in value],
            [v[1:-1] for v in value],
            [v[2:] for v in value],
            coef[number : number + size],
            coef[window],
            coef[number + 2 : number + 2 + size],
            diag[inside],
        )
        newer = []
        for c in range(3):
            mid = value[c][1:-1]
            change = mid if older is None else mid - older[c][2:-2]
            left = source[c][window] - image[c]
            newer.append(mid + keep * change + gain * (left * inverse[inside]))
        older, value = value, newer

    planes = HX + 2
    flat = jnp.concatenate([v.reshape(planes * HY, HZ) for v in value], axis=0)
    fine = lax.broadcasted_iota(jnp.int32, (HZ, NZ), 1)
    half = lax.broadcasted_iota(jnp.int32, (HZ, NZ), 0)
    repeat = (lax.shift_right_logical(fine, 1) == half).astype(F32)
    amount = 3 * planes * HY
    rows[pl.ds(0, amount, stride=2), :] = flat
    rows[pl.ds(1, amount, stride=2), :] = flat
    wide = jnp.dot(rows[...], repeat, precision=HIGHEST, preferred_element_type=F32)
    for c in range(3):
        for p in range(CX + 2):
            at = (c * planes + (p + 1) // 2) * NY
            moved = smooth_ref[c, p] + wide[at : at + NY, :]
            field[c, p] = moved
            if 0 < p <= CX:
                moved_ref[0, c, p - 1] = moved

    sh = Shifts(4, True)

    @pl.loop(1, CX + 1, unroll=UNROLL)
    def _(p):
        planes = [[tiles(field[c, p + o]) for c in range(3)] for o in (-1, 0, 1)]
        factors = [tiles(coef_ref[p + o]) for o in (-1, 0, 1)]
        image = operate(sh, *planes, *factors, tiles(diag_ref[p - 1]))
        mid = planes[1]
        energy[p - 1] = plane(mid[0] * image[0] + mid[1] * image[1] + mid[2] * image[2])

    part = NY // 4
    for q in range(4):

        @pl.when(mine == q)
        def _():
            for ref, owner in ((kept_ref, q), (sent_1_ref, q ^ 1), (sent_2_ref.at[0], q ^ 2), (sent_2_ref.at[1], q ^ 3)):
                ref[...] = energy[:, owner * part : owner * part + part, :]


VMEM = pl.BlockSpec(memory_space=pltpu.VMEM)
HBM = pl.BlockSpec(memory_space=pltpu.HBM)
SMEM = pl.BlockSpec(memory_space=pltpu.SMEM)
PARAMS = pltpu.CompilerParams(vmem_limit_bytes=32 << 20)


def shaped(*shape):
    return jax.ShapeDtypeStruct(shape, F32)


def body(load_force, stiffness, material, face_src, face_count, face_dst):
    slabs = lax.axis_size("space")
    forward = [(i, (i + 1) % slabs) for i in range(slabs)]
    backward = [(target, origin) for origin, target in forward]
    first_pairs = [(i, i ^ 1) for i in range(slabs)]
    second_pairs = [(i, min(max(((i + 1) ^ 1) - 1, 0), slabs - 1)) for i in range(slabs)]
    pack_low, pack_high, coarse_coef, own_coef = pl.pallas_call(
        pack_kernel,
        out_shape=(
            shaped(PACK, NY, NZ),
            shaped(PACK, NY, NZ),
            shaped(HX, HY, HZ),
            shaped(CX, NY, NZ),
        ),
        in_specs=[HBM, HBM, HBM],
        out_specs=(VMEM, VMEM, VMEM, VMEM),
        scratch_shapes=[
            pltpu.SMEM((1, NY // BY), jnp.int32),
            pltpu.VMEM((CX, NY, NZ), F32),
            pltpu.VMEM((HX * NY, HZ), F32),
            pltpu.SemaphoreType.DMA((8,)),
        ],
        compiler_params=PARAMS,
        name="pack",
    )(*[
        pltpu.with_memory_space_constraint(x, pltpu.HBM) for x in (material, load_force, stiffness)
    ])
    below = lax.ppermute(pack_high, "space", forward)
    above = lax.ppermute(pack_low, "space", backward)

    rows_kept = slabs + 8
    line, column, where, index, *inner = pl.pallas_call(
        plan_kernel,
        out_shape=(
            shaped(slabs, SLOTS),
            shaped(slabs, SLOTS),
            jax.ShapeDtypeStruct((slabs + 1,), jnp.int32),
            jax.ShapeDtypeStruct((rows_kept, SLOTS), jnp.int32),
            shaped(CX, NY, NZ),
            shaped(3, CX, NY, NZ),
            shaped(3, CX, NY, NZ),
            shaped(3, CX - 6, NY, NZ),
        ),
        in_specs=[SMEM, VMEM, VMEM, VMEM, VMEM],
        out_specs=(VMEM, VMEM, SMEM, VMEM, VMEM, VMEM, VMEM, VMEM),
        compiler_params=PARAMS,
        name="plan",
    )(face_count, face_src, face_dst, load_force, own_coef)

    smooth, coef, diag, local, picked = pl.pallas_call(
        fine_kernel,
        out_shape=(
            shaped(3, CX + 2, NY, NZ),
            shaped(CX + 2, NY, NZ),
            shaped(CX, NY, NZ),
            shaped(3 * HX * HY, HZ),
            shaped(slabs, 3 * SLOTS),
        ),
        in_specs=[SMEM, SMEM] + [VMEM] * 9,
        out_specs=(VMEM, VMEM, VMEM, VMEM, VMEM),
        scratch_shapes=[
            pltpu.VMEM((COEF_PLANES, NY, NZ), F32),
            pltpu.VMEM((FINE_PLANES, NY, NZ), F32),
            pltpu.VMEM((FINE_PLANES, NY, NZ), F32),
            pltpu.VMEM((3, FINE_PLANES, NY, NZ), F32),
            pltpu.VMEM((3, FINE_PLANES, NY, NZ), F32),
            pltpu.VMEM((3, FINE_PLANES, NY, NZ), F32),
            pltpu.VMEM((3 * CX * NY, 2 * NZ), BF16),
            pltpu.VMEM((3 * HX * NY, HZ), F32),
            pltpu.VMEM((3 * CX * NY, NZ), F32),
            pltpu.VMEM((rows_kept, 8, SLOTS), F32),
        ],
        compiler_params=PARAMS,
        name="fine",
    )(face_count, where, load_force, own_coef, below, above, index, *inner)

    arrived = lax.all_to_all(picked, "space", split_axis=0, concat_axis=0, tiled=True)

    tail = pl.BlockSpec((1, NY, NZ), lambda i: (PACK - 1, 0, 0))

    def whole(*shape):
        return pl.BlockSpec(shape, lambda i: (0,) * len(shape))

    grid_shape = (3, HX, HY, HZ)
    source, send_first, send_second = pl.pallas_call(
        gather_kernel,
        grid=(1,),
        out_shape=(shaped(*grid_shape), shaped(*grid_shape), shaped(*grid_shape)),
        in_specs=[
            whole(slabs, 3 * SLOTS),
            whole(slabs, SLOTS),
            whole(slabs, SLOTS),
            whole(3 * HX * HY, HZ),
            tail,
            whole(HX, HY, HZ),
            tail,
        ],
        out_specs=(whole(*grid_shape), whole(*grid_shape), whole(*grid_shape)),
        scratch_shapes=[
            pltpu.VMEM((6 * HX * HY, HZ), F32),
        ],
        compiler_params=PARAMS,
        name="reflux",
    )(arrived, line, column, local, below, coarse_coef, above)
    met_second = lax.ppermute(send_second, "space", second_pairs)
    met_first = lax.ppermute(send_first, "space", first_pairs)

    part = (CX, NY // 4, NZ)
    moved, kept, near, far = pl.pallas_call(
        coarse_kernel,
        grid=(1,),
        out_shape=(shaped(1, 3, CX, NY, NZ),) + (shaped(*part),) * 2 + (shaped(2, *part),),
        in_specs=[
            whole(*grid_shape),
            whole(*grid_shape),
            whole(*grid_shape),
            tail,
            whole(HX, HY, HZ),
            tail,
            whole(3, CX + 2, NY, NZ),
            whole(CX + 2, NY, NZ),
            whole(CX, NY, NZ),
        ],
        out_specs=(whole(1, 3, CX, NY, NZ),) + (whole(*part),) * 2 + (whole(2, *part),),
        scratch_shapes=[
            pltpu.VMEM((3 * (HX + 2) * NY, HZ), F32),
            pltpu.VMEM((3, CX + 2, NY, NZ), F32),
            pltpu.VMEM((CX, NY, NZ), F32),
        ],
        compiler_params=PARAMS,
        name="coarse",
    )(source, met_first, met_second, below, coarse_coef, above, smooth, coef, diag)
    got = lax.ppermute(far, "load", [(i, i ^ 2) for i in range(4)])
    last = lax.ppermute(near + got[1], "load", [(i, i ^ 1) for i in range(4)])
    mine = lax.axis_index("load")
    ident = jnp.where(mine < 2, material[0, 0], material[0, 1])
    base = np.array(MODULI, np.float32)
    factors = jnp.asarray((base[None, :] - base[:, None]) / base[:, None])
    scale = jnp.where(ident == 0, factors[0], jnp.where(ident == 1, factors[1], factors[2]))
    total = (kept + got[0]) + last
    sensitivity = scale[:, None, None, None] * total[None]
    return moved, sensitivity


def solution(mesh):
    return jax.shard_map(
        body,
        mesh=mesh,
        in_specs=(
            P("load", None, "space", None, None),
            P("space", None, None),
            P("space", None),
            P("space", None, None),
            P("space", None),
            P("space", None, None),
        ),
        out_specs=(P("load", None, "space", None, None), P(None, "space", "load", None)),
        check_vma=False,
    )
```

```python
import jax
import jax.numpy as jnp
import numpy as np
from jax import lax
from jax.experimental import pallas as pl
from jax.experimental.pallas import tpu as pltpu
from jax.sharding import PartitionSpec as P

CX = 8
NY = 16
NZ = 256
BY = 8
SLOTS = 256
FINE_STEPS = 3
COARSE_STEPS = 4

UPPER_EDGE = 2.1
LOWER_EDGE = 0.15
COUPLING = 0.1
MODULI = (1.0, 0.55, 0.25)

MIDPOINT = (UPPER_EDGE + LOWER_EDGE) / 2.0
HALFWIDTH = (UPPER_EDGE - LOWER_EDGE) / 2.0

HX, HY, HZ = CX // 2, NY // 2, NZ // 2
FINE_PLANES = CX + 6
COEF_PLANES = CX + 6
PACK = 3 * 3 + 3 + 1
BATCH = 64
UNROLL = 4
F32 = jnp.float32
BF16 = jnp.bfloat16
HIGHEST = lax.Precision.HIGHEST


def step_factors(count):
    ratio = MIDPOINT / HALFWIDTH
    rho_old = 1.0 / ratio
    factors = []
    for _ in range(1, count):
        rho_new = 1.0 / (2.0 * ratio - rho_old)
        factors.append((rho_new * rho_old, 2.0 * rho_new / HALFWIDTH))
        rho_old = rho_new
    return factors


def tiles(plane):
    return jnp.stack([plane[:HY, :HZ], plane[:HY, HZ:], plane[HY:, :HZ], plane[HY:, HZ:]])


def plane(quarters):
    return jnp.concatenate(
        [
            jnp.concatenate([quarters[0], quarters[1]], axis=1),
            jnp.concatenate([quarters[2], quarters[3]], axis=1),
        ],
        axis=0,
    )


class Shifts:
    def __init__(self, count, quarters):
        shape = (count, HY, HZ)
        y = lax.broadcasted_iota(jnp.int32, shape, 1)
        z = lax.broadcasted_iota(jnp.int32, shape, 2)
        self.quarters = quarters
        self.first_y, self.last_y = y == 0, y == HY - 1
        self.first_z, self.last_z = z == 0, z == HZ - 1

    def fill(self, turned, order):
        if not self.quarters:
            return 0.0
        zero = jnp.zeros((HY, HZ), F32)
        return jnp.stack([zero if i is None else turned[i] for i in order])

    def up_y(self, x):
        turned = pltpu.roll(x, HY - 1, 1)
        return jnp.where(self.last_y, self.fill(turned, (2, 3, None, None)), turned)

    def down_y(self, x):
        turned = pltpu.roll(x, 1, 1)
        return jnp.where(self.first_y, self.fill(turned, (None, None, 0, 1)), turned)

    def up_z(self, x):
        turned = pltpu.roll(x, HZ - 1, 2)
        return jnp.where(self.last_z, self.fill(turned, (1, None, 3, None)), turned)

    def down_z(self, x):
        turned = pltpu.roll(x, 1, 2)
        return jnp.where(self.first_z, self.fill(turned, (None, 0, None, 2)), turned)

    def spread_y(self, x):
        return x + 0.5 * (self.up_y(x) + self.down_y(x))

    def spread_z(self, x):
        return x + 0.5 * (self.up_z(x) + self.down_z(x))

    def spread(self, x):
        return self.spread_z(self.spread_y(x))


def diagonal(sh, k_below, k_mid, k_above):
    return (3.0 / 7.0) * k_mid + (1.0 / 14.0) * sh.spread(k_mid + 0.5 * (k_below + k_above))


def operate(sh, below, mid, above, k_below, k_mid, k_above, diag):
    centre = diag + (1.0 / 7.0) * k_mid
    slope = [above[c] - below[c] for c in range(3)]
    cross = 0.25 * COUPLING
    plain = [mid[c] + 0.5 * (below[c] + above[c]) for c in range(3)]

    def close_y(x, skew):
        x, skew, own = (1.0 / 28.0) * x, cross * skew, (1.0 / 14.0) * x
        return own + sh.up_y(x + skew) + sh.down_y(x - skew)

    def close_z(x, skew):
        x, skew, own = (1.0 / 28.0) * x, cross * skew, (1.0 / 14.0) * x
        return own + sh.up_z(x + skew) + sh.down_z(x - skew)

    inner = (
        close_z(sh.spread_y(plain[0]), slope[2])
        + cross * (sh.up_y(slope[1]) - sh.down_y(slope[1])),
        close_y(sh.spread_z(plain[1]), slope[0] + (sh.up_z(mid[2]) - sh.down_z(mid[2]))),
        close_z(sh.spread_y(plain[2]), slope[0] + (sh.up_y(mid[1]) - sh.down_y(mid[1]))),
    )
    result = []
    for c in range(3):
        scaled = sh.spread(k_mid * mid[c] + 0.5 * (k_below * below[c] + k_above * above[c]))
        result.append(centre * mid[c] - k_mid * inner[c] - (1.0 / 14.0) * scaled)
    return result


def modulus(material_ref, brick):
    ident = material_ref[0, brick]
    return jnp.where(ident == 0, MODULI[0], jnp.where(ident == 1, MODULI[1], MODULI[2])).astype(F32)


def own_plane(material_ref):
    row = lax.broadcasted_iota(jnp.int32, (NY, NZ), 0)
    return jnp.where(row < BY, modulus(material_ref, 0), modulus(material_ref, 1))


def pair_columns():
    fine = lax.broadcasted_iota(jnp.int32, (NZ, HZ), 0)
    coarse = lax.broadcasted_iota(jnp.int32, (NZ, HZ), 1)
    return (lax.shift_right_logical(fine, 1) == coarse).astype(F32)


def coarse_sum(planes, narrow_ref):
    narrow_ref[...] = jnp.dot(
        planes, pair_columns(), precision=HIGHEST, preferred_element_type=F32
    )
    rows = narrow_ref.shape[0] // 2
    return narrow_ref[pl.ds(0, rows, stride=2), :] + narrow_ref[pl.ds(1, rows, stride=2), :]


def pack_kernel(
    material_hbm, force_hbm, stiff_hbm,
    low_ref, high_ref, coarse_ref, coef_ref,
    material, stiff, sums, sems,
):
    copies = [
        pltpu.make_async_copy(stiff_hbm, stiff, sems.at[0]),
        pltpu.make_async_copy(material_hbm, material, sems.at[1]),
    ]
    for c in range(3):
        rows = pl.ds(3 * c, 3)
        copies += [
            pltpu.make_async_copy(force_hbm.at[0, c, pl.ds(0, 3)], low_ref.at[rows], sems.at[2 + c]),
            pltpu.make_async_copy(
                force_hbm.at[0, c, pl.ds(CX - 3, 3)], high_ref.at[rows], sems.at[5 + c]
            ),
        ]
    for copy in copies:
        copy.start()
    for copy in copies:
        copy.wait()
    own = own_plane(material)
    sh = Shifts(4, True)
    coef = [stiff[p] * own for p in range(CX)]
    for p in range(CX):
        coef_ref[p] = coef[p]
    for p in range(3):
        low_ref[9 + p] = coef[p]
        high_ref[9 + p] = coef[CX - 3 + p]
    for ref, p, slot in ((low_ref, 2, 2), (high_ref, CX - 3, 0)):
        scale = (1.0 / MIDPOINT) / diagonal(sh, *[tiles(coef[p + o]) for o in (-1, 0, 1)])
        scale = plane(scale)
        for c in range(3):
            ref[3 * c + slot] = ref[3 * c + slot] * scale
    pairs = jnp.concatenate([coef[2 * p] + coef[2 * p + 1] for p in range(HX)], axis=0)
    coarse = (0.125 * coarse_sum(pairs, sums)).reshape(HX, HY, HZ)
    coarse_ref[...] = coarse
    for p in range(HX):
        y, z = (p // 2) * HY, (p % 2) * HZ
        low_ref[PACK - 1, y : y + HY, z : z + HZ] = coarse[p]
        high_ref[PACK - 1, y : y + HY, z : z + HZ] = coarse[p]


def plan_kernel(
    count_ref,
    source_ref,
    target_ref,
    force_ref,
    coef_ref,
    line_ref,
    column_ref,
    where_ref,
    index_ref,
    diag_ref,
    first_ref,
    second_ref,
    third_ref,
):
    slabs = count_ref.shape[1]
    lane = lax.broadcasted_iota(jnp.int32, (1, SLOTS), 1)
    cells = target_ref[0]
    line_ref[...] = lax.shift_right_logical(cells, 7).astype(F32)
    column_ref[...] = (cells & (HZ - 1)).astype(F32)

    def place(o, carry):
        at, row = carry
        where_ref[o] = at
        tile = lax.shift_right_logical(at, 8)
        offset = at & (SLOTS - 1)
        turned = pltpu.roll(source_ref[0, pl.ds(o, 1), :], offset, 1)
        row = jnp.where(lane >= offset, turned, row)
        index_ref[pl.ds(tile, 1), :] = row
        index_ref[pl.ds(tile + 1, 1), :] = turned
        after = at + count_ref[0, o]
        crossed = lax.shift_right_logical(after, 8) != tile
        return after, jnp.where(crossed, turned, row)

    start = (jnp.int32(0), jnp.zeros((1, SLOTS), jnp.int32))
    where_ref[slabs] = lax.fori_loop(0, slabs, place, start, unroll=8)[0]

    sh = Shifts(4, True)
    (keep_2, gain_2), (keep_3, gain_3) = step_factors(FINE_STEPS)

    @pl.loop(1, CX - 1, unroll=2)
    def _(p):
        d = diagonal(sh, *[tiles(coef_ref[p + o]) for o in (-1, 0, 1)])
        scale = (1.0 / MIDPOINT) / d
        diag_ref[p] = plane(d)
        for c in range(3):
            first_ref[c, p] = plane(tiles(force_ref[0, c, p]) * scale)

    def advance(src, p):
        planes = [[tiles(src[c, p + o]) for c in range(3)] for o in (-1, 0, 1)]
        factors = [tiles(coef_ref[p + o]) for o in (-1, 0, 1)]
        d = tiles(diag_ref[p])
        image = operate(sh, *planes, *factors, d)
        return planes[1], [(tiles(force_ref[0, c, p]) - image[c]) / d for c in range(3)]

    @pl.loop(2, CX - 2, unroll=2)
    def _(p):
        value, left = advance(first_ref, p)
        for c in range(3):
            second_ref[c, p] = plane((1.0 + keep_2) * value[c] + gain_2 * left[c])

    @pl.loop(3, CX - 3, unroll=2)
    def _(p):
        value, left = advance(second_ref, p)
        for c in range(3):
            step = keep_3 * (value[c] - tiles(first_ref[c, p])) + gain_3 * left[c]
            third_ref[c, p - 3] = plane(value[c] + step)


def unpack_coarse(plane_ref):
    return [
        plane_ref[0, (p // 2) * HY : (p // 2) * HY + HY, (p % 2) * HZ : (p % 2) * HZ + HZ]
        for p in range(HX)
    ]


def fine_kernel(
    count_ref,
    where_ref,
    force_ref,
    own_ref,
    below_ref,
    above_ref,
    index_ref,
    inner_diag_ref,
    inner_first_ref,
    inner_second_ref,
    inner_third_ref,
    smooth_ref,
    coef_out_ref,
    diag_out_ref,
    coarse_ref,
    picked_ref,
    coef,
    diag,
    inverse,
    force,
    first,
    second,
    table,
    sums,
    residual,
    found,
):
    slab = lax.axis_index("space")
    slabs = lax.axis_size("space")
    sh = Shifts(4, True)
    has_below = slab > 0
    has_above = slab < slabs - 1
    for p in range(CX):
        coef[3 + p] = own_ref[p]
    for p in range(3):
        coef[p] = jnp.where(has_below, below_ref[9 + p], 0.0)
        coef[3 + CX + p] = jnp.where(has_above, above_ref[9 + p], 0.0)
    for c in range(3):
        first[c, 0] = jnp.where(has_below, below_ref[3 * c], 0.0)
        first[c, FINE_PLANES - 1] = jnp.where(has_above, above_ref[3 * c + 2], 0.0)
        for p in range(2):
            force[c, 1 + p] = below_ref[3 * c + 1 + p]
            force[c, 3 + CX + p] = above_ref[3 * c + p]
        for p in range(CX):
            force[c, 3 + p] = force_ref[0, c, p]

    for p in range(1, CX - 1):
        diag[p + 3] = inner_diag_ref[p]
        for c in range(3):
            first[c, p + 3] = inner_first_ref[c, p]
    for p in (1, 2, CX - 3, CX - 2):
        inverse[p + 3] = 1.0 / inner_diag_ref[p]
    for c in range(3):
        for p in range(2, CX - 2):
            second[c, p + 3] = inner_second_ref[c, p]
        for p in range(3, CX - 3):
            smooth_ref[c, p + 1] = inner_third_ref[c, p - 3]

    @pl.loop(0, 6, unroll=2)
    def _(i):
        p = 1 + i + jnp.where(i >= 3, CX - 2, 0)
        d = plane(diagonal(sh, *[tiles(coef[p + o]) for o in (-1, 0, 1)]))
        place = slab * CX + p - 3
        valid = jnp.logical_and(place >= 0, place < slabs * CX)
        inv = jnp.where(valid, 1.0 / d, 0.0)
        diag[p] = d
        inverse[p] = inv
        for c in range(3):
            first[c, p] = force[c, p] * inv * (1.0 / MIDPOINT)

    def remainder(src, p, base):
        planes = [[tiles(src[c, p + o - base]) for c in range(3)] for o in (-1, 0, 1)]
        factors = [tiles(coef[p + o]) for o in (-1, 0, 1)]
        image = operate(sh, *planes, *factors, tiles(diag[p]))
        return planes[1], [tiles(force[c, p]) - image[c] for c in range(3)]

    (keep_2, gain_2), (keep_3, gain_3) = step_factors(FINE_STEPS)

    @pl.loop(0, 8, unroll=UNROLL)
    def _(i):
        p = 1 + i + jnp.where(i >= 4, CX - 4, 0)
        value, left = remainder(first, p, 0)
        inv = tiles(inverse[p])
        for c in range(3):
            second[c, p] = plane((1.0 + keep_2) * value[c] + gain_2 * (left[c] * inv))

    @pl.loop(0, 8, unroll=UNROLL)
    def _(i):
        p = 2 + i + jnp.where(i >= 4, CX - 6, 0)
        value, left = remainder(second, p, 0)
        inv = tiles(inverse[p])
        for c in range(3):
            step = keep_3 * (value[c] - tiles(first[c, p])) + gain_3 * (left[c] * inv)
            smooth_ref[c, p - 2] = plane(value[c] + step)

    @pl.loop(3, FINE_PLANES - 3, unroll=UNROLL)
    def _(p):
        _, left = remainder(smooth_ref, p, 2)
        for c in range(3):
            row = pl.multiple_of(c * (CX * NY) + (p - 3) * NY, NY)
            whole = plane(left[c])
            residual[pl.ds(row, NY), :] = whole
            head = whole.astype(BF16)
            table[pl.ds(row, NY), 0:NZ] = head
            table[pl.ds(row, NY), NZ : 2 * NZ] = (whole - head.astype(F32)).astype(BF16)

    for p in range(CX + 2):
        coef_out_ref[p] = coef[p + 2]
    for p in range(CX):
        diag_out_ref[p] = diag[p + 3]

    planes = residual[...].reshape(3 * HX, 2, NY, NZ)
    pairs = (planes[:, 0] + planes[:, 1]).reshape(3 * HX * NY, NZ)
    coarse_ref[...] = 0.5 * coarse_sum(pairs, sums)

    plane_rows = CX * NY
    groups = plane_rows // 8
    column = lax.broadcasted_iota(jnp.int32, (NZ, SLOTS), 0).astype(F32).astype(BF16)
    line = lax.broadcasted_iota(jnp.int32, (8, SLOTS), 0)
    lane = lax.broadcasted_iota(jnp.int32, (8, SLOTS), 1)
    one = jnp.ones((), BF16)
    zero = jnp.zeros((), BF16)

    half_line = lax.broadcasted_iota(jnp.int32, (8, HZ), 0)

    def pick(t):
        index = index_ref[pl.ds(t, 1), :]
        group = lax.shift_right_logical(index, 11)
        inner = line == (lax.shift_right_logical(index, 8) & 7)
        hot = jnp.where(column == (index & (NZ - 1)).astype(F32).astype(BF16), one, zero)
        amount = 2 * plane_rows
        both = jnp.dot(table[0:amount, 0:NZ], hot, preferred_element_type=F32) + jnp.dot(
            table[0:amount, NZ : 2 * NZ], hot, preferred_element_type=F32
        )
        for c in range(2):
            held = both[c * plane_rows : c * plane_rows + 8, :]
            for g in range(1, groups):
                at = c * plane_rows + 8 * g
                held = jnp.where(group == g, both[at : at + 8, :], held)
            found[t, c : c + 1, :] = jnp.sum(jnp.where(inner, held, 0.0), axis=0, keepdims=True)
        for c in range(2, 3):
            halves = []
            for h in range(2):
                part = index[:, h * HZ : (h + 1) * HZ]
                lane_of = jnp.broadcast_to(part & (HZ - 1), (8, HZ))
                right = (part & HZ) != 0
                group_h = group[:, h * HZ : (h + 1) * HZ]
                held = None
                for g in range(groups):
                    at = c * plane_rows + 8 * g
                    rows8 = residual[at : at + 8, :]
                    got = jnp.where(
                        right,
                        jnp.take_along_axis(rows8[:, HZ:], lane_of, axis=1, mode="promise_in_bounds"),
                        jnp.take_along_axis(rows8[:, :HZ], lane_of, axis=1, mode="promise_in_bounds"),
                    )
                    held = got if held is None else jnp.where(group_h == g, got, held)
                halves.append(held)
            held = jnp.concatenate(halves, axis=1)
            found[t, c : c + 1, :] = jnp.sum(jnp.where(inner, held, 0.0), axis=0, keepdims=True)

    @pl.loop(0, lax.div(where_ref[slabs] + (6 * SLOTS - 1), jnp.int32(6 * SLOTS)))
    def _(trip):
        for u in range(6):
            pick(6 * trip + u)

    @pl.loop(0, slabs, unroll=32)
    def _(o):
        at = where_ref[o]
        tile = lax.shift_right_logical(at, 8)
        offset = at & (SLOTS - 1)
        joined = jnp.where(lane >= offset, found[tile], found[tile + 1])
        turned = pltpu.roll(joined, SLOTS - offset, 1)
        turned = jnp.where(lane < count_ref[0, o], turned, 0.0)
        for c in range(3):
            picked_ref[pl.ds(o, 1), c * SLOTS : (c + 1) * SLOTS] = turned[c : c + 1, :]


def coarse_extent(below_pack_ref, coarse_ref, above_pack_ref, slab, slabs):
    low = [jnp.where(slab > 0, x, 0.0) for x in unpack_coarse(below_pack_ref)]
    high = [jnp.where(slab < slabs - 1, x, 0.0) for x in unpack_coarse(above_pack_ref)]
    return low + [coarse_ref[p] for p in range(HX)] + high


def gather_kernel(
    arrived_ref,
    line_ref,
    column_ref,
    local_ref,
    coef_below_ref,
    coef_ref,
    coef_above_ref,
    source_ref,
    first_ref,
    second_ref,
    total,
):
    slab = lax.axis_index("space")
    slabs = lax.axis_size("space")
    lines = HX * HY
    column = lax.broadcasted_iota(jnp.int32, (HZ, SLOTS), 0).astype(F32).astype(BF16)
    line = lax.broadcasted_iota(jnp.int32, (lines, SLOTS), 0).astype(F32).astype(BF16)
    total[...] = jnp.zeros_like(total)
    one = jnp.ones((), BF16)
    zero = jnp.zeros((), BF16)

    @pl.loop(0, slabs, step=BATCH)
    def _(s):
        hots, lefts = [], []
        for u in range(BATCH):
            hots.append(jnp.where(column == column_ref[pl.ds(s + u, 1), :].astype(BF16), one, zero))
            chosen = line == line_ref[pl.ds(s + u, 1), :].astype(BF16)
            heads, tails = [], []
            for c in range(3):
                value = arrived_ref[pl.ds(s + u, 1), c * SLOTS : (c + 1) * SLOTS]
                head = value.astype(BF16)
                tail = (value - head.astype(F32)).astype(BF16)
                heads.append(jnp.where(chosen, head, zero))
                tails.append(jnp.where(chosen, tail, zero))
            lefts.append(jnp.concatenate(heads + tails, axis=0))
        total[...] += lax.dot_general(
            jnp.concatenate(lefts, axis=1),
            jnp.concatenate(hots, axis=1),
            (((1,), (1,)), ((), ())),
            preferred_element_type=F32,
        )

    count = 3 * lines
    source = (total[0:count, :] + total[count : 2 * count, :] + local_ref[...]).reshape(3, HX, HY, HZ)
    source_ref[...] = source
    first_ref[...] = source
    second_ref[...] = source
    coef = coarse_extent(coef_below_ref, coef_ref, coef_above_ref, slab, slabs)
    sh = Shifts(1, False)
    even = (slab & 1) == 0
    for p, upward in ((0, True), (HX - 1, False)):
        d = diagonal(sh, *[coef[HX + p + o][None] for o in (-1, 0, 1)])
        scale = (1.0 / MIDPOINT) / d[0]
        to_first = even if upward else jnp.logical_not(even)
        for c in range(3):
            plain, scaled = source[c, p], source[c, p] * scale
            first_ref[c, p] = jnp.where(to_first, scaled, plain)
            second_ref[c, p] = jnp.where(to_first, plain, scaled)


def coarse_kernel(
    source_ref,
    first_ref,
    second_ref,
    coef_below_ref,
    coarse_coef_ref,
    coef_above_ref,
    smooth_ref,
    coef_ref,
    diag_ref,
    moved_ref,
    kept_ref,
    sent_1_ref,
    sent_2_ref,
    rows,
    field,
    energy,
):
    slab = lax.axis_index("space")
    slabs = lax.axis_size("space")
    mine = lax.axis_index("load")
    coef = jnp.stack(coarse_extent(coef_below_ref, coarse_coef_ref, coef_above_ref, slab, slabs))
    even = (slab & 1) == 0
    source = []
    for c in range(3):
        below = jnp.where(even, second_ref[c], first_ref[c])
        above = jnp.where(even, first_ref[c], second_ref[c])
        source.append(jnp.concatenate([below, source_ref[c], above], axis=0))
    count = 3 * HX - 2
    place = lax.broadcasted_iota(jnp.int32, (count, HY, HZ), 0) + (slab * HX - HX + 1)
    valid = jnp.logical_and(place >= 0, place < slabs * HX)
    diag = diagonal(Shifts(count, False), coef[:-2], coef[1:-1], coef[2:])
    inverse = jnp.where(valid, 1.0 / diag, 0.0)
    older = None
    value = []
    for c in range(3):
        low = jnp.where(slab > 0, source[c][:1], 0.0)
        high = jnp.where(slab < slabs - 1, source[c][-1:], 0.0)
        inner = source[c][1:-1] * inverse * (1.0 / MIDPOINT)
        value.append(jnp.concatenate([low, inner, high], axis=0))
    for number, (keep, gain) in enumerate(step_factors(COARSE_STEPS)):
        size = count - 2 * number
        inside = slice(number, number + size)
        window = slice(number + 1, number + 1 + size)
        image = operate(
            Shifts(size, False),
            [v[:-2] for v in value],
            [v[1:-1] for v in value],
            [v[2:] for v in value],
            coef[number : number + size],
            coef[window],
            coef[number + 2 : number + 2 + size],
            diag[inside],
        )
        newer = []
        for c in range(3):
            mid = value[c][1:-1]
            change = mid if older is None else mid - older[c][2:-2]
            left = source[c][window] - image[c]
            newer.append(mid + keep * change + gain * (left * inverse[inside]))
        older, value = value, newer

    planes = HX + 2
    flat = jnp.concatenate([v.reshape(planes * HY, HZ) for v in value], axis=0)
    fine = lax.broadcasted_iota(jnp.int32, (HZ, NZ), 1)
    half = lax.broadcasted_iota(jnp.int32, (HZ, NZ), 0)
    repeat = (lax.shift_right_logical(fine, 1) == half).astype(F32)
    amount = 3 * planes * HY
    rows[pl.ds(0, amount, stride=2), :] = flat
    rows[pl.ds(1, amount, stride=2), :] = flat
    wide = jnp.dot(rows[...], repeat, precision=HIGHEST, preferred_element_type=F32)
    for c in range(3):
        for p in range(CX + 2):
            at = (c * planes + (p + 1) // 2) * NY
            moved = smooth_ref[c, p] + wide[at : at + NY, :]
            field[c, p] = moved
            if 0 < p <= CX:
                moved_ref[0, c, p - 1] = moved

    sh = Shifts(4, True)

    @pl.loop(1, CX + 1, unroll=UNROLL)
    def _(p):
        planes = [[tiles(field[c, p + o]) for c in range(3)] for o in (-1, 0, 1)]
        factors = [tiles(coef_ref[p + o]) for o in (-1, 0, 1)]
        image = operate(sh, *planes, *factors, tiles(diag_ref[p - 1]))
        mid = planes[1]
        energy[p - 1] = plane(mid[0] * image[0] + mid[1] * image[1] + mid[2] * image[2])

    part = NY // 4
    for q in range(4):

        @pl.when(mine == q)
        def _():
            for ref, owner in ((kept_ref, q), (sent_1_ref, q ^ 1), (sent_2_ref.at[0], q ^ 2), (sent_2_ref.at[1], q ^ 3)):
                ref[...] = energy[:, owner * part : owner * part + part, :]


VMEM = pl.BlockSpec(memory_space=pltpu.VMEM)
HBM = pl.BlockSpec(memory_space=pltpu.HBM)
SMEM = pl.BlockSpec(memory_space=pltpu.SMEM)
PARAMS = pltpu.CompilerParams(vmem_limit_bytes=32 << 20)


def shaped(*shape):
    return jax.ShapeDtypeStruct(shape, F32)


def body(load_force, stiffness, material, face_src, face_count, face_dst):
    slabs = lax.axis_size("space")
    forward = [(i, (i + 1) % slabs) for i in range(slabs)]
    backward = [(target, origin) for origin, target in forward]
    first_pairs = [(i, i ^ 1) for i in range(slabs)]
    second_pairs = [(i, min(max(((i + 1) ^ 1) - 1, 0), slabs - 1)) for i in range(slabs)]
    pack_low, pack_high, coarse_coef, own_coef = pl.pallas_call(
        pack_kernel,
        out_shape=(
            shaped(PACK, NY, NZ),
            shaped(PACK, NY, NZ),
            shaped(HX, HY, HZ),
            shaped(CX, NY, NZ),
        ),
        in_specs=[HBM, HBM, HBM],
        out_specs=(VMEM, VMEM, VMEM, VMEM),
        scratch_shapes=[
            pltpu.SMEM((1, NY // BY), jnp.int32),
            pltpu.VMEM((CX, NY, NZ), F32),
            pltpu.VMEM((HX * NY, HZ), F32),
            pltpu.SemaphoreType.DMA((8,)),
        ],
        compiler_params=PARAMS,
        name="pack",
    )(*[
        pltpu.with_memory_space_constraint(x, pltpu.HBM) for x in (material, load_force, stiffness)
    ])
    below = lax.ppermute(pack_high, "space", forward)
    above = lax.ppermute(pack_low, "space", backward)

    rows_kept = slabs + 8
    line, column, where, index, *inner = pl.pallas_call(
        plan_kernel,
        out_shape=(
            shaped(slabs, SLOTS),
            shaped(slabs, SLOTS),
            jax.ShapeDtypeStruct((slabs + 1,), jnp.int32),
            jax.ShapeDtypeStruct((rows_kept, SLOTS), jnp.int32),
            shaped(CX, NY, NZ),
            shaped(3, CX, NY, NZ),
            shaped(3, CX, NY, NZ),
            shaped(3, CX - 6, NY, NZ),
        ),
        in_specs=[SMEM, VMEM, VMEM, VMEM, VMEM],
        out_specs=(VMEM, VMEM, SMEM, VMEM, VMEM, VMEM, VMEM, VMEM),
        compiler_params=PARAMS,
        name="plan",
    )(face_count, face_src, face_dst, load_force, own_coef)

    smooth, coef, diag, local, picked = pl.pallas_call(
        fine_kernel,
        out_shape=(
            shaped(3, CX + 2, NY, NZ),
            shaped(CX + 2, NY, NZ),
            shaped(CX, NY, NZ),
            shaped(3 * HX * HY, HZ),
            shaped(slabs, 3 * SLOTS),
        ),
        in_specs=[SMEM, SMEM] + [VMEM] * 9,
        out_specs=(VMEM, VMEM, VMEM, VMEM, VMEM),
        scratch_shapes=[
            pltpu.VMEM((COEF_PLANES, NY, NZ), F32),
            pltpu.VMEM((FINE_PLANES, NY, NZ), F32),
            pltpu.VMEM((FINE_PLANES, NY, NZ), F32),
            pltpu.VMEM((3, FINE_PLANES, NY, NZ), F32),
            pltpu.VMEM((3, FINE_PLANES, NY, NZ), F32),
            pltpu.VMEM((3, FINE_PLANES, NY, NZ), F32),
            pltpu.VMEM((3 * CX * NY, 2 * NZ), BF16),
            pltpu.VMEM((3 * HX * NY, HZ), F32),
            pltpu.VMEM((3 * CX * NY, NZ), F32),
            pltpu.VMEM((rows_kept, 8, SLOTS), F32),
        ],
        compiler_params=PARAMS,
        name="fine",
    )(face_count, where, load_force, own_coef, below, above, index, *inner)

    arrived = lax.all_to_all(picked, "space", split_axis=0, concat_axis=0, tiled=True)

    tail = pl.BlockSpec((1, NY, NZ), lambda i: (PACK - 1, 0, 0))

    def whole(*shape):
        return pl.BlockSpec(shape, lambda i: (0,) * len(shape))

    grid_shape = (3, HX, HY, HZ)
    source, send_first, send_second = pl.pallas_call(
        gather_kernel,
        grid=(1,),
        out_shape=(shaped(*grid_shape), shaped(*grid_shape), shaped(*grid_shape)),
        in_specs=[
            whole(slabs, 3 * SLOTS),
            whole(slabs, SLOTS),
            whole(slabs, SLOTS),
            whole(3 * HX * HY, HZ),
            tail,
            whole(HX, HY, HZ),
            tail,
        ],
        out_specs=(whole(*grid_shape), whole(*grid_shape), whole(*grid_shape)),
        scratch_shapes=[
            pltpu.VMEM((6 * HX * HY, HZ), F32),
        ],
        compiler_params=PARAMS,
        name="reflux",
    )(arrived, line, column, local, below, coarse_coef, above)
    met_second = lax.ppermute(send_second, "space", second_pairs)
    met_first = lax.ppermute(send_first, "space", first_pairs)

    part = (CX, NY // 4, NZ)
    moved, kept, near, far = pl.pallas_call(
        coarse_kernel,
        grid=(1,),
        out_shape=(shaped(1, 3, CX, NY, NZ),) + (shaped(*part),) * 2 + (shaped(2, *part),),
        in_specs=[
            whole(*grid_shape),
            whole(*grid_shape),
            whole(*grid_shape),
            tail,
            whole(HX, HY, HZ),
            tail,
            whole(3, CX + 2, NY, NZ),
            whole(CX + 2, NY, NZ),
            whole(CX, NY, NZ),
        ],
        out_specs=(whole(1, 3, CX, NY, NZ),) + (whole(*part),) * 2 + (whole(2, *part),),
        scratch_shapes=[
            pltpu.VMEM((3 * (HX + 2) * NY, HZ), F32),
            pltpu.VMEM((3, CX + 2, NY, NZ), F32),
            pltpu.VMEM((CX, NY, NZ), F32),
        ],
        compiler_params=PARAMS,
        name="coarse",
    )(source, met_first, met_second, below, coarse_coef, above, smooth, coef, diag)
    got = lax.ppermute(far, "load", [(i, i ^ 2) for i in range(4)])
    last = lax.ppermute(near + got[1], "load", [(i, i ^ 1) for i in range(4)])
    mine = lax.axis_index("load")
    ident = jnp.where(mine < 2, material[0, 0], material[0, 1])
    base = np.array(MODULI, np.float32)
    factors = jnp.asarray((base[None, :] - base[:, None]) / base[:, None])
    scale = jnp.where(ident == 0, factors[0], jnp.where(ident == 1, factors[1], factors[2]))
    total = (kept + got[0]) + last
    sensitivity = scale[:, None, None, None] * total[None]
    return moved, sensitivity


def solution(mesh):
    return jax.shard_map(
        body,
        mesh=mesh,
        in_specs=(
            P("load", None, "space", None, None),
            P("space", None, None),
            P("space", None),
            P("space", None, None),
            P("space", None),
            P("space", None, None),
        ),
        out_specs=(P("load", None, "space", None, None), P(None, "space", "load", None)),
        check_vma=False,
    )
```

```python
import jax
import jax.numpy as jnp
import numpy as np
from jax import lax
from jax.experimental import pallas as pl
from jax.experimental.pallas import tpu as pltpu
from jax.sharding import PartitionSpec as P

CX = 8
NY = 16
NZ = 256
BY = 8
SLOTS = 256
FINE_STEPS = 3
COARSE_STEPS = 4

UPPER_EDGE = 2.1
LOWER_EDGE = 0.15
COUPLING = 0.1
MODULI = (1.0, 0.55, 0.25)

MIDPOINT = (UPPER_EDGE + LOWER_EDGE) / 2.0
HALFWIDTH = (UPPER_EDGE - LOWER_EDGE) / 2.0

HX, HY, HZ = CX // 2, NY // 2, NZ // 2
FINE_PLANES = CX + 6
COEF_PLANES = CX + 6
PACK = 3 * 3 + 3 + 1
BATCH = 64
UNROLL = 4
F32 = jnp.float32
BF16 = jnp.bfloat16
HIGHEST = lax.Precision.HIGHEST


def step_factors(count):
    ratio = MIDPOINT / HALFWIDTH
    rho_old = 1.0 / ratio
    factors = []
    for _ in range(1, count):
        rho_new = 1.0 / (2.0 * ratio - rho_old)
        factors.append((rho_new * rho_old, 2.0 * rho_new / HALFWIDTH))
        rho_old = rho_new
    return factors


def tiles(plane):
    return jnp.stack([plane[:HY, :HZ], plane[:HY, HZ:], plane[HY:, :HZ], plane[HY:, HZ:]])


def plane(quarters):
    return jnp.concatenate(
        [
            jnp.concatenate([quarters[0], quarters[1]], axis=1),
            jnp.concatenate([quarters[2], quarters[3]], axis=1),
        ],
        axis=0,
    )


class Shifts:
    def __init__(self, count, quarters):
        shape = (count, HY, HZ)
        y = lax.broadcasted_iota(jnp.int32, shape, 1)
        z = lax.broadcasted_iota(jnp.int32, shape, 2)
        self.quarters = quarters
        self.first_y, self.last_y = y == 0, y == HY - 1
        self.first_z, self.last_z = z == 0, z == HZ - 1

    def fill(self, turned, order):
        if not self.quarters:
            return 0.0
        zero = jnp.zeros((HY, HZ), F32)
        return jnp.stack([zero if i is None else turned[i] for i in order])

    def up_y(self, x):
        turned = pltpu.roll(x, HY - 1, 1)
        return jnp.where(self.last_y, self.fill(turned, (2, 3, None, None)), turned)

    def down_y(self, x):
        turned = pltpu.roll(x, 1, 1)
        return jnp.where(self.first_y, self.fill(turned, (None, None, 0, 1)), turned)

    def up_z(self, x):
        turned = pltpu.roll(x, HZ - 1, 2)
        return jnp.where(self.last_z, self.fill(turned, (1, None, 3, None)), turned)

    def down_z(self, x):
        turned = pltpu.roll(x, 1, 2)
        return jnp.where(self.first_z, self.fill(turned, (None, 0, None, 2)), turned)

    def spread_y(self, x):
        return x + 0.5 * (self.up_y(x) + self.down_y(x))

    def spread_z(self, x):
        return x + 0.5 * (self.up_z(x) + self.down_z(x))

    def spread(self, x):
        return self.spread_z(self.spread_y(x))


def diagonal(sh, k_below, k_mid, k_above):
    return (3.0 / 7.0) * k_mid + (1.0 / 14.0) * sh.spread(k_mid + 0.5 * (k_below + k_above))


def operate(sh, below, mid, above, k_below, k_mid, k_above, diag):
    centre = diag + (1.0 / 7.0) * k_mid
    slope = [above[c] - below[c] for c in range(3)]
    cross = 0.25 * COUPLING
    plain = [mid[c] + 0.5 * (below[c] + above[c]) for c in range(3)]

    def close_y(x, skew):
        x, skew, own = (1.0 / 28.0) * x, cross * skew, (1.0 / 14.0) * x
        return own + sh.up_y(x + skew) + sh.down_y(x - skew)

    def close_z(x, skew):
        x, skew, own = (1.0 / 28.0) * x, cross * skew, (1.0 / 14.0) * x
        return own + sh.up_z(x + skew) + sh.down_z(x - skew)

    inner = (
        close_z(sh.spread_y(plain[0]), slope[2])
        + cross * (sh.up_y(slope[1]) - sh.down_y(slope[1])),
        close_y(sh.spread_z(plain[1]), slope[0] + (sh.up_z(mid[2]) - sh.down_z(mid[2]))),
        close_z(sh.spread_y(plain[2]), slope[0] + (sh.up_y(mid[1]) - sh.down_y(mid[1]))),
    )
    result = []
    for c in range(3):
        scaled = sh.spread(k_mid * mid[c] + 0.5 * (k_below * below[c] + k_above * above[c]))
        result.append(centre * mid[c] - k_mid * inner[c] - (1.0 / 14.0) * scaled)
    return result


def modulus(material_ref, brick):
    ident = material_ref[0, brick]
    return jnp.where(ident == 0, MODULI[0], jnp.where(ident == 1, MODULI[1], MODULI[2])).astype(F32)


def own_plane(material_ref):
    row = lax.broadcasted_iota(jnp.int32, (NY, NZ), 0)
    return jnp.where(row < BY, modulus(material_ref, 0), modulus(material_ref, 1))


def pair_columns():
    fine = lax.broadcasted_iota(jnp.int32, (NZ, HZ), 0)
    coarse = lax.broadcasted_iota(jnp.int32, (NZ, HZ), 1)
    return (lax.shift_right_logical(fine, 1) == coarse).astype(F32)


def coarse_sum(planes, narrow_ref):
    narrow_ref[...] = jnp.dot(
        planes, pair_columns(), precision=HIGHEST, preferred_element_type=F32
    )
    rows = narrow_ref.shape[0] // 2
    return narrow_ref[pl.ds(0, rows, stride=2), :] + narrow_ref[pl.ds(1, rows, stride=2), :]


def pack_kernel(
    material_hbm, force_hbm, stiff_hbm,
    low_ref, high_ref, coarse_ref, coef_ref,
    material, stiff, sums, sems,
):
    copies = [
        pltpu.make_async_copy(stiff_hbm, stiff, sems.at[0]),
        pltpu.make_async_copy(material_hbm, material, sems.at[1]),
    ]
    for c in range(3):
        rows = pl.ds(3 * c, 3)
        copies += [
            pltpu.make_async_copy(force_hbm.at[0, c, pl.ds(0, 3)], low_ref.at[rows], sems.at[2 + c]),
            pltpu.make_async_copy(
                force_hbm.at[0, c, pl.ds(CX - 3, 3)], high_ref.at[rows], sems.at[5 + c]
            ),
        ]
    for copy in copies:
        copy.start()
    for copy in copies:
        copy.wait()
    own = own_plane(material)
    sh = Shifts(4, True)
    coef = [stiff[p] * own for p in range(CX)]
    for p in range(CX):
        coef_ref[p] = coef[p]
    for p in range(3):
        low_ref[9 + p] = coef[p]
        high_ref[9 + p] = coef[CX - 3 + p]
    for ref, p, slot in ((low_ref, 2, 2), (high_ref, CX - 3, 0)):
        scale = (1.0 / MIDPOINT) / diagonal(sh, *[tiles(coef[p + o]) for o in (-1, 0, 1)])
        scale = plane(scale)
        for c in range(3):
            ref[3 * c + slot] = ref[3 * c + slot] * scale
    pairs = jnp.concatenate([coef[2 * p] + coef[2 * p + 1] for p in range(HX)], axis=0)
    coarse = (0.125 * coarse_sum(pairs, sums)).reshape(HX, HY, HZ)
    coarse_ref[...] = coarse
    for p in range(HX):
        y, z = (p // 2) * HY, (p % 2) * HZ
        low_ref[PACK - 1, y : y + HY, z : z + HZ] = coarse[p]
        high_ref[PACK - 1, y : y + HY, z : z + HZ] = coarse[p]


def plan_kernel(
    count_ref,
    source_ref,
    target_ref,
    force_ref,
    coef_ref,
    line_ref,
    column_ref,
    where_ref,
    index_ref,
    diag_ref,
    first_ref,
    second_ref,
    third_ref,
):
    slabs = count_ref.shape[1]
    lane = lax.broadcasted_iota(jnp.int32, (1, SLOTS), 1)
    cells = target_ref[0]
    line_ref[...] = lax.shift_right_logical(cells, 7).astype(F32)
    column_ref[...] = (cells & (HZ - 1)).astype(F32)

    def place(o, carry):
        at, row = carry
        where_ref[o] = at
        tile = lax.shift_right_logical(at, 8)
        offset = at & (SLOTS - 1)
        turned = pltpu.roll(source_ref[0, pl.ds(o, 1), :], offset, 1)
        row = jnp.where(lane >= offset, turned, row)
        index_ref[pl.ds(tile, 1), :] = row
        index_ref[pl.ds(tile + 1, 1), :] = turned
        after = at + count_ref[0, o]
        crossed = lax.shift_right_logical(after, 8) != tile
        return after, jnp.where(crossed, turned, row)

    start = (jnp.int32(0), jnp.zeros((1, SLOTS), jnp.int32))
    where_ref[slabs] = lax.fori_loop(0, slabs, place, start, unroll=8)[0]

    sh = Shifts(4, True)
    (keep_2, gain_2), (keep_3, gain_3) = step_factors(FINE_STEPS)

    @pl.loop(1, CX - 1, unroll=2)
    def _(p):
        d = diagonal(sh, *[tiles(coef_ref[p + o]) for o in (-1, 0, 1)])
        scale = (1.0 / MIDPOINT) / d
        diag_ref[p] = plane(d)
        for c in range(3):
            first_ref[c, p] = plane(tiles(force_ref[0, c, p]) * scale)

    def advance(src, p):
        planes = [[tiles(src[c, p + o]) for c in range(3)] for o in (-1, 0, 1)]
        factors = [tiles(coef_ref[p + o]) for o in (-1, 0, 1)]
        d = tiles(diag_ref[p])
        image = operate(sh, *planes, *factors, d)
        return planes[1], [(tiles(force_ref[0, c, p]) - image[c]) / d for c in range(3)]

    @pl.loop(2, CX - 2, unroll=2)
    def _(p):
        value, left = advance(first_ref, p)
        for c in range(3):
            second_ref[c, p] = plane((1.0 + keep_2) * value[c] + gain_2 * left[c])

    @pl.loop(3, CX - 3, unroll=2)
    def _(p):
        value, left = advance(second_ref, p)
        for c in range(3):
            step = keep_3 * (value[c] - tiles(first_ref[c, p])) + gain_3 * left[c]
            third_ref[c, p - 3] = plane(value[c] + step)


def unpack_coarse(plane_ref):
    return [
        plane_ref[0, (p // 2) * HY : (p // 2) * HY + HY, (p % 2) * HZ : (p % 2) * HZ + HZ]
        for p in range(HX)
    ]


def fine_kernel(
    count_ref,
    where_ref,
    force_ref,
    own_ref,
    below_ref,
    above_ref,
    index_ref,
    inner_diag_ref,
    inner_first_ref,
    inner_second_ref,
    inner_third_ref,
    smooth_ref,
    coef_out_ref,
    diag_out_ref,
    coarse_ref,
    picked_ref,
    coef,
    diag,
    inverse,
    force,
    first,
    second,
    table,
    sums,
    residual,
    found,
):
    slab = lax.axis_index("space")
    slabs = lax.axis_size("space")
    sh = Shifts(4, True)
    has_below = slab > 0
    has_above = slab < slabs - 1
    for p in range(CX):
        coef[3 + p] = own_ref[p]
    for p in range(3):
        coef[p] = jnp.where(has_below, below_ref[9 + p], 0.0)
        coef[3 + CX + p] = jnp.where(has_above, above_ref[9 + p], 0.0)
    for c in range(3):
        first[c, 0] = jnp.where(has_below, below_ref[3 * c], 0.0)
        first[c, FINE_PLANES - 1] = jnp.where(has_above, above_ref[3 * c + 2], 0.0)
        for p in range(2):
            force[c, 1 + p] = below_ref[3 * c + 1 + p]
            force[c, 3 + CX + p] = above_ref[3 * c + p]
        for p in range(CX):
            force[c, 3 + p] = force_ref[0, c, p]

    for p in range(1, CX - 1):
        diag[p + 3] = inner_diag_ref[p]
        for c in range(3):
            first[c, p + 3] = inner_first_ref[c, p]
    for p in (1, 2, CX - 3, CX - 2):
        inverse[p + 3] = 1.0 / inner_diag_ref[p]
    for c in range(3):
        for p in range(2, CX - 2):
            second[c, p + 3] = inner_second_ref[c, p]
        for p in range(3, CX - 3):
            smooth_ref[c, p + 1] = inner_third_ref[c, p - 3]

    @pl.loop(0, 6, unroll=6)
    def _(i):
        p = 1 + i + jnp.where(i >= 3, CX - 2, 0)
        d = plane(diagonal(sh, *[tiles(coef[p + o]) for o in (-1, 0, 1)]))
        place = slab * CX + p - 3
        valid = jnp.logical_and(place >= 0, place < slabs * CX)
        inv = jnp.where(valid, 1.0 / d, 0.0)
        diag[p] = d
        inverse[p] = inv
        for c in range(3):
            first[c, p] = force[c, p] * inv * (1.0 / MIDPOINT)

    def remainder(src, p, base):
        planes = [[tiles(src[c, p + o - base]) for c in range(3)] for o in (-1, 0, 1)]
        factors = [tiles(coef[p + o]) for o in (-1, 0, 1)]
        image = operate(sh, *planes, *factors, tiles(diag[p]))
        return planes[1], [tiles(force[c, p]) - image[c] for c in range(3)]

    (keep_2, gain_2), (keep_3, gain_3) = step_factors(FINE_STEPS)

    @pl.loop(0, 8, unroll=UNROLL)
    def _(i):
        p = 1 + i + jnp.where(i >= 4, CX - 4, 0)
        value, left = remainder(first, p, 0)
        inv = tiles(inverse[p])
        for c in range(3):
            second[c, p] = plane((1.0 + keep_2) * value[c] + gain_2 * (left[c] * inv))

    @pl.loop(0, 8, unroll=UNROLL)
    def _(i):
        p = 2 + i + jnp.where(i >= 4, CX - 6, 0)
        value, left = remainder(second, p, 0)
        inv = tiles(inverse[p])
        for c in range(3):
            step = keep_3 * (value[c] - tiles(first[c, p])) + gain_3 * (left[c] * inv)
            smooth_ref[c, p - 2] = plane(value[c] + step)

    @pl.loop(3, FINE_PLANES - 3, unroll=UNROLL)
    def _(p):
        _, left = remainder(smooth_ref, p, 2)
        for c in range(3):
            row = pl.multiple_of(c * (CX * NY) + (p - 3) * NY, NY)
            whole = plane(left[c])
            residual[pl.ds(row, NY), :] = whole
            head = whole.astype(BF16)
            table[pl.ds(row, NY), 0:NZ] = head
            table[pl.ds(row, NY), NZ : 2 * NZ] = (whole - head.astype(F32)).astype(BF16)

    for p in range(CX + 2):
        coef_out_ref[p] = coef[p + 2]
    for p in range(CX):
        diag_out_ref[p] = diag[p + 3]

    planes = residual[...].reshape(3 * HX, 2, NY, NZ)
    pairs = (planes[:, 0] + planes[:, 1]).reshape(3 * HX * NY, NZ)
    coarse_ref[...] = 0.5 * coarse_sum(pairs, sums)

    plane_rows = CX * NY
    groups = plane_rows // 8
    column = lax.broadcasted_iota(jnp.int32, (NZ, SLOTS), 0).astype(F32).astype(BF16)
    line = lax.broadcasted_iota(jnp.int32, (8, SLOTS), 0)
    lane = lax.broadcasted_iota(jnp.int32, (8, SLOTS), 1)
    one = jnp.ones((), BF16)
    zero = jnp.zeros((), BF16)

    half_line = lax.broadcasted_iota(jnp.int32, (8, HZ), 0)

    def pick(t):
        index = index_ref[pl.ds(t, 1), :]
        group = lax.shift_right_logical(index, 11)
        inner = line == (lax.shift_right_logical(index, 8) & 7)
        hot = jnp.where(column == (index & (NZ - 1)).astype(F32).astype(BF16), one, zero)
        amount = 2 * plane_rows
        both = jnp.dot(table[0:amount, 0:NZ], hot, preferred_element_type=F32) + jnp.dot(
            table[0:amount, NZ : 2 * NZ], hot, preferred_element_type=F32
        )
        for c in range(2):
            held = both[c * plane_rows : c * plane_rows + 8, :]
            for g in range(1, groups):
                at = c * plane_rows + 8 * g
                held = jnp.where(group == g, both[at : at + 8, :], held)
            found[t, c : c + 1, :] = jnp.sum(jnp.where(inner, held, 0.0), axis=0, keepdims=True)
        for c in range(2, 3):
            halves = []
            for h in range(2):
                part = index[:, h * HZ : (h + 1) * HZ]
                lane_of = jnp.broadcast_to(part & (HZ - 1), (8, HZ))
                right = (part & HZ) != 0
                group_h = group[:, h * HZ : (h + 1) * HZ]
                held = None
                for g in range(groups):
                    at = c * plane_rows + 8 * g
                    rows8 = residual[at : at + 8, :]
                    got = jnp.where(
                        right,
                        jnp.take_along_axis(rows8[:, HZ:], lane_of, axis=1, mode="promise_in_bounds"),
                        jnp.take_along_axis(rows8[:, :HZ], lane_of, axis=1, mode="promise_in_bounds"),
                    )
                    held = got if held is None else jnp.where(group_h == g, got, held)
                halves.append(held)
            held = jnp.concatenate(halves, axis=1)
            found[t, c : c + 1, :] = jnp.sum(jnp.where(inner, held, 0.0), axis=0, keepdims=True)

    @pl.loop(0, lax.div(where_ref[slabs] + (6 * SLOTS - 1), jnp.int32(6 * SLOTS)))
    def _(trip):
        for u in range(6):
            pick(6 * trip + u)

    @pl.loop(0, slabs, unroll=32)
    def _(o):
        at = where_ref[o]
        tile = lax.shift_right_logical(at, 8)
        offset = at & (SLOTS - 1)
        joined = jnp.where(lane >= offset, found[tile], found[tile + 1])
        turned = pltpu.roll(joined, SLOTS - offset, 1)
        turned = jnp.where(lane < count_ref[0, o], turned, 0.0)
        for c in range(3):
            picked_ref[pl.ds(o, 1), c * SLOTS : (c + 1) * SLOTS] = turned[c : c + 1, :]


def coarse_extent(below_pack_ref, coarse_ref, above_pack_ref, slab, slabs):
    low = [jnp.where(slab > 0, x, 0.0) for x in unpack_coarse(below_pack_ref)]
    high = [jnp.where(slab < slabs - 1, x, 0.0) for x in unpack_coarse(above_pack_ref)]
    return low + [coarse_ref[p] for p in range(HX)] + high


def gather_kernel(
    arrived_ref,
    line_ref,
    column_ref,
    local_ref,
    coef_below_ref,
    coef_ref,
    coef_above_ref,
    source_ref,
    first_ref,
    second_ref,
    total,
):
    slab = lax.axis_index("space")
    slabs = lax.axis_size("space")
    lines = HX * HY
    column = lax.broadcasted_iota(jnp.int32, (HZ, SLOTS), 0).astype(F32).astype(BF16)
    line = lax.broadcasted_iota(jnp.int32, (lines, SLOTS), 0).astype(F32).astype(BF16)
    total[...] = jnp.zeros_like(total)
    one = jnp.ones((), BF16)
    zero = jnp.zeros((), BF16)

    @pl.loop(0, slabs, step=BATCH)
    def _(s):
        hots, lefts = [], []
        for u in range(BATCH):
            hots.append(jnp.where(column == column_ref[pl.ds(s + u, 1), :].astype(BF16), one, zero))
            chosen = line == line_ref[pl.ds(s + u, 1), :].astype(BF16)
            heads, tails = [], []
            for c in range(3):
                value = arrived_ref[pl.ds(s + u, 1), c * SLOTS : (c + 1) * SLOTS]
                head = value.astype(BF16)
                tail = (value - head.astype(F32)).astype(BF16)
                heads.append(jnp.where(chosen, head, zero))
                tails.append(jnp.where(chosen, tail, zero))
            lefts.append(jnp.concatenate(heads + tails, axis=0))
        total[...] += lax.dot_general(
            jnp.concatenate(lefts, axis=1),
            jnp.concatenate(hots, axis=1),
            (((1,), (1,)), ((), ())),
            preferred_element_type=F32,
        )

    count = 3 * lines
    source = (total[0:count, :] + total[count : 2 * count, :] + local_ref[...]).reshape(3, HX, HY, HZ)
    source_ref[...] = source
    first_ref[...] = source
    second_ref[...] = source
    coef = coarse_extent(coef_below_ref, coef_ref, coef_above_ref, slab, slabs)
    sh = Shifts(1, False)
    even = (slab & 1) == 0
    for p, upward in ((0, True), (HX - 1, False)):
        d = diagonal(sh, *[coef[HX + p + o][None] for o in (-1, 0, 1)])
        scale = (1.0 / MIDPOINT) / d[0]
        to_first = even if upward else jnp.logical_not(even)
        for c in range(3):
            plain, scaled = source[c, p], source[c, p] * scale
            first_ref[c, p] = jnp.where(to_first, scaled, plain)
            second_ref[c, p] = jnp.where(to_first, plain, scaled)


def coarse_kernel(
    source_ref,
    first_ref,
    second_ref,
    coef_below_ref,
    coarse_coef_ref,
    coef_above_ref,
    smooth_ref,
    coef_ref,
    diag_ref,
    moved_ref,
    kept_ref,
    sent_1_ref,
    sent_2_ref,
    rows,
    field,
    energy,
):
    slab = lax.axis_index("space")
    slabs = lax.axis_size("space")
    mine = lax.axis_index("load")
    coef = jnp.stack(coarse_extent(coef_below_ref, coarse_coef_ref, coef_above_ref, slab, slabs))
    even = (slab & 1) == 0
    source = []
    for c in range(3):
        below = jnp.where(even, second_ref[c], first_ref[c])
        above = jnp.where(even, first_ref[c], second_ref[c])
        source.append(jnp.concatenate([below, source_ref[c], above], axis=0))
    count = 3 * HX - 2
    place = lax.broadcasted_iota(jnp.int32, (count, HY, HZ), 0) + (slab * HX - HX + 1)
    valid = jnp.logical_and(place >= 0, place < slabs * HX)
    diag = diagonal(Shifts(count, False), coef[:-2], coef[1:-1], coef[2:])
    inverse = jnp.where(valid, 1.0 / diag, 0.0)
    older = None
    value = []
    for c in range(3):
        low = jnp.where(slab > 0, source[c][:1], 0.0)
        high = jnp.where(slab < slabs - 1, source[c][-1:], 0.0)
        inner = source[c][1:-1] * inverse * (1.0 / MIDPOINT)
        value.append(jnp.concatenate([low, inner, high], axis=0))
    for number, (keep, gain) in enumerate(step_factors(COARSE_STEPS)):
        size = count - 2 * number
        inside = slice(number, number + size)
        window = slice(number + 1, number + 1 + size)
        image = operate(
            Shifts(size, False),
            [v[:-2] for v in value],
            [v[1:-1] for v in value],
            [v[2:] for v in value],
            coef[number : number + size],
            coef[window],
            coef[number + 2 : number + 2 + size],
            diag[inside],
        )
        newer = []
        for c in range(3):
            mid = value[c][1:-1]
            change = mid if older is None else mid - older[c][2:-2]
            left = source[c][window] - image[c]
            newer.append(mid + keep * change + gain * (left * inverse[inside]))
        older, value = value, newer

    planes = HX + 2
    flat = jnp.concatenate([v.reshape(planes * HY, HZ) for v in value], axis=0)
    fine = lax.broadcasted_iota(jnp.int32, (HZ, NZ), 1)
    half = lax.broadcasted_iota(jnp.int32, (HZ, NZ), 0)
    repeat = (lax.shift_right_logical(fine, 1) == half).astype(F32)
    amount = 3 * planes * HY
    rows[pl.ds(0, amount, stride=2), :] = flat
    rows[pl.ds(1, amount, stride=2), :] = flat
    wide = jnp.dot(rows[...], repeat, precision=HIGHEST, preferred_element_type=F32)
    for c in range(3):
        for p in range(CX + 2):
            at = (c * planes + (p + 1) // 2) * NY
            moved = smooth_ref[c, p] + wide[at : at + NY, :]
            field[c, p] = moved
            if 0 < p <= CX:
                moved_ref[0, c, p - 1] = moved

    sh = Shifts(4, True)

    @pl.loop(1, CX + 1, unroll=8)
    def _(p):
        planes = [[tiles(field[c, p + o]) for c in range(3)] for o in (-1, 0, 1)]
        factors = [tiles(coef_ref[p + o]) for o in (-1, 0, 1)]
        image = operate(sh, *planes, *factors, tiles(diag_ref[p - 1]))
        mid = planes[1]
        energy[p - 1] = plane(mid[0] * image[0] + mid[1] * image[1] + mid[2] * image[2])

    part = NY // 4
    for q in range(4):

        @pl.when(mine == q)
        def _():
            for ref, owner in ((kept_ref, q), (sent_1_ref, q ^ 1), (sent_2_ref.at[0], q ^ 2), (sent_2_ref.at[1], q ^ 3)):
                ref[...] = energy[:, owner * part : owner * part + part, :]


VMEM = pl.BlockSpec(memory_space=pltpu.VMEM)
HBM = pl.BlockSpec(memory_space=pltpu.HBM)
SMEM = pl.BlockSpec(memory_space=pltpu.SMEM)
PARAMS = pltpu.CompilerParams(vmem_limit_bytes=32 << 20)


def shaped(*shape):
    return jax.ShapeDtypeStruct(shape, F32)


def body(load_force, stiffness, material, face_src, face_count, face_dst):
    slabs = lax.axis_size("space")
    forward = [(i, (i + 1) % slabs) for i in range(slabs)]
    backward = [(target, origin) for origin, target in forward]
    first_pairs = [(i, i ^ 1) for i in range(slabs)]
    second_pairs = [(i, min(max(((i + 1) ^ 1) - 1, 0), slabs - 1)) for i in range(slabs)]
    pack_low, pack_high, coarse_coef, own_coef = pl.pallas_call(
        pack_kernel,
        out_shape=(
            shaped(PACK, NY, NZ),
            shaped(PACK, NY, NZ),
            shaped(HX, HY, HZ),
            shaped(CX, NY, NZ),
        ),
        in_specs=[HBM, HBM, HBM],
        out_specs=(VMEM, VMEM, VMEM, VMEM),
        scratch_shapes=[
            pltpu.SMEM((1, NY // BY), jnp.int32),
            pltpu.VMEM((CX, NY, NZ), F32),
            pltpu.VMEM((HX * NY, HZ), F32),
            pltpu.SemaphoreType.DMA((8,)),
        ],
        compiler_params=PARAMS,
        name="pack",
    )(*[
        pltpu.with_memory_space_constraint(x, pltpu.HBM) for x in (material, load_force, stiffness)
    ])
    below = lax.ppermute(pack_high, "space", forward)
    above = lax.ppermute(pack_low, "space", backward)

    rows_kept = slabs + 8
    line, column, where, index, *inner = pl.pallas_call(
        plan_kernel,
        out_shape=(
            shaped(slabs, SLOTS),
            shaped(slabs, SLOTS),
            jax.ShapeDtypeStruct((slabs + 1,), jnp.int32),
            jax.ShapeDtypeStruct((rows_kept, SLOTS), jnp.int32),
            shaped(CX, NY, NZ),
            shaped(3, CX, NY, NZ),
            shaped(3, CX, NY, NZ),
            shaped(3, CX - 6, NY, NZ),
        ),
        in_specs=[SMEM, VMEM, VMEM, VMEM, VMEM],
        out_specs=(VMEM, VMEM, SMEM, VMEM, VMEM, VMEM, VMEM, VMEM),
        compiler_params=PARAMS,
        name="plan",
    )(face_count, face_src, face_dst, load_force, own_coef)

    smooth, coef, diag, local, picked = pl.pallas_call(
        fine_kernel,
        out_shape=(
            shaped(3, CX + 2, NY, NZ),
            shaped(CX + 2, NY, NZ),
            shaped(CX, NY, NZ),
            shaped(3 * HX * HY, HZ),
            shaped(slabs, 3 * SLOTS),
        ),
        in_specs=[SMEM, SMEM] + [VMEM] * 9,
        out_specs=(VMEM, VMEM, VMEM, VMEM, VMEM),
        scratch_shapes=[
            pltpu.VMEM((COEF_PLANES, NY, NZ), F32),
            pltpu.VMEM((FINE_PLANES, NY, NZ), F32),
            pltpu.VMEM((FINE_PLANES, NY, NZ), F32),
            pltpu.VMEM((3, FINE_PLANES, NY, NZ), F32),
            pltpu.VMEM((3, FINE_PLANES, NY, NZ), F32),
            pltpu.VMEM((3, FINE_PLANES, NY, NZ), F32),
            pltpu.VMEM((3 * CX * NY, 2 * NZ), BF16),
            pltpu.VMEM((3 * HX * NY, HZ), F32),
            pltpu.VMEM((3 * CX * NY, NZ), F32),
            pltpu.VMEM((rows_kept, 8, SLOTS), F32),
        ],
        compiler_params=PARAMS,
        name="fine",
    )(face_count, where, load_force, own_coef, below, above, index, *inner)

    arrived = lax.all_to_all(picked, "space", split_axis=0, concat_axis=0, tiled=True)

    tail = pl.BlockSpec((1, NY, NZ), lambda i: (PACK - 1, 0, 0))

    def whole(*shape):
        return pl.BlockSpec(shape, lambda i: (0,) * len(shape))

    grid_shape = (3, HX, HY, HZ)
    source, send_first, send_second = pl.pallas_call(
        gather_kernel,
        grid=(1,),
        out_shape=(shaped(*grid_shape), shaped(*grid_shape), shaped(*grid_shape)),
        in_specs=[
            whole(slabs, 3 * SLOTS),
            whole(slabs, SLOTS),
            whole(slabs, SLOTS),
            whole(3 * HX * HY, HZ),
            tail,
            whole(HX, HY, HZ),
            tail,
        ],
        out_specs=(whole(*grid_shape), whole(*grid_shape), whole(*grid_shape)),
        scratch_shapes=[
            pltpu.VMEM((6 * HX * HY, HZ), F32),
        ],
        compiler_params=PARAMS,
        name="reflux",
    )(arrived, line, column, local, below, coarse_coef, above)
    met_second = lax.ppermute(send_second, "space", second_pairs)
    met_first = lax.ppermute(send_first, "space", first_pairs)

    part = (CX, NY // 4, NZ)
    moved, kept, near, far = pl.pallas_call(
        coarse_kernel,
        grid=(1,),
        out_shape=(shaped(1, 3, CX, NY, NZ),) + (shaped(*part),) * 2 + (shaped(2, *part),),
        in_specs=[
            whole(*grid_shape),
            whole(*grid_shape),
            whole(*grid_shape),
            tail,
            whole(HX, HY, HZ),
            tail,
            whole(3, CX + 2, NY, NZ),
            whole(CX + 2, NY, NZ),
            whole(CX, NY, NZ),
        ],
        out_specs=(whole(1, 3, CX, NY, NZ),) + (whole(*part),) * 2 + (whole(2, *part),),
        scratch_shapes=[
            pltpu.VMEM((3 * (HX + 2) * NY, HZ), F32),
            pltpu.VMEM((3, CX + 2, NY, NZ), F32),
            pltpu.VMEM((CX, NY, NZ), F32),
        ],
        compiler_params=PARAMS,
        name="coarse",
    )(source, met_first, met_second, below, coarse_coef, above, smooth, coef, diag)
    got = lax.ppermute(far, "load", [(i, i ^ 2) for i in range(4)])
    last = lax.ppermute(near + got[1], "load", [(i, i ^ 1) for i in range(4)])
    mine = lax.axis_index("load")
    ident = jnp.where(mine < 2, material[0, 0], material[0, 1])
    base = np.array(MODULI, np.float32)
    factors = jnp.asarray((base[None, :] - base[:, None]) / base[:, None])
    scale = jnp.where(ident == 0, factors[0], jnp.where(ident == 1, factors[1], factors[2]))
    total = (kept + got[0]) + last
    sensitivity = scale[:, None, None, None] * total[None]
    return moved, sensitivity


def solution(mesh):
    return jax.shard_map(
        body,
        mesh=mesh,
        in_specs=(
            P("load", None, "space", None, None),
            P("space", None, None),
            P("space", None),
            P("space", None, None),
            P("space", None),
            P("space", None, None),
        ),
        out_specs=(P("load", None, "space", None, None), P(None, "space", "load", None)),
        check_vma=False,
    )
```
